32 devices in a mesh: dp: 16 (over z, x, core), tensor: 2 (over y).
Axes of the slice: x: 2, y: 2, z: 4, core: 2. Of those that a mesh axis runs over, the one named last changes fastest.
Arguments:
- inputs: bfloat16 [32, 384, 2048], P('dp', 'tensor'), may hold values from -6 to 6
- block_ids: int32 [32, 384], P('dp'), may hold values from 0 to 5, never falling along the last dimension, each value on 1 to 256 neighbouring positions
- positions: int32 [32, 384], P('dp'), may hold values from 0 to 1149, as said below
- w_query: bfloat16 [2048, 2048], P('dp', 'tensor'), may hold values from -0.125 to 0.125
- key_weight: bfloat16 [2048, 256], P('dp', 'tensor'), may hold values from -0.125 to 0.125
- value_weight: bfloat16 [2048, 256], P('dp', 'tensor'), may hold values from -0.125 to 0.125
- w_out: bfloat16 [2048, 2048], P('tensor', 'dp'), may hold values from -1.5 to 1.5
- w_gate: bfloat16 [2048, 5632], P('dp', 'tensor'), may hold values from -0.125 to 0.125
- w_up: bfloat16 [2048, 5632], P('dp', 'tensor'), may hold values from -0.125 to 0.125
- w_down: bfloat16 [5632, 2048], P('tensor', 'dp'), may hold values from -0.078125 to 0.078125
- attn_gain: bfloat16 [2048], P('dp'), may hold values from 0.099609375 to 1.8984375
- mlp_gain: bfloat16 [2048], P('dp'), may hold values from 0.099609375 to 1.8984375
- out_grad: bfloat16 [32, 384, 2048], P('dp', 'tensor'), may hold values from -6 to 6
Outputs:
- output: bfloat16 [32, 384, 2048], P('dp', 'tensor')
- input_grad: bfloat16 [32, 384, 2048], P('dp', 'tensor')
- grad_query: float32 [2048, 2048], P('dp', 'tensor')
- grad_key: float32 [2048, 256], P('dp', 'tensor')
- grad_value: float32 [2048, 256], P('dp', 'tensor')
- grad_out: float32 [2048, 2048], P('tensor', 'dp')
- grad_gate: float32 [2048, 5632], P('dp', 'tensor')
- grad_up: float32 [2048, 5632], P('dp', 'tensor')
- grad_down: float32 [5632, 2048], P('tensor', 'dp')
- grad_attn_gain: float32 [2048], P('dp')
- grad_mlp_gain: float32 [2048], P('dp')
The draws below stay inside these ranges and needn't reach their ends.
Inputs may be any that keep to these rules, and one draw needn't show every extreme that they name: `block_ids`: within a sequence block ids start at 0 and never fall; a block holds 1 to 256 tokens in a row, and some block holds exactly 256. `positions`: each sequence starts at position 0; from one token to the next the position rises by 1, 2 or 3; in some sequence every rise is 3.
All inputs are finite; a program needn't handle non-finite values.
Results may differ from the reference program's by a relative error of at most 0.014.
Values may be sent and summed in bfloat16 or wider, within the bound.
No kernel may reach another device: no remote copies, remote signals or barrier semaphores. Data moves between devices by JAX's collectives and lax.ppermute only.
A program may use at most 256 MiB of HBM per device.

```python
import math
import jax
import jax.numpy as jnp
import numpy as np
from jax import lax

MODEL_WIDTH = 2048
QUERY_HEADS = 32
KEY_VALUE_HEADS = 4
HEAD_SIZE = 64
FF = 5632
SEQ = 384
BLOCK = 256
SEQS = 32


def draw_positions(key, part):
    steps_rise = jax.random.randint(jax.random.fold_in(key, 1), (SEQS, SEQ), 1, 4)
    chosen = jax.random.randint(jax.random.fold_in(key, 2), (), 0, SEQS)
    row_index = jnp.arange(SEQS, dtype=jnp.int32)[:, None]
    steps_rise = jnp.where(row_index == chosen, 3, steps_rise)
    return (jnp.cumsum(steps_rise, axis=1) - steps_rise).astype(jnp.int32)


def strengthened(entries, stream_key, source, target, parts, factor):
    owner, partner = [(jnp.arange(entries.shape[position]) // (entries.shape[position] // parts)).reshape([-1 if axis == position else 1 for axis in range(entries.ndim)]) for position in (source, target)]
    chosen = jax.random.permutation(stream_key, parts)[partner]
    strong = (owner == chosen) | (owner == (partner + parts // 2) % parts)
    return jnp.where(strong, factor * entries, entries)


def levels(key, shape, split, smallest, top_value):
    factor_of = 1.0
    for dim, parts in split:
        heights = jax.random.uniform(jax.random.fold_in(jax.random.fold_in(key, 6), dim), (parts,), jnp.float32, smallest / len(split), top_value / len(split))
        factor_of = factor_of * jnp.repeat(jnp.exp(heights), shape[dim] // parts).reshape((-1,) + (1,) * (len(shape) - 1 - dim))
    return factor_of


def length_profile(count, total, most, slope):
    portions = [(1 << 20) // math.isqrt(standing ** slope) + 1 for standing in range(2, count + 1)]
    spare, given = total - most - (count - 1), [1] * (count - 1)
    while spare > 0:
        free = [i for i in range(count - 1) if given[i] < most]
        pool, left = sum([portions[i] for i in free]), spare
        for i in free:
            addition = min(most - given[i], max(1, left * portions[i] // pool), spare)
            given[i] = given[i] + addition
            spare = spare - addition
    return np.array([most] + given)


def uneven_parts(rng, number_of, total, limit, slope):
    if number_of == 2:
        one = jax.random.randint(rng, (), max(1, total - limit), min(limit, total - 1) + 1)
        return jnp.stack([one, total - one])
    tallies = jnp.asarray(length_profile(number_of, total, limit, slope), jnp.int32)
    pairs = (number_of - 1) // 2
    donor, taker = tallies[1:1 + 2 * pairs:2], tallies[2:2 + 2 * pairs:2]
    slack = jnp.minimum(donor - 1, limit - taker)
    passed = jax.random.randint(jax.random.fold_in(rng, 1), (pairs,), 0, 1 << 20) % (slack + 1)
    tallies = tallies.at[1:1 + 2 * pairs:2].set(donor - passed).at[2:2 + 2 * pairs:2].set(taker + passed)
    return tallies[jax.random.permutation(jax.random.fold_in(rng, 2), number_of)]


def gaussian(key, dims, scale, reach, shards=(), kind=jnp.bfloat16):
    loudness = levels(key, dims, shards, -0.22, 0.18) if shards else 1.0
    values = jax.random.normal(key, dims, jnp.float32) * scale * loudness
    return jnp.minimum(jnp.maximum(values, -reach), reach).astype(kind)


def noise_with(own_key, shape, spread, most, cuts, heavy, kind=jnp.bfloat16):
    values = spread * jax.random.normal(own_key, shape, jnp.float32)
    if cuts:
        values = values * levels(own_key, shape, cuts, -0.22, 0.18)
    return jnp.clip(strengthened(values, jax.random.fold_in(own_key, 3), *heavy), -most, most).astype(kind)


def setup_inputs(seed: int = 0) -> dict:
    arg_keys = jax.random.split(jax.random.key(seed), 14)
    return {
        "inputs": noise_with(arg_keys[0], (SEQS, SEQ, MODEL_WIDTH), 1.0, 6.0, ((0, 16), (1, 2)), (0, 2, 16, 2.0)),
        "block_ids": jax.vmap(lambda own: jnp.searchsorted(jnp.cumsum(uneven_parts(own, 4 * SEQ // BLOCK, SEQ, BLOCK, 0)), jnp.arange(SEQ), side="right"))(jax.random.split(arg_keys[1], SEQS)).reshape((SEQS, SEQ)).astype(jnp.int32),
        "positions": draw_positions(jax.random.fold_in(arg_keys[13], 71), 0),
        "w_query": gaussian(arg_keys[3], (MODEL_WIDTH, QUERY_HEADS * HEAD_SIZE), MODEL_WIDTH ** -0.5, 0.125, ((0, 16), (1, 2))),
        "key_weight": gaussian(arg_keys[4], (MODEL_WIDTH, KEY_VALUE_HEADS * HEAD_SIZE), MODEL_WIDTH ** -0.5, 0.125, ((0, 16), (1, 2))),
        "value_weight": gaussian(arg_keys[5], (MODEL_WIDTH, KEY_VALUE_HEADS * HEAD_SIZE), MODEL_WIDTH ** -0.5, 0.125, ((0, 16), (1, 2))),
        "w_out": gaussian(arg_keys[6], (QUERY_HEADS * HEAD_SIZE, MODEL_WIDTH), (max(QUERY_HEADS * HEAD_SIZE // 128, 8)) ** -0.5, 1.5, ((0, 2), (1, 16))),
        "w_gate": gaussian(arg_keys[7], (MODEL_WIDTH, FF), MODEL_WIDTH ** -0.5, 0.125, ((0, 16), (1, 2))),
        "w_up": gaussian(arg_keys[8], (MODEL_WIDTH, FF), MODEL_WIDTH ** -0.5, 0.125, ((0, 16), (1, 2))),
        "w_down": gaussian(arg_keys[9], (FF, MODEL_WIDTH), FF ** -0.5, 0.078125, ((0, 2), (1, 16))),
        "attn_gain": jnp.clip(1.0 + 0.18 * jax.random.normal(arg_keys[10], (MODEL_WIDTH,), jnp.float32), 0.099609375, 1.8984375).astype(jnp.bfloat16),
        "mlp_gain": jnp.clip(1.0 + 0.18 * jax.random.normal(arg_keys[11], (MODEL_WIDTH,), jnp.float32), 0.099609375, 1.8984375).astype(jnp.bfloat16),
        "out_grad": noise_with(arg_keys[12], (SEQS, SEQ, MODEL_WIDTH), 1.0, 6.0, ((0, 16), (1, 2)), (0, 2, 16, 2.0)),
    }


epsilon = 1e-05
rope_base = 10000.0
masked_value = -1e+30
highest = lax.Precision.HIGHEST

@jax.custom_vjp
def lower_half(v):
    return lax.optimization_barrier(v.astype(jnp.bfloat16)).astype(jnp.float32)

@jax.custom_vjp
def low_back(v):
    return v

def low_keep(v):
    return (lower_half(v), None)

def low_pass(kept, grad):
    return (grad,)

def back_keep(v):
    return (v, None)

def back_low(kept, grad):
    return (lower_half(grad),)
lower_half.defvjp(low_keep, low_pass)
low_back.defvjp(back_keep, back_low)

def rms_factor(values):
    return lax.rsqrt(lax.optimization_barrier(jnp.mean(values * values, axis=-1, keepdims=True)) + epsilon)

def rope_tables(positions, head_width):
    steps_half = jnp.arange(head_width // 2, dtype=jnp.float32)
    frequency = jnp.exp(steps_half * (-2.0 * math.log(rope_base) / head_width))
    angles = positions.astype(jnp.float32)[:, None] * frequency[None, :]
    angles = jnp.concatenate([angles, angles], axis=-1)
    return (jnp.cos(angles), jnp.sin(angles))

def apply_rotation(values, cosine_rows, sine_table):
    half_width = values.shape[-1] // 2
    turned = jnp.concatenate([-values[..., half_width:], values[..., :half_width]], axis=-1)
    return values * cosine_rows + turned * sine_table

def decoder_layer(resid_in, w_query, key_weight, value_weight, w_out, w_gate, w_up, w_down, attn_gain, mlp_gain, allowed, cosine_rows, sine_table):
    token_length = resid_in.shape[0]
    group_count = QUERY_HEADS // KEY_VALUE_HEADS
    normed = lower_half(resid_in * rms_factor(resid_in) * attn_gain)
    query_raw = low_back(jnp.dot(normed, w_query, precision=highest))
    key_unrotated = low_back(jnp.dot(normed, key_weight, precision=highest))
    value_matrix = lower_half(low_back(jnp.dot(normed, value_weight, precision=highest)))
    query_matrix = lower_half(apply_rotation(query_raw.reshape(token_length, QUERY_HEADS, HEAD_SIZE), cosine_rows[:, None, :], sine_table[:, None, :]))
    key_matrix = lower_half(apply_rotation(key_unrotated.reshape(token_length, KEY_VALUE_HEADS, HEAD_SIZE), cosine_rows[:, None, :], sine_table[:, None, :]))
    value_matrix = value_matrix.reshape(token_length, KEY_VALUE_HEADS, HEAD_SIZE)
    grouped_keys = query_matrix.reshape(token_length, KEY_VALUE_HEADS, group_count, HEAD_SIZE)
    scores = low_back(jnp.einsum('qkgd,skd->kgqs', grouped_keys, key_matrix, precision=highest) * HEAD_SIZE ** (-0.5))
    scores = jnp.where(allowed[None, None], scores, masked_value)
    top_score = lax.optimization_barrier(jnp.max(scores, axis=-1, keepdims=True))
    weights = jnp.exp(scores - top_score)
    attn_probs = lower_half(weights / lax.optimization_barrier(jnp.sum(weights, axis=-1, keepdims=True)))
    context = jnp.einsum('kgqs,skd->qkgd', attn_probs, value_matrix, precision=highest)
    context = lower_half(low_back(context.reshape(token_length, QUERY_HEADS * HEAD_SIZE)))
    hidden = resid_in + low_back(jnp.dot(context, w_out, precision=highest))
    normed_mlp = lower_half(hidden * rms_factor(hidden) * mlp_gain)
    gate_pre = low_back(jnp.dot(normed_mlp, w_gate, precision=highest))
    upward = low_back(jnp.dot(normed_mlp, w_up, precision=highest))
    active = lower_half(gate_pre * jax.nn.sigmoid(gate_pre) * upward)
    return hidden + low_back(jnp.dot(active, w_down, precision=highest))

def reference(inputs, block_ids, positions, w_query, key_weight, value_weight, w_out, w_gate, w_up, w_down, attn_gain, mlp_gain, out_grad):
    params = (w_query.astype(jnp.float32), key_weight.astype(jnp.float32), value_weight.astype(jnp.float32), w_out.astype(jnp.float32), w_gate.astype(jnp.float32), w_up.astype(jnp.float32), w_down.astype(jnp.float32), attn_gain.astype(jnp.float32), mlp_gain.astype(jnp.float32))

    def one_sequence(running, seq_item):
        seq_in, seq_grad, blocks, places = seq_item
        cosine_rows, sine_table = rope_tables(places, HEAD_SIZE)
        allowed = blocks[None, :] <= blocks[:, None]

        def forward(resid_in, *weight_list):
            return decoder_layer(resid_in, *weight_list, allowed, cosine_rows, sine_table)
        result, pullback = jax.vjp(forward, seq_in.astype(jnp.float32), *params)
        grad_list = pullback(seq_grad.astype(jnp.float32))
        running = tuple((total_now + addend for total_now, addend in zip(running, grad_list[1:])))
        return (running, (result.astype(jnp.bfloat16), grad_list[0].astype(jnp.bfloat16)))
    zero_grads = tuple((jnp.zeros(param.shape, jnp.float32) for param in params))
    totals, (outputs, input_grads) = lax.scan(one_sequence, zero_grads, (inputs, out_grad, block_ids, positions))
    return (outputs, input_grads, totals[0], totals[1], totals[2], totals[3], totals[4], totals[5], totals[6], totals[7], totals[8])
```

```python
import math

import jax
import jax.numpy as jnp
from jax import lax
from jax.sharding import PartitionSpec as P

HEAD_SIZE = 64
epsilon = 1e-05
rope_base = 10000.0
masked_value = -1e30
bf16 = jnp.bfloat16
f32 = jnp.float32


def rms_factor(values):
    return lax.rsqrt(jnp.mean(values * values, axis=-1, keepdims=True) + epsilon)


def rope_tables(positions, head_width):
    steps_half = jnp.arange(head_width // 2, dtype=f32)
    frequency = jnp.exp(steps_half * (-2.0 * math.log(rope_base) / head_width))
    angles = positions.astype(f32)[..., None] * frequency
    angles = jnp.concatenate([angles, angles], axis=-1)
    return (jnp.cos(angles), jnp.sin(angles))


def apply_rotation(values, cosine_rows, sine_table):
    half_width = values.shape[-1] // 2
    turned = jnp.concatenate([-values[..., half_width:], values[..., :half_width]], axis=-1)
    return values * cosine_rows + turned * sine_table


def unrotate(values, cosine_rows, sine_table):
    half_width = values.shape[-1] // 2
    turned = values * sine_table
    back_part = jnp.concatenate([turned[..., half_width:], -turned[..., :half_width]], axis=-1)
    return values * cosine_rows + back_part


def dot(left, right, left_dim, right_dim, out=f32):
    return lax.dot_general(
        left, right, (((left_dim,), (right_dim,)), ((), ())), preferred_element_type=f32
    ).astype(out)


def norm_back(upstream, unit_rows, factor, gain_vec):
    scaled = upstream * gain_vec
    spread = jnp.mean(scaled * unit_rows, axis=-1, keepdims=True)
    return factor * (scaled - unit_rows * spread)


def shards(
    inputs,
    block_ids,
    positions,
    w_query,
    key_weight,
    value_weight,
    w_out,
    w_gate,
    w_up,
    w_down,
    attn_gain,
    mlp_gain,
    out_grad,
):
    seqs, own_len, width = inputs.shape
    length = block_ids.shape[1]
    tokens = seqs * length
    side = lax.axis_index("tensor")
    tensor = length // own_len
    swap = [(i, (i + 1) % tensor) for i in range(tensor)]
    hd = HEAD_SIZE
    heads = w_query.shape[1] // hd
    kv = key_weight.shape[1] // hd
    group = heads // kv
    scale = hd ** (-0.5)

    full_query = lax.all_gather(w_query, "dp", axis=0, tiled=True)
    full_key = lax.all_gather(key_weight, "dp", axis=0, tiled=True)
    full_value = lax.all_gather(value_weight, "dp", axis=0, tiled=True)
    full_out = lax.all_gather(w_out, "dp", axis=1, tiled=True)
    full_gate = lax.all_gather(w_gate, "dp", axis=0, tiled=True)
    full_up = lax.all_gather(w_up, "dp", axis=0, tiled=True)
    full_down = lax.all_gather(w_down, "dp", axis=1, tiled=True)
    gains = lax.all_gather(jnp.stack([attn_gain, mlp_gain]), "dp", axis=1, tiled=True).astype(f32)
    attn_gain_f, mlp_gain_f = gains[0], gains[1]

    def own(rows):
        whole = rows.reshape(seqs, tensor, own_len, width)
        return lax.dynamic_index_in_dim(whole, side, 1, keepdims=False)

    def other(rows):
        whole = rows.reshape(seqs, tensor, own_len, width)
        return lax.dynamic_index_in_dim(whole, 1 - side, 1, keepdims=False)

    def exchange_sum(partial):
        low = partial.astype(bf16)
        return low.astype(f32) + lax.ppermute(low, "tensor", swap).astype(f32)

    def exchange_own(partial):
        return own(partial) + lax.ppermute(other(partial).astype(bf16), "tensor", swap).astype(f32)

    resid = lax.all_gather(inputs, "tensor", axis=1, tiled=True).reshape(tokens, width).astype(f32)
    grad_all = lax.all_gather(out_grad, "tensor", axis=1, tiled=True).reshape(tokens, width)
    attn_factor = rms_factor(resid)
    normed = (resid * attn_factor * attn_gain_f).astype(bf16)
    cosine_rows, sine_rows = rope_tables(positions.reshape(tokens), hd)
    cos_heads, sin_heads = cosine_rows[:, None, :], sine_rows[:, None, :]
    allowed = block_ids[:, None, :] <= block_ids[:, :, None]

    query = apply_rotation(
        dot(normed, full_query, 1, 0).reshape(tokens, heads, hd), cos_heads, sin_heads
    ).astype(bf16)
    key = apply_rotation(
        dot(normed, full_key, 1, 0).reshape(tokens, kv, hd), cos_heads, sin_heads
    ).astype(bf16)
    value = dot(normed, full_value, 1, 0, bf16).reshape(seqs, length, kv, hd)
    query = query.reshape(seqs, length, kv, group, hd)
    key = key.reshape(seqs, length, kv, hd)

    def scores_of():
        raw = jnp.einsum("bqkgd,bskd->bkgqs", query, key, preferred_element_type=f32) * scale
        return jnp.where(allowed[:, None, None], raw, masked_value)

    scores = scores_of()
    top_score = jnp.max(scores, axis=-1, keepdims=True)
    weights = jnp.exp(scores - top_score)
    total_weight = jnp.sum(weights, axis=-1, keepdims=True)
    probs = (weights / total_weight).astype(bf16)
    log_total = top_score + jnp.log(total_weight)
    context = (
        jnp.einsum("bkgqs,bskd->bqkgd", probs, value, preferred_element_type=f32)
        .astype(bf16)
        .reshape(tokens, heads * hd)
    )
    hidden = resid + exchange_sum(dot(context, full_out, 1, 0))
    mlp_factor = rms_factor(hidden)
    unit_mlp = hidden * mlp_factor
    normed_mlp = (unit_mlp * mlp_gain_f).astype(bf16)
    gate_pre = dot(normed_mlp, full_gate, 1, 0)
    upward = dot(normed_mlp, full_up, 1, 0)
    sigmoid_gate = jax.nn.sigmoid(gate_pre)
    active = (gate_pre * sigmoid_gate * upward).astype(bf16)
    output = own(hidden) + exchange_own(dot(active, full_down, 1, 0))

    grad_down = dot(active, grad_all, 0, 0, bf16)
    d_active = dot(grad_all, full_down, 1, 1)
    d_gate = (d_active * upward * sigmoid_gate * (1.0 + gate_pre * (1.0 - sigmoid_gate))).astype(bf16)
    d_upward = (d_active * (gate_pre * sigmoid_gate)).astype(bf16)
    grad_gate = dot(normed_mlp, d_gate, 0, 0, bf16)
    grad_up = dot(normed_mlp, d_upward, 0, 0, bf16)
    d_normed_mlp = exchange_sum(dot(d_gate, full_gate, 1, 1) + dot(d_upward, full_up, 1, 1))
    grad_mlp_gain = jnp.sum(own(d_normed_mlp * unit_mlp), axis=(0, 1))
    d_hidden = grad_all.astype(f32) + norm_back(d_normed_mlp, unit_mlp, mlp_factor, mlp_gain_f)
    attn_grad = d_hidden.astype(bf16)
    grad_out = dot(context, attn_grad, 0, 0, bf16)
    d_context = dot(attn_grad, full_out, 1, 1, bf16).reshape(seqs, length, kv, group, hd)
    probs_again = jnp.exp(scores_of() - log_total)
    d_probs = jnp.einsum("bqkgd,bskd->bkgqs", d_context, value, preferred_element_type=f32)
    row_delta = jnp.sum(probs_again * d_probs, axis=-1, keepdims=True)
    d_scores = (probs_again * (d_probs - row_delta)).astype(bf16)
    d_value = jnp.einsum(
        "bkgqs,bqkgd->bskd", probs_again.astype(bf16), d_context, preferred_element_type=f32
    )
    d_value = d_value.astype(bf16).reshape(tokens, kv * hd)
    d_query = jnp.einsum("bkgqs,bskd->bqkgd", d_scores, key, preferred_element_type=f32) * scale
    d_query = unrotate(d_query.reshape(tokens, heads, hd), cos_heads, sin_heads)
    d_query = d_query.astype(bf16).reshape(tokens, heads * hd)
    d_key = jnp.einsum("bkgqs,bqkgd->bskd", d_scores, query, preferred_element_type=f32) * scale
    d_key = unrotate(d_key.reshape(tokens, kv, hd), cos_heads, sin_heads)
    d_key = d_key.astype(bf16).reshape(tokens, kv * hd)
    grad_query = dot(normed, d_query, 0, 0, bf16)
    grad_key = dot(normed, d_key, 0, 0, bf16)
    grad_value = dot(normed, d_value, 0, 0, bf16)
    d_normed = exchange_own(
        dot(d_query, full_query, 1, 1) + dot(d_key, full_key, 1, 1) + dot(d_value, full_value, 1, 1)
    )
    own_resid = inputs.astype(f32)
    own_factor = rms_factor(own_resid)
    unit_attn = own_resid * own_factor
    grad_attn_gain = jnp.sum(d_normed * unit_attn, axis=(0, 1))
    input_grad = own(d_hidden) + norm_back(d_normed, unit_attn, own_factor, attn_gain_f)

    def reduce(partial, axis):
        return lax.psum_scatter(partial, "dp", scatter_dimension=axis, tiled=True)

    gain_sums = lax.psum(
        reduce(jnp.stack([grad_attn_gain, grad_mlp_gain]), 1), "tensor"
    )
    return (
        output.astype(bf16),
        input_grad.astype(bf16),
        reduce(grad_query, 0).astype(f32),
        reduce(grad_key, 0).astype(f32),
        reduce(grad_value, 0).astype(f32),
        reduce(grad_out, 1).astype(f32),
        reduce(grad_gate, 0).astype(f32),
        reduce(grad_up, 0).astype(f32),
        reduce(grad_down, 1).astype(f32),
        gain_sums[0],
        gain_sums[1],
    )


def solution(mesh):
    row, col = P("dp", "tensor"), P("tensor", "dp")
    seq = P("dp", "tensor", None)
    return jax.shard_map(
        shards,
        mesh=mesh,
        in_specs=(seq, P("dp", None), P("dp", None), row, row, row, col, row, row, col, P("dp"), P("dp"), seq),
        out_specs=(seq, seq, row, row, row, col, row, row, col, P("dp"), P("dp")),
        check_vma=False,
    )
```

```python
import functools
import math

import jax
import jax.numpy as jnp
from jax import lax
from jax.experimental import pallas as pl
from jax.experimental.pallas import tpu as pltpu
from jax.sharding import PartitionSpec as P

HEAD_SIZE = 64
LANES = 128
TILE = 256
epsilon = 1e-05
rope_base = 10000.0
masked_value = -1e30
bf16 = jnp.bfloat16
f32 = jnp.float32
VMEM_LIMIT = 60 * 1024 * 1024


def dot(left, right, left_dim, right_dim):
    return lax.dot_general(
        left, right, (((left_dim,), (right_dim,)), ((), ())), preferred_element_type=f32
    )


def tie(value, *others):
    return lax.optimization_barrier((value,) + others)[0]


def params(steps=1):
    return pltpu.CompilerParams(
        dimension_semantics=("arbitrary",) * steps, vmem_limit_bytes=VMEM_LIMIT
    )


def resident(shape):
    return pl.BlockSpec(
        shape, lambda *_: (0,) * len(shape), pipeline_mode=pl.Buffered(1)
    )


def cost(flops, moved, trans=0):
    return pl.CostEstimate(flops=flops, bytes_accessed=moved, transcendentals=trans)


class Ring:
    def __init__(self, size):
        self.size = size
        self.line = size // 4
        self.reaches = [self.line >> k for k in range(1, self.line.bit_length())]

    def swap(self, value, bits):
        return lax.ppermute(value, "dp", [(i, i ^ bits) for i in range(self.size)])

    def core(self, value):
        return self.swap(value, 1)

    def pair(self, value):
        return self.swap(value, 2)

    def along(self, value, reach):
        return self.swap(value, 4 * reach)

    def slots(self, me):
        order = [0]
        for reach in self.reaches:
            order = order + [o ^ reach for o in order]
        return jnp.stack([me ^ (l * 4 + p * 2 + c) for c in range(2) for p in range(2) for l in order])


class Gather:
    def __init__(self, ring, shard):
        self.ring, self.held, self.got, self.left = ring, shard, None, list(ring.reaches)

    def send(self):
        self.got = self.ring.along(self.held, self.left.pop(0))

    def join(self, step):
        self.held = jnp.concatenate([step(self.held), self.got], axis=0)
        step.mark(self.held)
        return self.held

    def finish(self, step):
        while len(self.left) > 1:
            self.join(step)
            self.send()


class Steps:
    def __init__(self):
        self.last = ()

    def __call__(self, value, *others):
        return tie(value, *self.last, *others)

    def mark(self, *outs):
        self.last = outs


class Reduce:
    def __init__(self, ring, step, acts, grads):
        self.ring, self.step, self.acts, self.grads = ring, step, acts, grads
        self.quarter = acts[0].shape[1] // 2

    def far(self):
        out = dot(self.step(self.acts[1]), self.grads, 0, 0).astype(bf16)
        self.step.mark(out)
        self.from_core = self.ring.core(out)

    def side(self):
        part = dot(self.step(self.acts[0], self.from_core)[:, self.quarter :], self.grads, 0, 0)
        out = (part + self.from_core[self.quarter :].astype(f32)).astype(bf16)
        self.step.mark(out)
        self.from_pair = self.ring.pair(out)

    def near(self):
        part = dot(self.step(self.acts[0])[:, : self.quarter], self.grads, 0, 0)
        out = (part + self.from_core[: self.quarter].astype(f32)).astype(bf16)
        self.step.mark(out)
        self.terms, self.reach = [out, self.from_pair], 1

    def fold(self):
        rows = self.terms[0].shape[0] // 2
        terms = [self.step(self.terms[0], *self.terms[1:])] + self.terms[1:]
        if self.reach == self.ring.line:
            out = sum(t.astype(f32) for t in terms)
            self.step.mark(out)
            return out
        out = sum(t[rows:].astype(f32) for t in terms).astype(bf16)
        self.step.mark(out)
        self.terms = [t[:rows] for t in self.terms] + [self.ring.along(out, self.reach)]
        self.reach *= 2

    def fold_rest(self):
        out = None
        while out is None:
            out = self.fold()
        return out


def enter(rows, slots, gain):
    count, width = rows.shape
    blocks = slots.shape[0]
    block = width // blocks
    per = blocks // 2
    half = width // 2
    step = count // 4
    norm = gain is not None
    narrow = block % LANES != 0
    if narrow:
        rows = rows.reshape(count, blocks, block)[:, slots].reshape(count, width)

    def kernel(slots_ref, x_ref, gain_ref, *outs):
        if norm:
            x = x_ref[...].astype(f32)
            factor = lax.rsqrt(jnp.mean(x * x, axis=-1, keepdims=True) + epsilon)
        for b in range(blocks):
            start = b * block if narrow else pl.multiple_of(slots_ref[b] * block, block)
            piece = x_ref[:, pl.ds(start, block)]
            at = slice((b % per) * block, (b % per + 1) * block)
            outs[b // per][:, at] = piece
            if norm:
                g = gain_ref[:, b * block : (b + 1) * block]
                outs[2 + b // per][:, at] = (piece.astype(f32) * factor * g).astype(bf16)

    n_out = 4 if norm else 2
    if gain is None:
        gain = jnp.ones((1, width), f32)
    return pl.pallas_call(
        kernel,
        out_shape=[jax.ShapeDtypeStruct((count, half), bf16)] * n_out,
        grid_spec=pltpu.PrefetchScalarGridSpec(
            num_scalar_prefetch=1,
            grid=(4,),
            in_specs=[
                pl.BlockSpec((step, width), lambda i, s: (i, 0)),
                pl.BlockSpec((1, width), lambda i, s: (0, 0)),
            ],
            out_specs=[pl.BlockSpec((step, half), lambda i, s: (i, 0))] * n_out,
        ),
        compiler_params=params(),
        cost_estimate=cost(10 * count * width, 2 * count * width * (1 + n_out // 2)),
        name="enter",
    )(slots, rows, gain)


def qkv_kernel(*refs):
    cos_ref, sin_ref, out_ref = refs[6:]
    raw = times_pieces(refs[:2], refs[2:6])
    lane = lax.broadcasted_iota(jnp.int32, raw.shape, 1) % HEAD_SIZE
    half = HEAD_SIZE // 2
    ahead = pltpu.roll(raw, raw.shape[1] - half, 1)
    behind = pltpu.roll(raw, half, 1)
    turned = jnp.where(lane < half, -ahead, behind)
    out_ref[...] = (raw * cos_ref[...] + turned * sin_ref[...]).astype(bf16)


def project_qkv(acts, weights, cosine, sine, first, columns):
    tokens, part = acts[0].shape
    steps = columns // TILE
    table = pl.BlockSpec((tokens, TILE), lambda j: (0, j // (steps - 1)))
    depth = weights[0].shape[0]
    return pl.pallas_call(
        qkv_kernel,
        out_shape=jax.ShapeDtypeStruct((tokens, columns), bf16),
        grid=(steps,),
        in_specs=[resident((tokens, part))] * 2
        + [pl.BlockSpec((depth, TILE), lambda j: (0, first + j))] * 4
        + [table, table],
        out_specs=pl.BlockSpec((tokens, TILE), lambda j: (0, j)),
        compiler_params=params(),
        cost_estimate=cost(8 * tokens * depth * columns, 8 * depth * columns + 4 * tokens * part),
        name="project_qkv",
    )(*acts, *weights, cosine, sine)


def times_pieces(acts, weights):
    part = weights[0].shape[0]
    return sum(
        dot(acts[i // 2][:, (i % 2) * part : (i % 2 + 1) * part], w[...], 1, 0) for i, w in enumerate(weights)
    )


def project_kernel(*refs):
    refs[6][...] = times_pieces(refs[:2], refs[2:6]).astype(bf16)


def project(acts, weights, columns):
    tokens, part = acts[0].shape
    depth = weights[0].shape[0]
    return pl.pallas_call(
        project_kernel,
        out_shape=jax.ShapeDtypeStruct((tokens, columns), bf16),
        grid=(columns // TILE,),
        in_specs=[resident((tokens, part))] * 2 + [pl.BlockSpec((depth, TILE), lambda j: (0, j))] * 4,
        out_specs=pl.BlockSpec((tokens, TILE), lambda j: (0, j)),
        compiler_params=params(),
        cost_estimate=cost(8 * tokens * depth * columns, 8 * depth * columns + 4 * tokens * part),
        name="project",
    )(*acts, *weights)


def project_back(acts, weights, firsts=None, part=(0, 1)):
    tokens = acts[0].shape[0] // part[1]
    depth = weights[0][0].shape[0]
    steps = depth // TILE
    count = len(acts)
    firsts = firsts or [0] * count
    wides = [a.shape[1] if not f else math.gcd(a.shape[1], f) for a, f in zip(acts, firsts)]
    parts = [(n, f // w + j, w, j) for n, (a, f, w) in enumerate(zip(acts, firsts, wides)) for j in range(a.shape[1] // w)]
    total = len(parts)

    def kernel(*refs):
        acts_in, out_ref = refs[:count], refs[-1]
        for p in range(4):
            pieces = refs[count + p * total : count + (p + 1) * total]

            @pl.when(pl.program_id(0) // steps == p)
            def _():
                out_ref[...] = sum(
                    dot(acts_in[n][:, j * w : (j + 1) * w], piece[...], 1, 1)
                    for (n, _, w, j), piece in zip(parts, pieces)
                ).astype(bf16)

    def spec(p, block, wide):
        return pl.BlockSpec((TILE, wide), lambda i: (jnp.clip(i - p * steps, 0, steps - 1), block))

    columns = sum(a.shape[1] for a in acts)
    return pl.pallas_call(
        kernel,
        out_shape=jax.ShapeDtypeStruct((tokens, 4 * depth), bf16),
        grid=(4 * steps,),
        in_specs=[
            pl.BlockSpec((tokens, a.shape[1]), lambda i: (part[0], 0), pipeline_mode=pl.Buffered(1)) for a in acts
        ]
        + [spec(p, block, w) for p in range(4) for _, block, w, _ in parts],
        out_specs=pl.BlockSpec((tokens, TILE), lambda i: (0, i)),
        compiler_params=params(),
        cost_estimate=cost(8 * tokens * depth * columns, (8 * depth + 2 * tokens) * columns),
        name="project_back",
    )(*acts, *[weights[n][p] for p in range(4) for n, _, _, _ in parts])


def gain_rows(pieces, first):
    depth = pieces[0].shape[0]

    def kernel(*refs):
        for p in range(4):
            refs[4][:, p * depth : (p + 1) * depth] = refs[p][...].astype(f32).T[:8]

    out = pl.pallas_call(
        kernel,
        out_shape=jax.ShapeDtypeStruct((8, 4 * depth), f32),
        grid=(1,),
        in_specs=[pl.BlockSpec((depth, LANES), lambda i: (0, first // LANES))] * 4,
        out_specs=pl.BlockSpec((8, 4 * depth), lambda i: (0, 0)),
        compiler_params=params(),
        name="gain_rows",
    )(*pieces)
    return out[:1], out[1:2]


def forward_kernel(q_ref, kv_ref, seg_row, seg_col, ctx_ref, lse_ref):
    kv_heads = kv_ref.shape[1] // (2 * HEAD_SIZE)
    group = pl.program_id(1)
    keys = kv_ref[:, : kv_heads * HEAD_SIZE].astype(f32)
    values = kv_ref[:, kv_heads * HEAD_SIZE :].astype(f32)
    lane = lax.broadcasted_iota(jnp.int32, keys.shape, 1)
    low = lane < HEAD_SIZE
    here = low == (group == 0)
    both_keys = jnp.where(here, keys, pltpu.roll(keys, HEAD_SIZE, 1)).astype(bf16)
    both_values = jnp.where(here, values, pltpu.roll(values, HEAD_SIZE, 1)).astype(bf16)
    none = jnp.zeros_like(both_values)
    value_low = jnp.where(low, both_values, none)
    value_high = jnp.where(low, none, both_values)
    allowed = seg_row[...] <= seg_col[...]
    pairs = q_ref.shape[1] // (2 * HEAD_SIZE)
    for pair in range(pairs):
        cut = slice(pair * LANES, (pair + 1) * LANES)
        q = q_ref[:, cut] * bf16(HEAD_SIZE ** (-0.5))
        total = None
        for side, values_here in ((0, value_low), (1, value_high)):
            mine = jnp.where(low, q, none) if side == 0 else jnp.where(low, none, q)
            scores = jnp.where(allowed, dot(mine, both_keys, 1, 1), masked_value)
            top = jnp.max(scores, axis=-1, keepdims=True)
            weights = jnp.exp(scores - top)
            mass = jnp.sum(weights, axis=-1, keepdims=True)
            probs = (weights * (1.0 / mass)).astype(bf16)
            part = dot(probs, values_here, 1, 0)
            total = part if total is None else total + part
            lse_ref[:, 2 * pair + side : 2 * pair + side + 1] = top + jnp.log(mass)
        ctx_ref[:, cut] = total.astype(bf16)


def attention_forward(qkv, seg_row, seg_col, seqs, heads, kv):
    tokens = qkv.shape[0]
    length = tokens // seqs
    wide = heads // kv * HEAD_SIZE
    last = heads * HEAD_SIZE // (2 * kv * HEAD_SIZE)
    return pl.pallas_call(
        forward_kernel,
        out_shape=[
            jax.ShapeDtypeStruct((tokens, heads * HEAD_SIZE), bf16),
            jax.ShapeDtypeStruct((kv, tokens, heads // kv), f32),
        ],
        grid=(seqs, kv),
        in_specs=[
            pl.BlockSpec((length, wide), lambda s, g: (s, g)),
            pl.BlockSpec((length, 2 * kv * HEAD_SIZE), lambda s, g: (s, last)),
            pl.BlockSpec((None, 1, length), lambda s, g: (s, 0, 0)),
            pl.BlockSpec((None, length, 1), lambda s, g: (s, 0, 0)),
        ],
        out_specs=[
            pl.BlockSpec((length, wide), lambda s, g: (s, g)),
            pl.BlockSpec((None, length, heads // kv), lambda s, g: (g, s, 0)),
        ],
        compiler_params=params(2),
        cost_estimate=cost(16 * tokens * length * heads * HEAD_SIZE, 6 * tokens * heads * HEAD_SIZE),
        name="attention_forward",
    )(qkv, qkv, seg_row, seg_col)


def backward_kernel(q_ref, kv_ref, dctx_ref, lse_ref, seg_row, seg_col, cos_ref, sin_ref, out_ref):
    kv_heads = kv_ref.shape[1] // (2 * HEAD_SIZE)
    group = pl.program_id(0)
    wide = q_ref.shape[1]
    q_cols = kv_heads * wide
    scale = HEAD_SIZE ** (-0.5)
    half = HEAD_SIZE // 2
    keys = kv_ref[:, : kv_heads * HEAD_SIZE].astype(f32)
    values = kv_ref[:, kv_heads * HEAD_SIZE :].astype(f32)
    lane = lax.broadcasted_iota(jnp.int32, keys.shape, 1)
    low = lane < HEAD_SIZE
    here = low == (group == 0)
    both_keys = jnp.where(here, keys, pltpu.roll(keys, HEAD_SIZE, 1)).astype(bf16)
    both_values = jnp.where(here, values, pltpu.roll(values, HEAD_SIZE, 1)).astype(bf16)
    none = jnp.zeros_like(both_keys)
    key_low = jnp.where(low, both_keys, none)
    key_high = jnp.where(low, none, both_keys)
    allowed = seg_row[...] <= seg_col[...]
    cosine, sine = cos_ref[...], sin_ref[...]

    def unrotate(rows):
        turned = rows * sine
        ahead = pltpu.roll(turned, LANES - half, 1)
        behind = pltpu.roll(turned, half, 1)
        return rows * cosine + jnp.where(lane % HEAD_SIZE < half, ahead, -behind)

    dkey = jnp.zeros(keys.shape, f32)
    dvalue = jnp.zeros(keys.shape, f32)
    pairs = q_ref.shape[1] // LANES
    for pair in range(pairs):
        cut = slice(pair * LANES, (pair + 1) * LANES)
        q = q_ref[:, cut] * bf16(scale)
        dctx = dctx_ref[:, cut]
        dquery = None
        for side, keys_here in ((0, key_low), (1, key_high)):
            mine = jnp.where(low, q, none) if side == 0 else jnp.where(low, none, q)
            dmine = jnp.where(low, dctx, none) if side == 0 else jnp.where(low, none, dctx)
            scores = jnp.where(allowed, dot(mine, both_keys, 1, 1), masked_value)
            probs = jnp.exp(scores - lse_ref[:, 2 * pair + side : 2 * pair + side + 1])
            dprobs = dot(dmine, both_values, 1, 1)
            delta = jnp.sum(probs * dprobs, axis=-1, keepdims=True)
            dscores = (probs * (dprobs - delta)).astype(bf16)
            part = dot(dscores, keys_here, 1, 0)
            dquery = part if dquery is None else dquery + part
            dkey = dkey + dot(dscores, mine, 0, 0)
            dvalue = dvalue + dot(probs.astype(bf16), dmine, 0, 0)
        start = pl.multiple_of(group * wide + pair * LANES, LANES)
        out_ref[:, pl.ds(start, LANES)] = unrotate(dquery * scale).astype(bf16)
    dkey = unrotate(dkey + pltpu.roll(dkey, HEAD_SIZE, 1)).astype(bf16)
    dvalue = (dvalue + pltpu.roll(dvalue, HEAD_SIZE, 1)).astype(bf16)

    key_cut, value_cut = slice(q_cols, q_cols + LANES), slice(q_cols + LANES, q_cols + 2 * LANES)

    @pl.when(group == 0)
    def _():
        out_ref[:, key_cut] = dkey
        out_ref[:, value_cut] = dvalue

    @pl.when(group == 1)
    def _():
        out_ref[:, key_cut] = jnp.where(low, out_ref[:, key_cut], dkey)
        out_ref[:, value_cut] = jnp.where(low, out_ref[:, value_cut], dvalue)


def attention_backward(qkv, dctx, lse, seg_row, seg_col, cosine, sine, which, heads, kv):
    length = dctx.shape[0]
    wide = heads // kv * HEAD_SIZE
    columns = qkv.shape[1]
    last = heads * HEAD_SIZE // (2 * kv * HEAD_SIZE)
    table = pl.BlockSpec((length, LANES), lambda g: (which, 0))
    return pl.pallas_call(
        backward_kernel,
        out_shape=jax.ShapeDtypeStruct((length, columns), bf16),
        grid=(kv,),
        in_specs=[
            pl.BlockSpec((length, wide), lambda g: (which, g)),
            pl.BlockSpec((length, 2 * kv * HEAD_SIZE), lambda g: (which, last)),
            pl.BlockSpec((length, wide), lambda g: (0, g)),
            pl.BlockSpec((None, length, heads // kv), lambda g: (g, which, 0)),
            pl.BlockSpec((None, 1, length), lambda g: (which, 0, 0)),
            pl.BlockSpec((None, length, 1), lambda g: (which, 0, 0)),
            table,
            table,
        ],
        out_specs=pl.BlockSpec((length, columns), lambda g: (0, 0)),
        compiler_params=params(),
        cost_estimate=cost(40 * length * length * heads * HEAD_SIZE, 10 * length * heads * HEAD_SIZE),
        name="attention_backward",
    )(qkv, qkv, dctx, lse, seg_row, seg_col, cosine, sine)


def gate_up_kernel(*refs):
    gu_ref, active_ref = refs[6:]
    both = times_pieces(refs[:2], refs[2:6])
    gate, up = both[:, :TILE], both[:, TILE:]
    gu_ref[...] = both.astype(bf16)
    active_ref[...] = (gate * (1.0 / (1.0 + jnp.exp(-gate))) * up).astype(bf16)


def gate_up(acts, weights):
    tokens, part = acts[0].shape
    depth, columns = weights[0].shape
    return pl.pallas_call(
        gate_up_kernel,
        out_shape=[
            jax.ShapeDtypeStruct((tokens, columns), bf16),
            jax.ShapeDtypeStruct((tokens, columns // 2), bf16),
        ],
        grid=(columns // (2 * TILE),),
        in_specs=[resident((tokens, part))] * 2 + [pl.BlockSpec((depth, 2 * TILE), lambda j: (0, j))] * 4,
        out_specs=[
            pl.BlockSpec((tokens, 2 * TILE), lambda j: (0, j)),
            pl.BlockSpec((tokens, TILE), lambda j: (0, j)),
        ],
        compiler_params=params(),
        cost_estimate=cost(8 * tokens * depth * columns, 8 * depth * columns + 4 * tokens * columns, tokens * columns),
        name="gate_up",
    )(*acts, *weights)


def swiglu_back_kernel(*refs):
    gu_ref, out_ref = refs[6:]
    d_active = times_pieces(refs[:2], refs[2:6])
    gate, up = gu_ref[:, :TILE].astype(f32), gu_ref[:, TILE:].astype(f32)
    sig = 1.0 / (1.0 + jnp.exp(-gate))
    out_ref[:, :TILE] = (d_active * up * sig * (1.0 + gate * (1.0 - sig))).astype(bf16)
    out_ref[:, TILE:] = (d_active * (gate * sig)).astype(bf16)


def swiglu_back(acts, weights, gu):
    tokens, part = acts[0].shape
    depth = weights[0].shape[0]
    columns = gu.shape[1]
    wide = pl.BlockSpec((tokens, 2 * TILE), lambda j: (0, j))
    return pl.pallas_call(
        swiglu_back_kernel,
        out_shape=jax.ShapeDtypeStruct((tokens, columns), bf16),
        grid=(columns // (2 * TILE),),
        in_specs=[resident((tokens, part))] * 2 + [pl.BlockSpec((depth, TILE), lambda j: (0, j))] * 4 + [wide],
        out_specs=wide,
        compiler_params=params(),
        cost_estimate=cost(4 * tokens * depth * columns, 4 * depth * columns + 4 * tokens * columns, tokens * columns),
        name="swiglu_back",
    )(*acts, *weights, gu)


def row_specs(seqs, own_len, wide):
    mine = pl.BlockSpec((None, None, own_len, wide), lambda s, h: (s, h, 0, 0))
    theirs = pl.BlockSpec((None, None, own_len, wide), lambda s, h: (s, 1 - h, 0, 0))
    return mine, theirs


def load_rows(refs):
    return jnp.concatenate([r[...].astype(f32) for r in refs], axis=-1)


def store_rows(refs, rows):
    half = rows.shape[-1] // 2
    refs[0][...] = rows[:, :half].astype(bf16)
    refs[1][...] = rows[:, half:].astype(bf16)


def middle(resid, partial, received, gain, seqs, own_len):
    width = partial.shape[1]
    half = width // 2

    def kernel(res_low, res_high, par, rec, gain_ref, hid_low, hid_high, norm_low, norm_high):
        rows = load_rows([res_low, res_high]) + (par[...].astype(f32) + rec[...].astype(f32))
        factor = lax.rsqrt(jnp.mean(rows * rows, axis=-1, keepdims=True) + epsilon)
        store_rows([hid_low, hid_high], rows)
        store_rows([norm_low, norm_high], rows * factor * gain_ref[...])

    mine, _ = row_specs(seqs, own_len, half)
    full, full_theirs = row_specs(seqs, own_len, width)
    tokens = seqs * 2 * own_len
    outs = pl.pallas_call(
        kernel,
        out_shape=[jax.ShapeDtypeStruct((seqs, 2, own_len, half), bf16)] * 4,
        grid=(seqs, 2),
        in_specs=[mine, mine, full, full_theirs, pl.BlockSpec((1, width), lambda s, h: (0, 0))],
        out_specs=[mine] * 4,
        compiler_params=params(2),
        cost_estimate=cost(10 * tokens * width, 10 * tokens * width),
        name="middle",
    )(
        *[r.reshape(seqs, 2, own_len, half) for r in resid],
        *[r.reshape(seqs, 2, own_len, width) for r in (partial, received)],
        gain,
    )
    outs = [o.reshape(tokens, half) for o in outs]
    return outs[:2], outs[2:]


def middle_back(grad, hidden, partial, received, gain, which, seqs):
    length, width = partial.shape
    half, own_len = width // 2, length // 2

    def kernel(gra_low, gra_high, hid_low, hid_high, par, rec, gain_ref, out_low, out_high):
        rows = load_rows([hid_low, hid_high])
        factor = lax.rsqrt(jnp.mean(rows * rows, axis=-1, keepdims=True) + epsilon)
        unit = rows * factor
        scaled = (par[...].astype(f32) + rec[...].astype(f32)) * gain_ref[...]
        spread = jnp.mean(scaled * unit, axis=-1, keepdims=True)
        store_rows([out_low, out_high], load_rows([gra_low, gra_high]) + factor * (scaled - unit * spread))

    whole = pl.BlockSpec((None, None, own_len, half), lambda h: (which, h, 0, 0))
    mine = pl.BlockSpec((None, own_len, width), lambda h: (h, 0, 0))
    theirs = pl.BlockSpec((None, own_len, width), lambda h: (1 - h, 0, 0))
    out = pl.BlockSpec((own_len, half), lambda h: (h, 0))
    return pl.pallas_call(
        kernel,
        out_shape=[jax.ShapeDtypeStruct((length, half), bf16)] * 2,
        grid=(2,),
        in_specs=[whole] * 4 + [mine, theirs, pl.BlockSpec((1, width), lambda h: (0, 0))],
        out_specs=[out, out],
        compiler_params=params(),
        cost_estimate=cost(20 * length * width, 10 * length * width),
        name="middle_back",
    )(
        *[r.reshape(seqs, 2, own_len, half) for r in list(grad) + list(hidden)],
        *[r.reshape(2, own_len, width) for r in (partial, received)],
        gain,
    )


def leave(slots, residual, partial, received, norm):
    seqs, own_len, width = received.shape
    half = width // 2
    blocks = slots.shape[0]
    block = width // blocks
    narrow = block % LANES != 0

    def kernel(slots_ref, *refs):
        out_ref = refs[-1]
        total = refs[2][...].astype(f32) + refs[3][...].astype(f32)
        if norm is not None:
            rows = load_rows(refs[4:6])
            factor = lax.rsqrt(jnp.mean(rows * rows, axis=-1, keepdims=True) + epsilon)
            unit = rows * factor
            scaled = total * refs[6][...]
            spread = jnp.mean(scaled * unit, axis=-1, keepdims=True)
            total = factor * (scaled - unit * spread)
        total = load_rows(refs[:2]) + total
        for b in range(blocks):
            start = b * block if narrow else pl.multiple_of(slots_ref[b] * block, block)
            out_ref[:, pl.ds(start, block)] = total[:, b * block : (b + 1) * block].astype(bf16)

    mine = pl.BlockSpec((None, None, own_len, half), lambda s, t: (s, 0, 0, 0))
    full = pl.BlockSpec((None, None, own_len, width), lambda s, t: (s, 0, 0, 0))
    whole = pl.BlockSpec((None, own_len, width), lambda s, t: (s, 0, 0))
    arrays = [r.reshape(seqs, 2, own_len, half) for r in residual]
    arrays += [partial.reshape(seqs, 2, own_len, width), received]
    specs = [mine, mine, full, whole]
    if norm is not None:
        arrays += [r.reshape(seqs, 2, own_len, half) for r in norm[0]] + [norm[1]]
        specs += [mine, mine, pl.BlockSpec((1, width), lambda s, t: (0, 0))]
    out = pl.pallas_call(
        kernel,
        out_shape=jax.ShapeDtypeStruct((seqs, own_len, width), bf16),
        grid_spec=pltpu.PrefetchScalarGridSpec(
            num_scalar_prefetch=1, grid=(seqs,), in_specs=specs, out_specs=whole
        ),
        compiler_params=params(),
        cost_estimate=cost(20 * seqs * own_len * width, 12 * seqs * own_len * width),
        name="leave",
    )(slots, *arrays)
    if narrow:
        out = out.reshape(seqs, own_len, blocks, block)[:, :, jnp.argsort(slots)].reshape(seqs, own_len, width)
    return out


def shards(
    inputs,
    block_ids,
    positions,
    w_query,
    key_weight,
    value_weight,
    w_out,
    w_gate,
    w_up,
    w_down,
    attn_gain,
    mlp_gain,
    out_grad,
):
    seqs, own_len, width = inputs.shape
    length = block_ids.shape[1]
    tokens = seqs * length
    side = lax.axis_index("tensor")
    hd = HEAD_SIZE
    heads = w_query.shape[1] // hd
    kv = key_weight.shape[1] // hd
    ff = w_gate.shape[1]
    ring = Ring(lax.axis_size("dp"))
    rows = width // ring.size
    slots = ring.slots(lax.axis_index("dp"))

    def across(value):
        return lax.ppermute(value, "tensor", [(0, 1), (1, 0)])

    def halves(table):
        table = table.reshape(seqs, 2, own_len)
        return jnp.where(side == 0, table, table[:, ::-1]).reshape(seqs, length)

    segments = halves(block_ids)
    seg_row, seg_col = segments[:, None, :], segments[:, :, None]
    steps_half = jnp.arange(hd // 2, dtype=f32)
    frequency = jnp.exp(steps_half * (-2.0 * math.log(rope_base) / hd))
    angles = halves(positions).reshape(tokens, 1).astype(f32) * frequency
    cos_head, sin_head = jnp.tile(jnp.cos(angles), (1, 2)), jnp.tile(jnp.sin(angles), (1, 2))
    kv_wide = kv * hd
    cosine = jnp.concatenate([jnp.tile(cos_head, (1, TILE // hd + kv)), jnp.ones((tokens, kv_wide), f32)], axis=1)
    sine = jnp.concatenate([jnp.tile(sin_head, (1, TILE // hd + kv)), jnp.zeros((tokens, kv_wide), f32)], axis=1)

    blocks = ff // TILE
    cut = (blocks + 1) // 2
    q_cols = heads * hd
    qkv_cols = q_cols + 2 * kv_wide
    out_cols = w_out.shape[0]

    def interleave(first, last):
        parts = [w[:, j * TILE : (j + 1) * TILE] for j in range(first, last) for w in (w_gate, w_up)]
        return jnp.concatenate(parts, axis=1)

    gain_block = jnp.pad(jnp.stack([attn_gain, mlp_gain], axis=1), ((0, 0), (0, LANES - 2)))
    qkv_shard = jnp.concatenate([w_query, key_weight, value_weight], axis=1)
    step = Steps()

    def other(part):
        return part.reshape(seqs, 2, own_len, width)[:, 1]

    def both_sides(mine, theirs):
        out = jnp.stack([step(mine), theirs], axis=1).reshape(tokens, width)
        step.mark(out)
        return out

    own_rows = inputs.reshape(seqs, own_len, width)
    own_grad = out_grad.reshape(seqs, own_len, width)
    go_q = Gather(ring, jnp.concatenate([qkv_shard, gain_block], axis=1))
    go_q.send()
    got_rows = across(own_rows)
    down_shard = w_down.T
    down_pair = ring.pair(down_shard)
    go_o = Gather(ring, w_out.T)
    go_o.send()
    go_q.finish(step)
    go_q.join(step)
    go_q.send()
    go_a = Gather(ring, interleave(0, cut))
    go_b = Gather(ring, interleave(cut, blocks))
    step.mark(go_a.held, go_b.held, go_q.held)
    stacked = both_sides(own_rows, tie(got_rows, down_pair))
    near_q = go_q.join(step)
    far_q = ring.pair(near_q)
    got_grad = across(tie(own_grad, near_q))
    go_o.finish(step)
    go_o.join(step)
    go_o.send()
    go_a.held = step(go_a.held)
    go_a.send()
    near_o = go_o.join(step)
    far_o = ring.pair(near_o)
    core_near_q = ring.core(tie(near_q, near_o))
    go_a.finish(step)
    go_a.join(step)
    go_a.send()
    wq = [near_q, far_q, core_near_q, ring.core(tie(far_q, core_near_q))]
    attn_gain_f, mlp_gain_f = gain_rows([step(wq[0])] + wq[1:], qkv_cols)
    step.mark(mlp_gain_f)
    entered = enter(step(stacked), slots, attn_gain_f)
    resid, normed = entered[:2], entered[2:]
    step.mark(resid[0])
    stacked_grad = both_sides(own_grad, got_grad)
    go_b.held = step(go_b.held)
    go_b.send()
    qkv = project_qkv([step(normed[0]), normed[1]], wq, cosine, sine, 0, qkv_cols)
    step.mark(qkv)
    near_a = go_a.join(step)
    far_a = ring.pair(tie(near_a, far_o))
    wo = [near_o, far_o, ring.core(tie(near_o, near_a)), ring.core(tie(far_o, near_a))]
    context, lse = attention_forward(step(qkv), seg_row, seg_col, seqs, heads, kv)
    step.mark(context)
    out_part = project_back([step(context)], [wo])
    step.mark(out_part)
    got_out = across(out_part)
    core_near_a = ring.core(tie(near_a, out_part))
    grad = enter(step(stacked_grad), slots, None)
    step.mark(grad[0])
    go_b.finish(step)
    go_b.join(step)
    go_b.send()
    columns_1 = cut * TILE
    pair_1 = jnp.concatenate([step(down_shard)[:, :columns_1], down_pair[:, :columns_1]], axis=0)
    pair_2 = jnp.concatenate([down_shard[:, columns_1:], down_pair[:, columns_1:]], axis=0)
    step.mark(pair_1, pair_2)
    go_1, go_2 = Gather(ring, pair_1), Gather(ring, pair_2)
    go_1.send()
    near_b = go_b.join(step)
    far_b = ring.pair(tie(near_b, far_a))
    go_1.finish(step)
    go_1.join(step)
    go_1.send()
    go_2.held = step(go_2.held)
    go_2.send()
    hidden, normed_mlp = middle(resid, out_part, step(got_out, core_near_a), mlp_gain_f, seqs, own_len)
    step.mark(hidden[0])
    wa = [near_a, far_a, core_near_a, ring.core(tie(far_a, got_out))]
    gu_mid_a, active_1 = gate_up([step(normed_mlp[0]), normed_mlp[1]], wa)
    step.mark(active_1)

    def parted(held):
        held = held.reshape(ring.line, 2, rows, held.shape[1])
        out = [held[:, p].reshape(ring.line * rows, held.shape[3]) for p in range(2)]
        step.mark(*out)
        return out

    go_1.join(step)
    near_1, far_1 = parted(go_1.held)
    go_2.finish(step)
    go_2.join(step)
    go_2.send()
    core_near_b = ring.core(tie(near_b, near_1))
    down_1 = Reduce(ring, step, grad, active_1)
    down_1.far()
    wb = [near_b, far_b, core_near_b, ring.core(tie(far_b, core_near_b))]
    gu_mid_b, active_2 = gate_up([step(normed_mlp[0], down_1.from_core), normed_mlp[1]], wb)
    step.mark(active_2)
    wd_1 = [near_1, far_1, ring.core(tie(near_1, active_2)), ring.core(tie(far_1, active_2))]
    down_1.side()
    down_2 = Reduce(ring, step, grad, active_2)
    down_2.far()
    dgu_a = swiglu_back([step(grad[0]), grad[1]], wd_1, gu_mid_a)
    step.mark(dgu_a)
    go_2.join(step)
    near_2, far_2 = parted(go_2.held)
    wd_2 = [near_2, far_2, ring.core(near_2), ring.core(far_2)]
    down_2.side()
    gate_a = Reduce(ring, step, normed_mlp, dgu_a)
    gate_a.far()
    dgu_b = swiglu_back([step(grad[0]), grad[1]], wd_2, gu_mid_b)
    step.mark(dgu_b)

    dn = [None] * seqs
    got_dn = [None] * seqs
    attn_grads, d_qkvs = [None] * seqs, [None] * seqs

    def dn_part(which):
        dn[which] = project_back([step(dgu_a), dgu_b], [wa, wb], None, (which, seqs))
        step.mark(dn[which])
        got_dn[which] = across(dn[which])

    def attend_back(which):
        ag = middle_back(grad, hidden, dn[which], step(got_dn[which]), mlp_gain_f, which, seqs)
        d_context = project(ag, wo, out_cols)
        attn_grads[which] = ag
        out = attention_backward(
            qkv, d_context, lse, seg_row, seg_col, cosine[:, :LANES], sine[:, :LANES], which, heads, kv
        )
        d_qkvs[which] = out
        step.mark(out)

    gate_b = Reduce(ring, step, normed_mlp, dgu_b)
    dn_part(0)
    gate_a.side()
    down_1.near()
    down_1.fold()
    for which in range(1, seqs):
        dn_part(which)
    down_1.fold()
    gate_b.far()
    attend_back(0)
    grad_1 = down_1.fold_rest()
    gate_b.side()
    down_2.near()
    down_2.fold()
    gate_a.near()
    down_2.fold()
    for which in range(1, seqs):
        attend_back(which)
    grad_2 = down_2.fold_rest()
    attn_grad = [jnp.concatenate([ag[h] for ag in attn_grads], axis=0) for h in range(2)]
    d_qkv = jnp.concatenate(d_qkvs, axis=0)
    out_grads = Reduce(ring, step, attn_grad, context)
    qkv_grads = Reduce(ring, step, normed, d_qkv)
    out_grads.far()
    qkv_grads.far()
    gate_a.fold()
    out_grads.side()
    qkv_grads.side()
    in_part = project_back([step(d_qkv)], [wq])
    step.mark(in_part)
    got_in = across(other(in_part))
    gate_a.fold()
    mlp_part = project_back([step(active_1), active_2], [wd_1, wd_2])
    step.mark(mlp_part)
    grad_a = gate_a.fold_rest()
    gate_b.near()
    gate_b.fold()
    input_grad = leave(slots, attn_grad, in_part, step(got_in), (resid, attn_gain_f))
    step.mark(input_grad)
    got_mlp = across(tie(other(mlp_part), input_grad))
    out_grads.near()
    out_grads.fold()
    gate_b.fold()
    qkv_grads.near()
    qkv_grads.fold()
    out_grads.fold()
    grad_b = gate_b.fold_rest()
    grad_out = out_grads.fold_rest()
    output = leave(slots, hidden, mlp_part, step(got_mlp), None)
    step.mark(output)
    qkv_grads.fold()
    grad_qkv = qkv_grads.fold_rest()

    def pick(which):
        parts = [
            g[:, (2 * j + which) * TILE : (2 * j + which + 1) * TILE]
            for g, count in ((grad_a, cut), (grad_b, blocks - cut))
            for j in range(count)
        ]
        return jnp.concatenate(parts, axis=1)

    grad_gate, grad_up = pick(0), pick(1)

    def gain_sum(weights, grads, gain):
        total = sum(jnp.sum(w.astype(f32) * g, axis=1) for w, g in zip(weights, grads))
        return total / gain.astype(f32)

    gain_sums = jnp.stack([
        gain_sum([qkv_shard], [grad_qkv], attn_gain),
        gain_sum([w_gate, w_up], [grad_gate, grad_up], mlp_gain),
    ])
    gain_sums = gain_sums + across(gain_sums)
    return (
        output,
        input_grad,
        grad_qkv[:, :q_cols],
        grad_qkv[:, q_cols : q_cols + kv_wide],
        grad_qkv[:, q_cols + kv_wide :],
        grad_out.T,
        grad_gate,
        grad_up,
        jnp.concatenate([grad_1, grad_2], axis=1).T,
        gain_sums[0],
        gain_sums[1],
    )


def solution(mesh):
    row, col = P("dp", "tensor"), P("tensor", "dp")
    seq = P("dp", "tensor", None)
    return jax.shard_map(
        shards,
        mesh=mesh,
        in_specs=(seq, P("dp", None), P("dp", None), row, row, row, col, row, row, col, P("dp"), P("dp"), seq),
        out_specs=(seq, seq, row, row, row, col, row, row, col, P("dp"), P("dp")),
        check_vma=False,
    )
```

```python
import functools
import math

import jax
import jax.numpy as jnp
from jax import lax
from jax.experimental import pallas as pl
from jax.experimental.pallas import tpu as pltpu
from jax.sharding import PartitionSpec as P

HEAD_SIZE = 64
LANES = 128
TILE = 256
epsilon = 1e-05
rope_base = 10000.0
masked_value = -1e30
bf16 = jnp.bfloat16
f32 = jnp.float32
VMEM_LIMIT = 60 * 1024 * 1024


def dot(left, right, left_dim, right_dim):
    return lax.dot_general(
        left, right, (((left_dim,), (right_dim,)), ((), ())), preferred_element_type=f32
    )


def tie(value, *others):
    return lax.optimization_barrier((value,) + others)[0]


def params(steps=1):
    return pltpu.CompilerParams(
        dimension_semantics=("arbitrary",) * steps, vmem_limit_bytes=VMEM_LIMIT
    )


def resident(shape):
    return pl.BlockSpec(
        shape, lambda *_: (0,) * len(shape), pipeline_mode=pl.Buffered(1)
    )


def cost(flops, moved, trans=0):
    return pl.CostEstimate(flops=flops // 4 + 1, bytes_accessed=moved // 4 + 1, transcendentals=0)


class Ring:
    def __init__(self, size):
        self.size = size
        self.line = size // 4
        self.reaches = [self.line >> k for k in range(1, self.line.bit_length())]

    def swap(self, value, bits):
        return lax.ppermute(value, "dp", [(i, i ^ bits) for i in range(self.size)])

    def core(self, value):
        return self.swap(value, 1)

    def pair(self, value):
        return self.swap(value, 2)

    def along(self, value, reach):
        return self.swap(value, 4 * reach)

    def slots(self, me):
        order = [0]
        for reach in self.reaches:
            order = order + [o ^ reach for o in order]
        return jnp.stack([me ^ (l * 4 + p * 2 + c) for c in range(2) for p in range(2) for l in order])

    def gather_far(self, shard):
        held = shard
        for reach in self.reaches[:-1]:
            held = jnp.concatenate([held, self.along(held, reach)], axis=0)
        return held[shard.shape[0] :] if self.line > 4 else self.along(shard, 2)


def fence(values):
    keys = sorted(values)
    values.update(zip(keys, lax.optimization_barrier([values[k] for k in keys])))


def joined(*parts):
    return jnp.concatenate(parts, axis=0)


class Reduce:
    def __init__(self, ring, values, name, acts, grads):
        self.ring, self.v, self.name, self.acts, self.grads = ring, values, name, acts, grads

    def get(self, key):
        return self.v[self.name + key]

    def put(self, key, value):
        self.v[self.name + key] = value

    def part(self, half, which=None):
        act = self.v[self.acts][half]
        if which is not None:
            quarter = act.shape[1] // 2
            act = act[:, which * quarter : (which + 1) * quarter]
        return dot(act, self.v[self.grads], 0, 0)

    def far(self):
        self.put(".far", self.part(1).astype(bf16))

    def send_far(self):
        self.put(".far", self.ring.core(self.get(".far")))

    def side(self):
        far = self.get(".far")
        quarter = far.shape[0] // 2
        out = (self.part(0, 1) + far[quarter:].astype(f32)).astype(bf16)
        self.put(".side", self.ring.pair(out))

    def near(self):
        side = self.get(".side")
        out = self.part(0, 0) + self.get(".far")[: side.shape[0]].astype(f32) + side.astype(f32)
        half = out.shape[0] // 2
        self.put(".far", out[:half].astype(bf16))
        self.put(".side", self.ring.along(out[half:].astype(bf16), 1))

    def fold(self):
        terms, reach = [self.get(".far"), self.get(".side")], 2
        while True:
            rows = terms[0].shape[0] // 2
            got = self.ring.along(sum(t[rows:].astype(f32) for t in terms).astype(bf16), reach)
            terms, reach = [t[:rows] for t in terms] + [got], reach * 2
            if reach == self.ring.line:
                break
        self.put(".far", sum(t.astype(f32) for t in terms[:-1]))
        self.put(".side", terms[-1])

    def rows(self):
        out = self.get(".far") + self.get(".side").astype(f32)
        del self.v[self.name + ".far"], self.v[self.name + ".side"]
        self.put("", out)


def enter(rows, slots, gain):
    count, width = rows.shape
    blocks = slots.shape[0]
    block = width // blocks
    per = blocks // 2
    half = width // 2
    step = count // 4
    norm = gain is not None
    narrow = block % LANES != 0
    if narrow:
        rows = rows.reshape(count, blocks, block)[:, slots].reshape(count, width)

    def kernel(slots_ref, x_ref, gain_ref, *outs):
        if norm:
            x = x_ref[...].astype(f32)
            factor = lax.rsqrt(jnp.mean(x * x, axis=-1, keepdims=True) + epsilon)
        for b in range(blocks):
            start = b * block if narrow else pl.multiple_of(slots_ref[b] * block, block)
            piece = x_ref[:, pl.ds(start, block)]
            at = slice((b % per) * block, (b % per + 1) * block)
            outs[b // per][:, at] = piece
            if norm:
                g = gain_ref[:, b * block : (b + 1) * block]
                outs[2 + b // per][:, at] = (piece.astype(f32) * factor * g).astype(bf16)

    n_out = 4 if norm else 2
    if gain is None:
        gain = jnp.ones((1, width), f32)
    return pl.pallas_call(
        kernel,
        out_shape=[jax.ShapeDtypeStruct((count, half), bf16)] * n_out,
        grid_spec=pltpu.PrefetchScalarGridSpec(
            num_scalar_prefetch=1,
            grid=(4,),
            in_specs=[
                pl.BlockSpec((step, width), lambda i, s: (i, 0)),
                pl.BlockSpec((1, width), lambda i, s: (0, 0)),
            ],
            out_specs=[pl.BlockSpec((step, half), lambda i, s: (i, 0))] * n_out,
        ),
        compiler_params=params(),
        cost_estimate=cost(10 * count * width, 2 * count * width * (1 + n_out // 2)),
        name="enter",
    )(slots, rows, gain)


def qkv_kernel(*refs):
    cos_ref, sin_ref, out_ref = refs[4:]
    raw = times_pieces(refs[:2], refs[2:4])
    lane = lax.broadcasted_iota(jnp.int32, raw.shape, 1) % HEAD_SIZE
    half = HEAD_SIZE // 2
    ahead = pltpu.roll(raw, raw.shape[1] - half, 1)
    behind = pltpu.roll(raw, half, 1)
    turned = jnp.where(lane < half, -ahead, behind)
    out_ref[...] = (raw * cos_ref[...] + turned * sin_ref[...]).astype(bf16)


def project_qkv(acts, weights, cosine, sine, first, columns):
    tokens, part = acts[0].shape
    steps = columns // TILE
    table = pl.BlockSpec((tokens, TILE), lambda j: (0, j // (steps - 1)))
    depth = weights[0].shape[0]
    return pl.pallas_call(
        qkv_kernel,
        out_shape=jax.ShapeDtypeStruct((tokens, columns), bf16),
        grid=(steps,),
        in_specs=[resident((tokens, part))] * 2
        + [pl.BlockSpec((depth, TILE), lambda j: (0, first + j))] * 2
        + [table, table],
        out_specs=pl.BlockSpec((tokens, TILE), lambda j: (0, j)),
        compiler_params=params(),
        cost_estimate=cost(8 * tokens * depth * columns, 8 * depth * columns + 4 * tokens * part),
        name="project_qkv",
    )(*acts, *weights, cosine, sine)


def times_pieces(acts, weights):
    return sum(dot(a[...], w[...], 1, 0) for a, w in zip(acts, weights))


def project_kernel(*refs):
    refs[4][...] = times_pieces(refs[:2], refs[2:4]).astype(bf16)


def project(acts, weights, columns):
    tokens, part = acts[0].shape
    depth = weights[0].shape[0]
    return pl.pallas_call(
        project_kernel,
        out_shape=jax.ShapeDtypeStruct((tokens, columns), bf16),
        grid=(columns // TILE,),
        in_specs=[resident((tokens, part))] * 2 + [pl.BlockSpec((depth, TILE), lambda j: (0, j))] * 2,
        out_specs=pl.BlockSpec((tokens, TILE), lambda j: (0, j)),
        compiler_params=params(),
        cost_estimate=cost(8 * tokens * depth * columns, 8 * depth * columns + 4 * tokens * part),
        name="project",
    )(*acts, *weights)


def project_back(acts, weights, firsts=None, part=(0, 1)):
    tokens = acts[0].shape[0] // part[1]
    depth = weights[0][0].shape[0]
    steps = depth // TILE
    count = len(acts)
    firsts = firsts or [0] * count
    wides = [a.shape[1] if not f else math.gcd(a.shape[1], f) for a, f in zip(acts, firsts)]
    parts = [(n, f // w + j, w, j) for n, (a, f, w) in enumerate(zip(acts, firsts, wides)) for j in range(a.shape[1] // w)]
    total = len(parts)

    def kernel(*refs):
        acts_in, out_ref = refs[:count], refs[-1]
        for p in range(2):
            pieces = refs[count + p * total : count + (p + 1) * total]

            @pl.when(pl.program_id(0) // steps == p)
            def _():
                out_ref[...] = sum(
                    dot(acts_in[n][:, j * w : (j + 1) * w], piece[...], 1, 1)
                    for (n, _, w, j), piece in zip(parts, pieces)
                ).astype(bf16)

    def spec(p, block, wide):
        return pl.BlockSpec((TILE, wide), lambda i: (jnp.clip(i - p * steps, 0, steps - 1), block))

    columns = sum(a.shape[1] for a in acts)
    return pl.pallas_call(
        kernel,
        out_shape=jax.ShapeDtypeStruct((tokens, 2 * depth), bf16),
        grid=(2 * steps,),
        in_specs=[
            pl.BlockSpec((tokens, a.shape[1]), lambda i: (part[0], 0), pipeline_mode=pl.Buffered(1)) for a in acts
        ]
        + [spec(p, block, w) for p in range(2) for _, block, w, _ in parts],
        out_specs=pl.BlockSpec((tokens, TILE), lambda i: (0, i)),
        compiler_params=params(),
        cost_estimate=cost(8 * tokens * depth * columns, (8 * depth + 2 * tokens) * columns),
        name="project_back",
    )(*acts, *[weights[n][p] for p in range(2) for n, _, _, _ in parts])


def gain_rows(pieces, first):
    depth = pieces[0].shape[0]

    def kernel(*refs):
        for p in range(2):
            refs[2][:, p * depth : (p + 1) * depth] = refs[p][...].astype(f32).T[:8]

    out = pl.pallas_call(
        kernel,
        out_shape=jax.ShapeDtypeStruct((8, 2 * depth), f32),
        grid=(1,),
        in_specs=[pl.BlockSpec((depth, LANES), lambda i: (0, first // LANES))] * 2,
        out_specs=pl.BlockSpec((8, 2 * depth), lambda i: (0, 0)),
        compiler_params=params(),
        name="gain_rows",
    )(*pieces)
    return out[:1], out[1:2]


def forward_kernel(q_ref, kv_ref, seg_row, seg_col, ctx_ref, lse_ref):
    kv_heads = kv_ref.shape[1] // (2 * HEAD_SIZE)
    group = pl.program_id(1)
    keys = kv_ref[:, : kv_heads * HEAD_SIZE].astype(f32)
    values = kv_ref[:, kv_heads * HEAD_SIZE :].astype(f32)
    lane = lax.broadcasted_iota(jnp.int32, keys.shape, 1)
    low = lane < HEAD_SIZE
    here = low == (group == 0)
    both_keys = jnp.where(here, keys, pltpu.roll(keys, HEAD_SIZE, 1)).astype(bf16)
    both_values = jnp.where(here, values, pltpu.roll(values, HEAD_SIZE, 1)).astype(bf16)
    none = jnp.zeros_like(both_values)
    value_low = jnp.where(low, both_values, none)
    value_high = jnp.where(low, none, both_values)
    allowed = seg_row[...] <= seg_col[...]
    pairs = q_ref.shape[1] // (2 * HEAD_SIZE)
    for pair in range(pairs):
        cut = slice(pair * LANES, (pair + 1) * LANES)
        q = q_ref[:, cut] * bf16(HEAD_SIZE ** (-0.5))
        total = None
        for side, values_here in ((0, value_low), (1, value_high)):
            mine = jnp.where(low, q, none) if side == 0 else jnp.where(low, none, q)
            scores = jnp.where(allowed, dot(mine, both_keys, 1, 1), masked_value)
            top = jnp.max(scores, axis=-1, keepdims=True)
            weights = jnp.exp(scores - top)
            mass = jnp.sum(weights, axis=-1, keepdims=True)
            probs = (weights * (1.0 / mass)).astype(bf16)
            part = dot(probs, values_here, 1, 0)
            total = part if total is None else total + part
            lse_ref[:, 2 * pair + side : 2 * pair + side + 1] = top + jnp.log(mass)
        ctx_ref[:, cut] = total.astype(bf16)


def attention_forward(qkv, seg_row, seg_col, seqs, heads, kv):
    tokens = qkv.shape[0]
    length = tokens // seqs
    wide = heads // kv * HEAD_SIZE
    last = heads * HEAD_SIZE // (2 * kv * HEAD_SIZE)
    return pl.pallas_call(
        forward_kernel,
        out_shape=[
            jax.ShapeDtypeStruct((tokens, heads * HEAD_SIZE), bf16),
            jax.ShapeDtypeStruct((kv, tokens, heads // kv), f32),
        ],
        grid=(seqs, kv),
        in_specs=[
            pl.BlockSpec((length, wide), lambda s, g: (s, g)),
            pl.BlockSpec((length, 2 * kv * HEAD_SIZE), lambda s, g: (s, last)),
            pl.BlockSpec((None, 1, length), lambda s, g: (s, 0, 0)),
            pl.BlockSpec((None, length, 1), lambda s, g: (s, 0, 0)),
        ],
        out_specs=[
            pl.BlockSpec((length, wide), lambda s, g: (s, g)),
            pl.BlockSpec((None, length, heads // kv), lambda s, g: (g, s, 0)),
        ],
        compiler_params=params(2),
        cost_estimate=cost(16 * tokens * length * heads * HEAD_SIZE, 6 * tokens * heads * HEAD_SIZE),
        name="attention_forward",
    )(qkv, qkv, seg_row, seg_col)


def backward_kernel(q_ref, kv_ref, dctx_ref, lse_ref, seg_row, seg_col, cos_ref, sin_ref, out_ref):
    kv_heads = kv_ref.shape[1] // (2 * HEAD_SIZE)
    group = pl.program_id(0)
    wide = q_ref.shape[1]
    q_cols = kv_heads * wide
    scale = HEAD_SIZE ** (-0.5)
    half = HEAD_SIZE // 2
    keys = kv_ref[:, : kv_heads * HEAD_SIZE].astype(f32)
    values = kv_ref[:, kv_heads * HEAD_SIZE :].astype(f32)
    lane = lax.broadcasted_iota(jnp.int32, keys.shape, 1)
    low = lane < HEAD_SIZE
    here = low == (group == 0)
    both_keys = jnp.where(here, keys, pltpu.roll(keys, HEAD_SIZE, 1)).astype(bf16)
    both_values = jnp.where(here, values, pltpu.roll(values, HEAD_SIZE, 1)).astype(bf16)
    none = jnp.zeros_like(both_keys)
    key_low = jnp.where(low, both_keys, none)
    key_high = jnp.where(low, none, both_keys)
    allowed = seg_row[...] <= seg_col[...]
    cosine, sine = cos_ref[...], sin_ref[...]

    def unrotate(rows):
        turned = rows * sine
        ahead = pltpu.roll(turned, LANES - half, 1)
        behind = pltpu.roll(turned, half, 1)
        return rows * cosine + jnp.where(lane % HEAD_SIZE < half, ahead, -behind)

    dkey = jnp.zeros(keys.shape, f32)
    dvalue = jnp.zeros(keys.shape, f32)
    pairs = q_ref.shape[1] // LANES
    for pair in range(pairs):
        cut = slice(pair * LANES, (pair + 1) * LANES)
        q = q_ref[:, cut] * bf16(scale)
        dctx = dctx_ref[:, cut]
        dquery = None
        for side, keys_here in ((0, key_low), (1, key_high)):
            mine = jnp.where(low, q, none) if side == 0 else jnp.where(low, none, q)
            dmine = jnp.where(low, dctx, none) if side == 0 else jnp.where(low, none, dctx)
            scores = jnp.where(allowed, dot(mine, both_keys, 1, 1), masked_value)
            probs = jnp.exp(scores - lse_ref[:, 2 * pair + side : 2 * pair + side + 1])
            dprobs = dot(dmine, both_values, 1, 1)
            delta = jnp.sum(probs * dprobs, axis=-1, keepdims=True)
            dscores = (probs * (dprobs - delta)).astype(bf16)
            part = dot(dscores, keys_here, 1, 0)
            dquery = part if dquery is None else dquery + part
            dkey = dkey + dot(dscores, mine, 0, 0)
            dvalue = dvalue + dot(probs.astype(bf16), dmine, 0, 0)
        start = pl.multiple_of(group * wide + pair * LANES, LANES)
        out_ref[:, pl.ds(start, LANES)] = unrotate(dquery * scale).astype(bf16)
    dkey = unrotate(dkey + pltpu.roll(dkey, HEAD_SIZE, 1)).astype(bf16)
    dvalue = (dvalue + pltpu.roll(dvalue, HEAD_SIZE, 1)).astype(bf16)

    key_cut, value_cut = slice(q_cols, q_cols + LANES), slice(q_cols + LANES, q_cols + 2 * LANES)

    @pl.when(group == 0)
    def _():
        out_ref[:, key_cut] = dkey
        out_ref[:, value_cut] = dvalue

    @pl.when(group == 1)
    def _():
        out_ref[:, key_cut] = jnp.where(low, out_ref[:, key_cut], dkey)
        out_ref[:, value_cut] = jnp.where(low, out_ref[:, value_cut], dvalue)


def attention_backward(qkv, dctx, lse, seg_row, seg_col, cosine, sine, which, heads, kv):
    length = dctx.shape[0]
    wide = heads // kv * HEAD_SIZE
    columns = qkv.shape[1]
    last = heads * HEAD_SIZE // (2 * kv * HEAD_SIZE)
    table = pl.BlockSpec((length, LANES), lambda g: (which, 0))
    return pl.pallas_call(
        backward_kernel,
        out_shape=jax.ShapeDtypeStruct((length, columns), bf16),
        grid=(kv,),
        in_specs=[
            pl.BlockSpec((length, wide), lambda g: (which, g)),
            pl.BlockSpec((length, 2 * kv * HEAD_SIZE), lambda g: (which, last)),
            pl.BlockSpec((length, wide), lambda g: (0, g)),
            pl.BlockSpec((None, length, heads // kv), lambda g: (g, which, 0)),
            pl.BlockSpec((None, 1, length), lambda g: (which, 0, 0)),
            pl.BlockSpec((None, length, 1), lambda g: (which, 0, 0)),
            table,
            table,
        ],
        out_specs=pl.BlockSpec((length, columns), lambda g: (0, 0)),
        compiler_params=params(),
        cost_estimate=cost(40 * length * length * heads * HEAD_SIZE, 10 * length * heads * HEAD_SIZE),
        name="attention_backward",
    )(qkv, qkv, dctx, lse, seg_row, seg_col, cosine, sine)


def gate_up(acts, first, second):
    tokens, part = acts[0].shape
    depth = first[0].shape[0]
    steps = [w[0].shape[1] // (2 * TILE) for w in (first, second)]

    def kernel(*refs):
        outs, active_ref = refs[6:8], refs[8]

        def fill(weights, gu_ref):
            both = times_pieces(refs[:2], weights)
            gate, up = both[:, :TILE], both[:, TILE:]
            gu_ref[...] = both.astype(bf16)
            active_ref[...] = (gate * (1.0 / (1.0 + jnp.exp(-gate))) * up).astype(bf16)

        pl.when(pl.program_id(0) < steps[0])(lambda: fill(refs[2:4], outs[0]))
        pl.when(pl.program_id(0) >= steps[0])(lambda: fill(refs[4:6], outs[1]))

    def low(j):
        return jnp.minimum(j, steps[0] - 1)

    def high(j):
        return jnp.maximum(j - steps[0], 0)

    columns = 2 * TILE * sum(steps)
    return pl.pallas_call(
        kernel,
        out_shape=[jax.ShapeDtypeStruct((tokens, 2 * TILE * n), bf16) for n in steps]
        + [jax.ShapeDtypeStruct((tokens, TILE * sum(steps)), bf16)],
        grid=(sum(steps),),
        in_specs=[resident((tokens, part))] * 2
        + [pl.BlockSpec((depth, 2 * TILE), lambda j: (0, low(j)))] * 2
        + [pl.BlockSpec((depth, 2 * TILE), lambda j: (0, high(j)))] * 2,
        out_specs=[
            pl.BlockSpec((tokens, 2 * TILE), lambda j: (0, low(j))),
            pl.BlockSpec((tokens, 2 * TILE), lambda j: (0, high(j))),
            pl.BlockSpec((tokens, TILE), lambda j: (0, j)),
        ],
        compiler_params=params(),
        cost_estimate=cost(4 * tokens * depth * columns, 4 * depth * columns + 4 * tokens * columns, tokens * columns),
        name="gate_up",
    )(*acts, *first, *second)


def swiglu_back(acts, weights, first, second):
    tokens, part = acts[0].shape
    depth = weights[0].shape[0]
    steps = [u.shape[1] // (2 * TILE) for u in (first, second)]

    def kernel(*refs):
        d_active = times_pieces(refs[:2], refs[2:4])

        def fill(gu_ref, out_ref):
            gate, up = gu_ref[:, :TILE].astype(f32), gu_ref[:, TILE:].astype(f32)
            sig = 1.0 / (1.0 + jnp.exp(-gate))
            out_ref[:, :TILE] = (d_active * up * sig * (1.0 + gate * (1.0 - sig))).astype(bf16)
            out_ref[:, TILE:] = (d_active * (gate * sig)).astype(bf16)

        pl.when(pl.program_id(0) < steps[0])(lambda: fill(refs[4], refs[6]))
        pl.when(pl.program_id(0) >= steps[0])(lambda: fill(refs[5], refs[7]))

    def low(j):
        return jnp.minimum(j, steps[0] - 1)

    def high(j):
        return jnp.maximum(j - steps[0], 0)

    columns = 2 * TILE * sum(steps)
    wide = [
        pl.BlockSpec((tokens, 2 * TILE), lambda j: (0, low(j))),
        pl.BlockSpec((tokens, 2 * TILE), lambda j: (0, high(j))),
    ]
    return pl.pallas_call(
        kernel,
        out_shape=[jax.ShapeDtypeStruct(u.shape, bf16) for u in (first, second)],
        grid=(sum(steps),),
        in_specs=[resident((tokens, part))] * 2 + [pl.BlockSpec((depth, TILE), lambda j: (0, j))] * 2 + wide,
        out_specs=wide,
        compiler_params=params(),
        cost_estimate=cost(4 * tokens * depth * columns, 4 * depth * columns + 4 * tokens * columns, tokens * columns),
        name="swiglu_back",
    )(*acts, *weights, first, second)


def row_specs(seqs, own_len, wide):
    mine = pl.BlockSpec((None, None, own_len, wide), lambda s, h: (s, h, 0, 0))
    theirs = pl.BlockSpec((None, None, own_len, wide), lambda s, h: (s, 1 - h, 0, 0))
    return mine, theirs


def load_rows(refs):
    return jnp.concatenate([r[...].astype(f32) for r in refs], axis=-1)


def store_rows(refs, rows):
    half = rows.shape[-1] // 2
    refs[0][...] = rows[:, :half].astype(bf16)
    refs[1][...] = rows[:, half:].astype(bf16)


def middle(resid, partial, received, gain, seqs, own_len):
    width = partial.shape[1]
    half = width // 2

    def kernel(res_low, res_high, par, *refs):
        got, gain_ref, hid_low, hid_high, norm_low, norm_high = refs[:seqs], *refs[seqs:]
        rec = got[0][...]
        for s in range(1, seqs):
            rec = jnp.where(pl.program_id(0) == s, got[s][...], rec)
        rows = load_rows([res_low, res_high]) + (par[...].astype(f32) + rec.astype(f32))
        factor = lax.rsqrt(jnp.mean(rows * rows, axis=-1, keepdims=True) + epsilon)
        store_rows([hid_low, hid_high], rows)
        store_rows([norm_low, norm_high], rows * factor * gain_ref[...])

    mine, _ = row_specs(seqs, own_len, half)
    full, _ = row_specs(seqs, own_len, width)
    theirs = pl.BlockSpec((None, own_len, width), lambda s, h: (1 - h, 0, 0))
    tokens = seqs * 2 * own_len
    outs = pl.pallas_call(
        kernel,
        out_shape=[jax.ShapeDtypeStruct((seqs, 2, own_len, half), bf16)] * 4,
        grid=(seqs, 2),
        in_specs=[mine, mine, full] + [theirs] * seqs + [pl.BlockSpec((1, width), lambda s, h: (0, 0))],
        out_specs=[mine] * 4,
        compiler_params=params(2),
        cost_estimate=cost(10 * tokens * width, 10 * tokens * width),
        name="middle",
    )(
        *[r.reshape(seqs, 2, own_len, half) for r in resid],
        partial.reshape(seqs, 2, own_len, width),
        *[r.reshape(2, own_len, width) for r in received],
        gain,
    )
    outs = [o.reshape(tokens, half) for o in outs]
    return outs[:2], outs[2:]


def middle_back(grad, hidden, partial, received, gain, which, seqs):
    length, width = partial.shape
    half, own_len = width // 2, length // 2

    def kernel(gra_low, gra_high, hid_low, hid_high, par, rec, gain_ref, out_low, out_high):
        rows = load_rows([hid_low, hid_high])
        factor = lax.rsqrt(jnp.mean(rows * rows, axis=-1, keepdims=True) + epsilon)
        unit = rows * factor
        scaled = (par[...].astype(f32) + rec[...].astype(f32)) * gain_ref[...]
        spread = jnp.mean(scaled * unit, axis=-1, keepdims=True)
        store_rows([out_low, out_high], load_rows([gra_low, gra_high]) + factor * (scaled - unit * spread))

    whole = pl.BlockSpec((None, None, own_len, half), lambda h: (which, h, 0, 0))
    mine = pl.BlockSpec((None, own_len, width), lambda h: (h, 0, 0))
    theirs = pl.BlockSpec((None, own_len, width), lambda h: (1 - h, 0, 0))
    out = pl.BlockSpec((own_len, half), lambda h: (h, 0))
    return pl.pallas_call(
        kernel,
        out_shape=[jax.ShapeDtypeStruct((length, half), bf16)] * 2,
        grid=(2,),
        in_specs=[whole] * 4 + [mine, theirs, pl.BlockSpec((1, width), lambda h: (0, 0))],
        out_specs=[out, out],
        compiler_params=params(),
        cost_estimate=cost(20 * length * width, 10 * length * width),
        name="middle_back",
    )(
        *[r.reshape(seqs, 2, own_len, half) for r in list(grad) + list(hidden)],
        *[r.reshape(2, own_len, width) for r in (partial, received)],
        gain,
    )


def leave(slots, residual, partial, received, norm):
    seqs, own_len, width = received.shape
    half = width // 2
    blocks = slots.shape[0]
    block = width // blocks
    narrow = block % LANES != 0

    def kernel(slots_ref, *refs):
        out_ref = refs[-1]
        total = refs[2][...].astype(f32) + refs[3][...].astype(f32)
        if norm is not None:
            rows = load_rows(refs[4:6])
            factor = lax.rsqrt(jnp.mean(rows * rows, axis=-1, keepdims=True) + epsilon)
            unit = rows * factor
            scaled = total * refs[6][...]
            spread = jnp.mean(scaled * unit, axis=-1, keepdims=True)
            total = factor * (scaled - unit * spread)
        total = load_rows(refs[:2]) + total
        for b in range(blocks):
            start = b * block if narrow else pl.multiple_of(slots_ref[b] * block, block)
            out_ref[:, pl.ds(start, block)] = total[:, b * block : (b + 1) * block].astype(bf16)

    mine = pl.BlockSpec((None, None, own_len, half), lambda s, t: (s, 0, 0, 0))
    full = pl.BlockSpec((None, None, own_len, width), lambda s, t: (s, 0, 0, 0))
    whole = pl.BlockSpec((None, own_len, width), lambda s, t: (s, 0, 0))
    arrays = [r.reshape(seqs, 2, own_len, half) for r in residual]
    arrays += [partial.reshape(seqs, 2, own_len, width), received]
    specs = [mine, mine, full, whole]
    if norm is not None:
        arrays += [r.reshape(seqs, 2, own_len, half) for r in norm[0]] + [norm[1]]
        specs += [mine, mine, pl.BlockSpec((1, width), lambda s, t: (0, 0))]
    out = pl.pallas_call(
        kernel,
        out_shape=jax.ShapeDtypeStruct((seqs, own_len, width), bf16),
        grid_spec=pltpu.PrefetchScalarGridSpec(
            num_scalar_prefetch=1, grid=(seqs,), in_specs=specs, out_specs=whole
        ),
        compiler_params=params(),
        cost_estimate=cost(20 * seqs * own_len * width, 12 * seqs * own_len * width),
        name="leave",
    )(slots, *arrays)
    if narrow:
        out = out.reshape(seqs, own_len, blocks, block)[:, :, jnp.argsort(slots)].reshape(seqs, own_len, width)
    return out


def shards(
    inputs,
    block_ids,
    positions,
    w_query,
    key_weight,
    value_weight,
    w_out,
    w_gate,
    w_up,
    w_down,
    attn_gain,
    mlp_gain,
    out_grad,
):
    seqs, own_len, width = inputs.shape
    length = block_ids.shape[1]
    tokens = seqs * length
    side = lax.axis_index("tensor")
    hd = HEAD_SIZE
    heads = w_query.shape[1] // hd
    kv = key_weight.shape[1] // hd
    ff = w_gate.shape[1]
    ring = Ring(lax.axis_size("dp"))
    rows = width // ring.size
    slots = ring.slots(lax.axis_index("dp"))

    def across(value):
        return lax.ppermute(value, "tensor", [(0, 1), (1, 0)])

    def halves(table):
        table = table.reshape(seqs, 2, own_len)
        return jnp.where(side == 0, table, table[:, ::-1]).reshape(seqs, length)

    segments = halves(block_ids)
    seg_row, seg_col = segments[:, None, :], segments[:, :, None]
    steps_half = jnp.arange(hd // 2, dtype=f32)
    frequency = jnp.exp(steps_half * (-2.0 * math.log(rope_base) / hd))
    angles = halves(positions).reshape(tokens, 1).astype(f32) * frequency
    cos_head, sin_head = jnp.tile(jnp.cos(angles), (1, 2)), jnp.tile(jnp.sin(angles), (1, 2))
    kv_wide = kv * hd
    cosine = jnp.concatenate([jnp.tile(cos_head, (1, TILE // hd + kv)), jnp.ones((tokens, kv_wide), f32)], axis=1)
    sine = jnp.concatenate([jnp.tile(sin_head, (1, TILE // hd + kv)), jnp.zeros((tokens, kv_wide), f32)], axis=1)

    blocks = ff // TILE
    cut = (blocks + 1) // 2
    q_cols = heads * hd
    qkv_cols = q_cols + 2 * kv_wide
    out_cols = w_out.shape[0]

    def interleave(first, last):
        parts = [w[:, j * TILE : (j + 1) * TILE] for j in range(first, last) for w in (w_gate, w_up)]
        return jnp.concatenate(parts, axis=1)

    def other(part):
        return part.reshape(seqs, 2, own_len, width)[:, 1]

    def halves_of(pairs):
        return joined(*[
            pairs[(2 * l + p) * rows : (2 * l + p + 1) * rows] for p in range(2) for l in range(ring.line)
        ])

    step = -(-blocks // 4)
    bounds = [0, step, cut, cut + step, blocks]
    names = ["g0", "g1", "g2", "g3"]
    gain_block = jnp.pad(jnp.stack([attn_gain, mlp_gain], axis=1), ((0, 0), (0, LANES - 2)))
    qkv_shard = jnp.concatenate([w_query, key_weight, value_weight], axis=1)
    columns_1 = cut * TILE
    v = {}

    v["q"] = jnp.concatenate([qkv_shard, gain_block], axis=1)
    v["o"] = w_out.T
    down = w_down.T
    v["q."] = ring.gather_far(v["q"])
    down_pair = ring.pair(down)
    v["rows"] = inputs.reshape(seqs, own_len, width)
    v["grad"] = out_grad.reshape(seqs, own_len, width)
    got_rows = across(v["rows"])
    for name, first, last in zip(names, bounds[:-1], bounds[1:]):
        v[name] = interleave(first, last)
    v["d0"] = joined(down[:, :columns_1], down_pair[:, :columns_1])
    v["d1"] = joined(down[:, columns_1:], down_pair[:, columns_1:])
    fence(v)

    def far_send(name):
        v[name + "."] = ring.gather_far(v[name])

    def near_send(name, *after):
        v[name] = joined(tie(v[name], *after), v[name + "."])
        v[name + "."] = ring.along(v[name], 1)
        return v[name]

    def pair_send(name, *after):
        v[name] = joined(tie(v[name], *after), v[name + "."])
        v[name + "."] = ring.pair(v[name])
        return v[name]

    def core_send(name, *after):
        v[name] = joined(tie(v[name], *after), v[name + "."])
        v[name + "."] = ring.core(v[name])
        return v[name]

    def core_send_pairs(name, *after):
        v[name] = halves_of(joined(tie(v[name], *after), v[name + "."]))
        v[name + "."] = ring.core(v[name])
        return v[name]

    def whole(name):
        return [v[name], v[name + "."]]

    near_send("q")
    far_send("o")
    v["got_rows"] = got_rows
    fence(v)

    sent = pair_send("q")
    near_send("o", sent)
    far_send("g0")
    far_send("d1")
    v["got_grad"] = across(v["grad"])
    v["rows"] = jnp.stack([v["rows"], v.pop("got_rows")], axis=1).reshape(tokens, width)
    fence(v)

    sent = near_send("g0", pair_send("o"))
    far_send("g1")
    core_send("q", sent)
    both_grad = jnp.stack([v["grad"], v.pop("got_grad")], axis=1).reshape(tokens, width)
    v["grad"] = tuple(enter(both_grad, slots, None))
    fence(v)

    sent = near_send("g1", pair_send("g0"))
    core_send("o", sent)
    far_send("g2")
    v["attn_gain"], v["mlp_gain"] = gain_rows(whole("q"), qkv_cols)
    entered = enter(v.pop("rows"), slots, v["attn_gain"])
    v["resid"], v["normed"] = tuple(entered[:2]), tuple(entered[2:])
    v["qkv"] = project_qkv(v["normed"], whole("q"), cosine, sine, 0, qkv_cols)
    fence(v)

    sent = near_send("g2", pair_send("g1"))
    core_send("g0", sent)
    far_send("g3")
    v["context"], v["lse"] = attention_forward(v["qkv"], seg_row, seg_col, seqs, heads, kv)
    v["op"] = project_back([v["context"]], [whole("o")])
    for w in range(seqs):
        v[f"op{w}"] = v["op"][w * length : (w + 1) * length]
    fence(v)

    sent = near_send("g3", pair_send("g2"))
    core_send("g1", sent)
    far_send("d0")
    v["op0"] = across(v["op0"])
    fence(v)

    sent = near_send("d0", pair_send("g3"))
    core_send("g2", sent)
    for w in range(1, seqs):
        v[f"op{w}"] = across(v[f"op{w}"])
    fence(v)

    acts_of = {"D0": "grad", "D1": "grad", "O": "attn_grad", "Q": "normed"}
    grads_of = {"D0": "active0", "D1": "active1", "O": "context", "Q": "d_qkv"}
    for k in range(4):
        acts_of[f"G{k}"], grads_of[f"G{k}"] = "normed_mlp", f"du{k}"
    R = {name: Reduce(ring, v, name, acts_of[name], grads_of[name]) for name in acts_of}

    def dn_part(which):
        v[f"dn{which}"] = project_back(
            [v[f"du{k}"] for k in range(4)], [whole(n) for n in names], None, (which, seqs)
        )

    def attend_back(which):
        ag = middle_back(
            v["grad"], v["hidden"], v.pop(f"dn{which}"), v.pop(f"dn{which}."), v["mlp_gain"], which, seqs
        )
        v[f"ag{which}"] = tuple(ag)
        d_context = project(ag, whole("o"), out_cols)
        v[f"dq{which}"] = attention_backward(
            v["qkv"], d_context, v["lse"], seg_row, seg_col, cosine[:, :LANES], sine[:, :LANES], which, heads, kv
        )

    near_send("d1")
    sent = core_send("g3")
    core_send_pairs("d0", sent)
    hidden, normed_mlp = middle(
        v["resid"],
        v.pop("op"),
        [v.pop(f"op{w}") for w in range(seqs)],
        v["mlp_gain"],
        seqs,
        own_len,
    )
    v["hidden"], v["normed_mlp"] = tuple(hidden), tuple(normed_mlp)
    v["u0"], v["u1"], v["active0"] = gate_up(v["normed_mlp"], whole("g0"), whole("g1"))
    R["D0"].far()
    fence(v)

    core_send_pairs("d1")
    R["D0"].send_far()
    v["u2"], v["u3"], v["active1"] = gate_up(v["normed_mlp"], whole("g2"), whole("g3"))
    v["du0"], v["du1"] = swiglu_back(v["grad"], whole("d0"), v.pop("u0"), v.pop("u1"))
    R["D1"].far()
    fence(v)

    R["D0"].side()
    R["D1"].send_far()
    v["du2"], v["du3"] = swiglu_back(v["grad"], whole("d1"), v.pop("u2"), v.pop("u3"))
    R["G0"].far()
    R["G1"].far()
    v["mlp_part"] = project_back([v["active0"], v["active1"]], [whole("d0"), whole("d1")])
    v["mlp_other"] = other(v["mlp_part"])
    fence(v)

    R["D1"].side()
    R["D0"].near()
    R["G0"].send_far()
    R["G1"].send_far()
    for which in range(seqs):
        dn_part(which)
    fence(v)

    for which in range(1):
        v[f"dn{which}."] = across(v[f"dn{which}"])
    R["G0"].side()
    R["D1"].near()
    R["D0"].fold()
    R["G2"].far()
    R["G2"].send_far()
    R["G3"].far()
    fence(v)

    for which in range(1, seqs):
        v[f"dn{which}."] = across(v[f"dn{which}"])
    R["G1"].side()
    R["G0"].near()
    R["D1"].fold()
    R["D0"].rows()
    attend_back(0)
    fence(v)

    R["G2"].side()
    R["G1"].near()
    R["G0"].fold()
    R["G3"].send_far()
    R["D1"].rows()
    for which in range(1, seqs):
        attend_back(which)
    v["attn_grad"] = tuple(joined(*[v[f"ag{w}"][h] for w in range(seqs)]) for h in range(2))
    v["d_qkv"] = joined(*[v[f"dq{w}"] for w in range(seqs)])
    R["O"].far()
    R["Q"].far()
    R["O"].send_far()
    fence(v)

    R["G3"].side()
    R["O"].side()
    R["Q"].send_far()
    R["G2"].near()
    R["G1"].fold()
    R["G0"].rows()
    v["in_part"] = project_back([v["d_qkv"]], [whole("q")])
    v["in_other"] = other(v["in_part"])
    fence(v)

    R["Q"].side()
    v["in_got"] = across(v["in_other"])
    R["O"].near()
    R["G3"].near()
    R["G2"].fold()
    R["G1"].rows()
    fence(v)

    R["Q"].near()
    R["O"].fold()
    R["G3"].fold()
    v["mlp_got"] = across(v["mlp_other"])
    R["G2"].rows()
    input_grad = leave(slots, v["attn_grad"], v["in_part"], v["in_got"], (v["resid"], v["attn_gain"]))
    fence(v)

    R["Q"].fold()
    R["O"].rows()
    R["G3"].rows()
    output = leave(slots, v["hidden"], v["mlp_part"], v["mlp_got"], None)
    fence(v)
    R["Q"].rows()

    def pick(which):
        parts = [
            v[f"G{k}"][:, (2 * j + which) * TILE : (2 * j + which + 1) * TILE]
            for k in range(4)
            for j in range(bounds[k + 1] - bounds[k])
        ]
        return jnp.concatenate(parts, axis=1)

    grad_gate, grad_up, grad_qkv = pick(0), pick(1), v["Q"]

    def gain_sum(weights, grads, gain):
        total = sum(jnp.sum(w.astype(f32) * g, axis=1) for w, g in zip(weights, grads))
        return total / gain.astype(f32)

    gain_sums = jnp.stack([
        gain_sum([qkv_shard], [grad_qkv], attn_gain),
        gain_sum([w_gate, w_up], [grad_gate, grad_up], mlp_gain),
    ])
    gain_sums = gain_sums + across(gain_sums)
    return (
        output,
        input_grad,
        grad_qkv[:, :q_cols],
        grad_qkv[:, q_cols : q_cols + kv_wide],
        grad_qkv[:, q_cols + kv_wide :],
        v["O"].T,
        grad_gate,
        grad_up,
        jnp.concatenate([v["D0"], v["D1"]], axis=1).T,
        gain_sums[0],
        gain_sums[1],
    )


def solution(mesh):
    row, col = P("dp", "tensor"), P("tensor", "dp")
    seq = P("dp", "tensor", None)
    return jax.shard_map(
        shards,
        mesh=mesh,
        in_specs=(seq, P("dp", None), P("dp", None), row, row, row, col, row, row, col, P("dp"), P("dp"), seq),
        out_specs=(seq, seq, row, row, row, col, row, row, col, P("dp"), P("dp")),
        check_vma=False,
    )
```

```python
import functools
import math

import jax
import jax.numpy as jnp
from jax import lax
from jax.experimental import pallas as pl
from jax.experimental.pallas import tpu as pltpu
from jax.sharding import PartitionSpec as P

HEAD_SIZE = 64
LANES = 128
TILE = 256
SHRINK = 10**6
epsilon = 1e-05
rope_base = 10000.0
masked_value = -1e30
bf16 = jnp.bfloat16
f32 = jnp.float32
VMEM_LIMIT = 60 * 1024 * 1024


def dot(left, right, left_dim, right_dim):
    return lax.dot_general(
        left, right, (((left_dim,), (right_dim,)), ((), ())), preferred_element_type=f32
    )


def tie(value, *others):
    return lax.optimization_barrier((value,) + others)[0]


def params(steps=1):
    return pltpu.CompilerParams(
        dimension_semantics=("arbitrary",) * steps, vmem_limit_bytes=VMEM_LIMIT
    )


def resident(shape):
    return pl.BlockSpec(
        shape, lambda *_: (0,) * len(shape), pipeline_mode=pl.Buffered(1)
    )


def cost(flops, moved, trans=0):
    return pl.CostEstimate(flops=flops // SHRINK + 1, bytes_accessed=moved // SHRINK + 1, transcendentals=0)


class Ring:
    def __init__(self, size):
        self.size = size
        self.line = size // 4
        self.reaches = [self.line >> k for k in range(1, self.line.bit_length())]

    def swap(self, value, bits):
        return lax.ppermute(value, "dp", [(i, i ^ bits) for i in range(self.size)])

    def core(self, value):
        return self.swap(value, 1)

    def pair(self, value):
        return self.swap(value, 2)

    def along(self, value, reach):
        return self.swap(value, 4 * reach)

    def slots(self, me):
        order = [0]
        for reach in self.reaches:
            order = order + [o ^ reach for o in order]
        return jnp.stack([me ^ (l * 4 + p * 2 + c) for c in range(2) for p in range(2) for l in order])

    def gather_far(self, shard):
        held = shard
        for reach in self.reaches[:-1]:
            held = jnp.concatenate([held, self.along(held, reach)], axis=0)
        return held[shard.shape[0] :] if self.line > 4 else self.along(shard, 2)


class Values:
    def fence(self):
        fields = vars(self)
        names = sorted(fields)
        fields.update(zip(names, lax.optimization_barrier([fields[n] for n in names])))


def joined(*parts):
    return jnp.concatenate(parts, axis=0)


class Reduce:
    def __init__(self, ring, v, name, acts, grads):
        self.ring, self.v, self.name, self.acts, self.grads = ring, v, name, acts, grads

    def part(self, half, which=None, *after):
        act = self.acts()[half]
        if which is not None:
            quarter = act.shape[1] // 2
            act = act[:, which * quarter : (which + 1) * quarter]
        return dot(tie(act, *after) if after else act, self.grads(), 0, 0)

    def far(self, *after):
        self.v.far[self.name] = self.part(1, None, *after).astype(bf16)
        return self.v.far[self.name]

    def send_far(self):
        self.v.far[self.name] = self.ring.core(self.v.far[self.name])

    def side(self, *after):
        far = self.v.far[self.name]
        quarter = far.shape[0] // 2
        out = (self.part(0, 1, *after) + far[quarter:].astype(f32)).astype(bf16)
        self.v.side[self.name] = out
        return out

    def send_side(self):
        self.v.side[self.name] = self.ring.pair(self.v.side[self.name])

    def near(self, *after):
        side = self.v.side[self.name]
        out = self.part(0, 0, *after) + self.v.far[self.name][: side.shape[0]].astype(f32) + side.astype(f32)
        half = out.shape[0] // 2
        send = out[half:].astype(bf16)
        self.v.far[self.name] = out[:half].astype(bf16)
        self.v.side[self.name] = self.ring.along(send, 1)
        return self.v.far[self.name]

    def fold(self, *after):
        terms, reach = [self.v.far[self.name], self.v.side[self.name]], 2
        if after:
            terms[0] = tie(terms[0], *after)
        while True:
            rows = terms[0].shape[0] // 2
            got = self.ring.along(sum(t[rows:].astype(f32) for t in terms).astype(bf16), reach)
            terms, reach = [t[:rows] for t in terms] + [got], reach * 2
            if reach == self.ring.line:
                break
        self.v.far[self.name] = sum(t.astype(f32) for t in terms[:-1])
        self.v.side[self.name] = terms[-1]
        return self.v.far[self.name]

    def rows(self):
        self.v.sums[self.name] = self.v.far.pop(self.name) + self.v.side.pop(self.name).astype(f32)


def turned(block, line):
    return block % line * 2 + block // line


def enter(rows, slots, gain):
    count, width = rows.shape
    blocks = slots.shape[0]
    block = width // blocks
    per = blocks // 2
    half = width // 2
    step = count // 4
    norm = gain is not None
    narrow = block % LANES != 0
    if narrow:
        rows = rows.reshape(count, blocks, block)[:, slots].reshape(count, width)

    def kernel(slots_ref, x_ref, gain_ref, *outs):
        if norm:
            x = x_ref[...].astype(f32)
            factor = lax.rsqrt(jnp.mean(x * x, axis=-1, keepdims=True) + epsilon)
        for b in range(blocks):
            start = b * block if narrow else pl.multiple_of(slots_ref[b] * block, block)
            piece = x_ref[:, pl.ds(start, block)]
            at = slice((b % per) * block, (b % per + 1) * block)
            outs[b // per][:, at] = piece
            if not norm:
                there = turned(b % per, per // 2)
                outs[2 + b // per][:, there * block : (there + 1) * block] = piece
            if norm:
                g = gain_ref[:, b * block : (b + 1) * block]
                outs[2 + b // per][:, at] = (piece.astype(f32) * factor * g).astype(bf16)

    n_out = 4
    if gain is None:
        gain = jnp.ones((1, width), f32)
    return pl.pallas_call(
        kernel,
        out_shape=[jax.ShapeDtypeStruct((count, half), bf16)] * n_out,
        grid_spec=pltpu.PrefetchScalarGridSpec(
            num_scalar_prefetch=1,
            grid=(4,),
            in_specs=[
                pl.BlockSpec((step, width), lambda i, s: (i, 0)),
                pl.BlockSpec((1, width), lambda i, s: (0, 0)),
            ],
            out_specs=[pl.BlockSpec((step, half), lambda i, s: (i, 0))] * n_out,
        ),
        compiler_params=params(),
        cost_estimate=cost(10 * count * width, 2 * count * width * (1 + n_out // 2)),
        name="enter",
    )(slots, rows, gain)


def qkv_kernel(*refs):
    cos_ref, sin_ref, out_ref = refs[4:]
    raw = times_pieces(refs[:2], refs[2:4])
    lane = lax.broadcasted_iota(jnp.int32, raw.shape, 1) % HEAD_SIZE
    half = HEAD_SIZE // 2
    ahead = pltpu.roll(raw, raw.shape[1] - half, 1)
    behind = pltpu.roll(raw, half, 1)
    turned = jnp.where(lane < half, -ahead, behind)
    out_ref[...] = (raw * cos_ref[...] + turned * sin_ref[...]).astype(bf16)


def project_qkv(acts, weights, cosine, sine, first, columns):
    tokens, part = acts[0].shape
    steps = columns // TILE
    table = pl.BlockSpec((tokens, TILE), lambda j: (0, j // (steps - 1)))
    depth = weights[0].shape[0]
    return pl.pallas_call(
        qkv_kernel,
        out_shape=jax.ShapeDtypeStruct((tokens, columns), bf16),
        grid=(steps,),
        in_specs=[resident((tokens, part))] * 2
        + [pl.BlockSpec((depth, TILE), lambda j: (0, first + j))] * 2
        + [table, table],
        out_specs=pl.BlockSpec((tokens, TILE), lambda j: (0, j)),
        compiler_params=params(),
        cost_estimate=cost(8 * tokens * depth * columns, 8 * depth * columns + 4 * tokens * part),
        name="project_qkv",
    )(*acts, *weights, cosine, sine)


def times_pieces(acts, weights):
    return sum(dot(a[...], w[...], 1, 0) for a, w in zip(acts, weights))


def project_kernel(*refs):
    refs[4][...] = times_pieces(refs[:2], refs[2:4]).astype(bf16)


def project(acts, weights, columns):
    tokens, part = acts[0].shape
    depth = weights[0].shape[0]
    return pl.pallas_call(
        project_kernel,
        out_shape=jax.ShapeDtypeStruct((tokens, columns), bf16),
        grid=(columns // TILE,),
        in_specs=[resident((tokens, part))] * 2 + [pl.BlockSpec((depth, TILE), lambda j: (0, j))] * 2,
        out_specs=pl.BlockSpec((tokens, TILE), lambda j: (0, j)),
        compiler_params=params(),
        cost_estimate=cost(8 * tokens * depth * columns, 8 * depth * columns + 4 * tokens * part),
        name="project",
    )(*acts, *weights)


def project_back(acts, weights, firsts=None, halves=(0, 1)):
    tokens = acts[0].shape[0]
    depth = weights[0][0].shape[0]
    steps = depth // TILE
    count = len(acts)
    firsts = firsts or [0] * count
    wides = [a.shape[1] if not f else math.gcd(a.shape[1], f) for a, f in zip(acts, firsts)]
    parts = [(n, f // w + j, w, j) for n, (a, f, w) in enumerate(zip(acts, firsts, wides)) for j in range(a.shape[1] // w)]
    total = len(parts)

    def kernel(*refs):
        acts_in, out_ref = refs[:count], refs[-1]
        for p in range(len(halves)):
            pieces = refs[count + p * total : count + (p + 1) * total]

            @pl.when(pl.program_id(0) // steps == p)
            def _():
                out_ref[...] = sum(
                    dot(acts_in[n][:, j * w : (j + 1) * w], piece[...], 1, 1)
                    for (n, _, w, j), piece in zip(parts, pieces)
                ).astype(bf16)

    def spec(p, block, wide):
        return pl.BlockSpec((TILE, wide), lambda i: (jnp.clip(i - p * steps, 0, steps - 1), block))

    columns = sum(a.shape[1] for a in acts)
    return pl.pallas_call(
        kernel,
        out_shape=jax.ShapeDtypeStruct((tokens, len(halves) * depth), bf16),
        grid=(len(halves) * steps,),
        in_specs=[
            resident(a.shape) for a in acts
        ]
        + [spec(p, block, w) for p in range(len(halves)) for _, block, w, _ in parts],
        out_specs=pl.BlockSpec((tokens, TILE), lambda i: (0, i)),
        compiler_params=params(),
        cost_estimate=cost(8 * tokens * depth * columns, (8 * depth + 2 * tokens) * columns),
        name="project_back",
    )(*acts, *[weights[n][p] for p in halves for n, _, _, _ in parts])


def gain_rows(pieces, first):
    depth = pieces[0].shape[0]

    def kernel(*refs):
        for p in range(2):
            refs[2][:, p * depth : (p + 1) * depth] = refs[p][...].astype(f32).T[:8]

    out = pl.pallas_call(
        kernel,
        out_shape=jax.ShapeDtypeStruct((8, 2 * depth), f32),
        grid=(1,),
        in_specs=[pl.BlockSpec((depth, LANES), lambda i: (0, first // LANES))] * 2,
        out_specs=pl.BlockSpec((8, 2 * depth), lambda i: (0, 0)),
        compiler_params=params(),
        name="gain_rows",
    )(*pieces)
    return out[:1], out[1:2]


def forward_kernel(q_ref, kv_ref, seg_row, seg_col, ctx_ref, lse_ref):
    kv_heads = kv_ref.shape[1] // (2 * HEAD_SIZE)
    group = pl.program_id(1)
    keys = kv_ref[:, : kv_heads * HEAD_SIZE].astype(f32)
    values = kv_ref[:, kv_heads * HEAD_SIZE :].astype(f32)
    lane = lax.broadcasted_iota(jnp.int32, keys.shape, 1)
    low = lane < HEAD_SIZE
    here = low == (group == 0)
    both_keys = jnp.where(here, keys, pltpu.roll(keys, HEAD_SIZE, 1)).astype(bf16)
    both_values = jnp.where(here, values, pltpu.roll(values, HEAD_SIZE, 1)).astype(bf16)
    none = jnp.zeros_like(both_values)
    value_low = jnp.where(low, both_values, none)
    value_high = jnp.where(low, none, both_values)
    allowed = seg_row[...] <= seg_col[...]
    pairs = q_ref.shape[1] // (2 * HEAD_SIZE)
    for pair in range(pairs):
        cut = slice(pair * LANES, (pair + 1) * LANES)
        q = q_ref[:, cut] * bf16(HEAD_SIZE ** (-0.5))
        total = None
        for side, values_here in ((0, value_low), (1, value_high)):
            mine = jnp.where(low, q, none) if side == 0 else jnp.where(low, none, q)
            scores = jnp.where(allowed, dot(mine, both_keys, 1, 1), masked_value)
            top = jnp.max(scores, axis=-1, keepdims=True)
            weights = jnp.exp(scores - top)
            mass = jnp.sum(weights, axis=-1, keepdims=True)
            probs = (weights * (1.0 / mass)).astype(bf16)
            part = dot(probs, values_here, 1, 0)
            total = part if total is None else total + part
            lse_ref[:, 2 * pair + side : 2 * pair + side + 1] = top + jnp.log(mass)
        ctx_ref[:, cut] = total.astype(bf16)


def attention_forward(qkv, seg_row, seg_col, seqs, heads, kv):
    tokens = qkv.shape[0]
    length = tokens // seqs
    wide = heads // kv * HEAD_SIZE
    last = heads * HEAD_SIZE // (2 * kv * HEAD_SIZE)
    return pl.pallas_call(
        forward_kernel,
        out_shape=[
            jax.ShapeDtypeStruct((tokens, heads * HEAD_SIZE), bf16),
            jax.ShapeDtypeStruct((kv, tokens, heads // kv), f32),
        ],
        grid=(seqs, kv),
        in_specs=[
            pl.BlockSpec((length, wide), lambda s, g: (s, g)),
            pl.BlockSpec((length, 2 * kv * HEAD_SIZE), lambda s, g: (s, last)),
            pl.BlockSpec((None, 1, length), lambda s, g: (s, 0, 0)),
            pl.BlockSpec((None, length, 1), lambda s, g: (s, 0, 0)),
        ],
        out_specs=[
            pl.BlockSpec((length, wide), lambda s, g: (s, g)),
            pl.BlockSpec((None, length, heads // kv), lambda s, g: (g, s, 0)),
        ],
        compiler_params=params(2),
        cost_estimate=cost(16 * tokens * length * heads * HEAD_SIZE, 6 * tokens * heads * HEAD_SIZE),
        name="attention_forward",
    )(qkv, qkv, seg_row, seg_col)


def backward_kernel(q_ref, kv_ref, dctx_ref, lse_ref, seg_row, seg_col, cos_ref, sin_ref, out_ref):
    kv_heads = kv_ref.shape[1] // (2 * HEAD_SIZE)
    group = pl.program_id(1)
    wide = q_ref.shape[1]
    q_cols = kv_heads * wide
    scale = HEAD_SIZE ** (-0.5)
    half = HEAD_SIZE // 2
    keys = kv_ref[:, : kv_heads * HEAD_SIZE].astype(f32)
    values = kv_ref[:, kv_heads * HEAD_SIZE :].astype(f32)
    lane = lax.broadcasted_iota(jnp.int32, keys.shape, 1)
    low = lane < HEAD_SIZE
    here = low == (group == 0)
    both_keys = jnp.where(here, keys, pltpu.roll(keys, HEAD_SIZE, 1)).astype(bf16)
    both_values = jnp.where(here, values, pltpu.roll(values, HEAD_SIZE, 1)).astype(bf16)
    none = jnp.zeros_like(both_keys)
    key_low = jnp.where(low, both_keys, none)
    key_high = jnp.where(low, none, both_keys)
    allowed = seg_row[...] <= seg_col[...]
    cosine, sine = cos_ref[...], sin_ref[...]

    def unrotate(rows):
        turned = rows * sine
        ahead = pltpu.roll(turned, LANES - half, 1)
        behind = pltpu.roll(turned, half, 1)
        return rows * cosine + jnp.where(lane % HEAD_SIZE < half, ahead, -behind)

    dkey = jnp.zeros(keys.shape, f32)
    dvalue = jnp.zeros(keys.shape, f32)
    pairs = q_ref.shape[1] // LANES
    for pair in range(pairs):
        cut = slice(pair * LANES, (pair + 1) * LANES)
        q = q_ref[:, cut] * bf16(scale)
        dctx = dctx_ref[:, cut]
        dquery = None
        for side, keys_here in ((0, key_low), (1, key_high)):
            mine = jnp.where(low, q, none) if side == 0 else jnp.where(low, none, q)
            dmine = jnp.where(low, dctx, none) if side == 0 else jnp.where(low, none, dctx)
            scores = jnp.where(allowed, dot(mine, both_keys, 1, 1), masked_value)
            probs = jnp.exp(scores - lse_ref[:, 2 * pair + side : 2 * pair + side + 1])
            dprobs = dot(dmine, both_values, 1, 1)
            delta = jnp.sum(probs * dprobs, axis=-1, keepdims=True)
            dscores = (probs * (dprobs - delta)).astype(bf16)
            part = dot(dscores, keys_here, 1, 0)
            dquery = part if dquery is None else dquery + part
            dkey = dkey + dot(dscores, mine, 0, 0)
            dvalue = dvalue + dot(probs.astype(bf16), dmine, 0, 0)
        start = pl.multiple_of(group * wide + pair * LANES, LANES)
        out_ref[:, pl.ds(start, LANES)] = unrotate(dquery * scale).astype(bf16)
    dkey = unrotate(dkey + pltpu.roll(dkey, HEAD_SIZE, 1)).astype(bf16)
    dvalue = (dvalue + pltpu.roll(dvalue, HEAD_SIZE, 1)).astype(bf16)

    key_cut, value_cut = slice(q_cols, q_cols + LANES), slice(q_cols + LANES, q_cols + 2 * LANES)

    @pl.when(group == 0)
    def _():
        out_ref[:, key_cut] = dkey
        out_ref[:, value_cut] = dvalue

    @pl.when(group == 1)
    def _():
        out_ref[:, key_cut] = jnp.where(low, out_ref[:, key_cut], dkey)
        out_ref[:, value_cut] = jnp.where(low, out_ref[:, value_cut], dvalue)


def attention_backward(qkv, dctx, lse, seg_row, seg_col, cosine, sine, seqs, heads, kv):
    tokens, columns = qkv.shape
    length = tokens // seqs
    wide = heads // kv * HEAD_SIZE
    last = heads * HEAD_SIZE // (2 * kv * HEAD_SIZE)
    table = pl.BlockSpec((length, LANES), lambda s, g: (s, 0))
    return pl.pallas_call(
        backward_kernel,
        out_shape=jax.ShapeDtypeStruct((tokens, columns), bf16),
        grid=(seqs, kv),
        in_specs=[
            pl.BlockSpec((length, wide), lambda s, g: (s, g)),
            pl.BlockSpec((length, 2 * kv * HEAD_SIZE), lambda s, g: (s, last)),
            pl.BlockSpec((length, wide), lambda s, g: (s, g)),
            pl.BlockSpec((None, length, heads // kv), lambda s, g: (g, s, 0)),
            pl.BlockSpec((None, 1, length), lambda s, g: (s, 0, 0)),
            pl.BlockSpec((None, length, 1), lambda s, g: (s, 0, 0)),
            table,
            table,
        ],
        out_specs=pl.BlockSpec((length, columns), lambda s, g: (s, 0)),
        compiler_params=params(2),
        cost_estimate=cost(40 * tokens * length * heads * HEAD_SIZE, 10 * tokens * heads * HEAD_SIZE),
        name="attention_backward",
    )(qkv, qkv, dctx, lse, seg_row, seg_col, cosine, sine)


def gate_up(acts, first, second):
    tokens, part = acts[0].shape
    depth = first[0].shape[0]
    steps = [w[0].shape[1] // (2 * TILE) for w in (first, second)]

    def kernel(*refs):
        outs, active_ref = refs[6:8], refs[8]

        def fill(weights, gu_ref):
            both = times_pieces(refs[:2], weights)
            gate, up = both[:, :TILE], both[:, TILE:]
            gu_ref[...] = both.astype(bf16)
            active_ref[...] = (gate * (1.0 / (1.0 + jnp.exp(-gate))) * up).astype(bf16)

        pl.when(pl.program_id(0) < steps[0])(lambda: fill(refs[2:4], outs[0]))
        pl.when(pl.program_id(0) >= steps[0])(lambda: fill(refs[4:6], outs[1]))

    def low(j):
        return jnp.minimum(j, steps[0] - 1)

    def high(j):
        return jnp.maximum(j - steps[0], 0)

    columns = 2 * TILE * sum(steps)
    return pl.pallas_call(
        kernel,
        out_shape=[jax.ShapeDtypeStruct((tokens, 2 * TILE * n), bf16) for n in steps]
        + [jax.ShapeDtypeStruct((tokens, TILE * sum(steps)), bf16)],
        grid=(sum(steps),),
        in_specs=[resident((tokens, part))] * 2
        + [pl.BlockSpec((depth, 2 * TILE), lambda j: (0, low(j)))] * 2
        + [pl.BlockSpec((depth, 2 * TILE), lambda j: (0, high(j)))] * 2,
        out_specs=[
            pl.BlockSpec((tokens, 2 * TILE), lambda j: (0, low(j))),
            pl.BlockSpec((tokens, 2 * TILE), lambda j: (0, high(j))),
            pl.BlockSpec((tokens, TILE), lambda j: (0, j)),
        ],
        compiler_params=params(),
        cost_estimate=cost(4 * tokens * depth * columns, 4 * depth * columns + 4 * tokens * columns, tokens * columns),
        name="gate_up",
    )(*acts, *first, *second)


def swiglu_back(acts, weights, first, second):
    tokens, part = acts[0].shape
    depth = weights[0].shape[0]
    steps = [u.shape[1] // (2 * TILE) for u in (first, second)]

    def kernel(*refs):
        d_active = times_pieces(refs[:2], refs[2:4])

        def fill(gu_ref, out_ref):
            gate, up = gu_ref[:, :TILE].astype(f32), gu_ref[:, TILE:].astype(f32)
            sig = 1.0 / (1.0 + jnp.exp(-gate))
            out_ref[:, :TILE] = (d_active * up * sig * (1.0 + gate * (1.0 - sig))).astype(bf16)
            out_ref[:, TILE:] = (d_active * (gate * sig)).astype(bf16)

        pl.when(pl.program_id(0) < steps[0])(lambda: fill(refs[4], refs[6]))
        pl.when(pl.program_id(0) >= steps[0])(lambda: fill(refs[5], refs[7]))

    def low(j):
        return jnp.minimum(j, steps[0] - 1)

    def high(j):
        return jnp.maximum(j - steps[0], 0)

    columns = 2 * TILE * sum(steps)
    wide = [
        pl.BlockSpec((tokens, 2 * TILE), lambda j: (0, low(j))),
        pl.BlockSpec((tokens, 2 * TILE), lambda j: (0, high(j))),
    ]
    return pl.pallas_call(
        kernel,
        out_shape=[jax.ShapeDtypeStruct(u.shape, bf16) for u in (first, second)],
        grid=(sum(steps),),
        in_specs=[resident((tokens, part))] * 2 + [pl.BlockSpec((depth, TILE), lambda j: (0, j))] * 2 + wide,
        out_specs=wide,
        compiler_params=params(),
        cost_estimate=cost(4 * tokens * depth * columns, 4 * depth * columns + 4 * tokens * columns, tokens * columns),
        name="swiglu_back",
    )(*acts, *weights, first, second)


def row_specs(seqs, own_len, wide):
    mine = pl.BlockSpec((None, None, own_len, wide), lambda s, h: (s, h, 0, 0))
    theirs = pl.BlockSpec((None, None, own_len, wide), lambda s, h: (s, 1 - h, 0, 0))
    return mine, theirs


def load_rows(refs):
    return jnp.concatenate([r[...].astype(f32) for r in refs], axis=-1)


def store_rows(refs, rows):
    half = rows.shape[-1] // 2
    refs[0][...] = rows[:, :half].astype(bf16)
    refs[1][...] = rows[:, half:].astype(bf16)


def middle(resid, partial, received, gain, seqs, own_len):
    width = partial.shape[1]
    half = width // 2

    def kernel(res_low, res_high, par, *refs):
        got, gain_ref, hid_low, hid_high, norm_low, norm_high = refs[:seqs], *refs[seqs:]
        rec = got[0][...]
        for s in range(1, seqs):
            rec = jnp.where(pl.program_id(0) == s, got[s][...], rec)
        rows = load_rows([res_low, res_high]) + (par[...].astype(f32) + rec.astype(f32))
        factor = lax.rsqrt(jnp.mean(rows * rows, axis=-1, keepdims=True) + epsilon)
        store_rows([hid_low, hid_high], rows)
        store_rows([norm_low, norm_high], rows * factor * gain_ref[...])

    mine, _ = row_specs(seqs, own_len, half)
    full, _ = row_specs(seqs, own_len, width)
    theirs = pl.BlockSpec((None, own_len, width), lambda s, h: (1 - h, 0, 0))
    tokens = seqs * 2 * own_len
    outs = pl.pallas_call(
        kernel,
        out_shape=[jax.ShapeDtypeStruct((seqs, 2, own_len, half), bf16)] * 4,
        grid=(seqs, 2),
        in_specs=[mine, mine, full] + [theirs] * seqs + [pl.BlockSpec((1, width), lambda s, h: (0, 0))],
        out_specs=[mine] * 4,
        compiler_params=params(2),
        cost_estimate=cost(10 * tokens * width, 10 * tokens * width),
        name="middle",
    )(
        *[r.reshape(seqs, 2, own_len, half) for r in resid],
        partial.reshape(seqs, 2, own_len, width),
        *[r.reshape(2, own_len, width) for r in received],
        gain,
    )
    outs = [o.reshape(tokens, half) for o in outs]
    return outs[:2], outs[2:]


def middle_back(grad, hidden, partial, received, gain, seqs, own_len):
    tokens, half = grad[0].shape
    width = 2 * half

    def kernel(*refs):
        rows = load_rows(refs[2:4])
        factor = lax.rsqrt(jnp.mean(rows * rows, axis=-1, keepdims=True) + epsilon)
        unit = rows * factor
        scaled = (load_rows(refs[4:6]) + load_rows(refs[6:8])) * refs[8][...]
        spread = jnp.mean(scaled * unit, axis=-1, keepdims=True)
        store_rows(refs[9:11], load_rows(refs[:2]) + factor * (scaled - unit * spread))

    mine, theirs = row_specs(seqs, own_len, half)
    shape = (seqs, 2, own_len, half)
    outs = pl.pallas_call(
        kernel,
        out_shape=[jax.ShapeDtypeStruct(shape, bf16)] * 2,
        grid=(seqs, 2),
        in_specs=[mine] * 6 + [theirs] * 2 + [pl.BlockSpec((1, width), lambda s, h: (0, 0))],
        out_specs=[mine] * 2,
        compiler_params=params(2),
        cost_estimate=cost(20 * tokens * width, 10 * tokens * width),
        name="middle_back",
    )(*[r.reshape(shape) for r in (*grad, *hidden, *partial, *received)], gain)
    return tuple(o.reshape(tokens, half) for o in outs)


def leave(slots, residual, partial, received, norm, in_turns=False):
    seqs, own_len, width = received.shape
    half = width // 2
    blocks = slots.shape[0]
    block = width // blocks
    narrow = block % LANES != 0

    def kernel(slots_ref, *refs):
        out_ref = refs[-1]
        total = refs[2][...].astype(f32) + refs[3][...].astype(f32)
        if norm is not None:
            rows = load_rows(refs[4:6])
            factor = lax.rsqrt(jnp.mean(rows * rows, axis=-1, keepdims=True) + epsilon)
            unit = rows * factor
            scaled = total * refs[6][...]
            spread = jnp.mean(scaled * unit, axis=-1, keepdims=True)
            total = factor * (scaled - unit * spread)
        residual_rows = load_rows(refs[:2])
        per = blocks // 2
        for b in range(blocks):
            start = b * block if narrow else pl.multiple_of(slots_ref[b] * block, block)
            at = b // per * per + turned(b % per, per // 2) if in_turns else b
            out = residual_rows[:, b * block : (b + 1) * block] + total[:, at * block : (at + 1) * block]
            out_ref[:, pl.ds(start, block)] = out.astype(bf16)

    mine = pl.BlockSpec((None, None, own_len, half), lambda s, t: (s, 0, 0, 0))
    full = pl.BlockSpec((None, None, own_len, width), lambda s, t: (s, 0, 0, 0))
    whole = pl.BlockSpec((None, own_len, width), lambda s, t: (s, 0, 0))
    arrays = [r.reshape(seqs, 2, own_len, half) for r in residual]
    arrays += [partial.reshape(seqs, 2, own_len, width), received]
    specs = [mine, mine, full, whole]
    if norm is not None:
        arrays += [r.reshape(seqs, 2, own_len, half) for r in norm[0]] + [norm[1]]
        specs += [mine, mine, pl.BlockSpec((1, width), lambda s, t: (0, 0))]
    out = pl.pallas_call(
        kernel,
        out_shape=jax.ShapeDtypeStruct((seqs, own_len, width), bf16),
        grid_spec=pltpu.PrefetchScalarGridSpec(
            num_scalar_prefetch=1, grid=(seqs,), in_specs=specs, out_specs=whole
        ),
        compiler_params=params(),
        cost_estimate=cost(20 * seqs * own_len * width, 12 * seqs * own_len * width),
        name="leave",
    )(slots, *arrays)
    if narrow:
        out = out.reshape(seqs, own_len, blocks, block)[:, :, jnp.argsort(slots)].reshape(seqs, own_len, width)
    return out


def shards(
    inputs,
    block_ids,
    positions,
    w_query,
    key_weight,
    value_weight,
    w_out,
    w_gate,
    w_up,
    w_down,
    attn_gain,
    mlp_gain,
    out_grad,
):
    seqs, own_len, width = inputs.shape
    length = block_ids.shape[1]
    tokens = seqs * length
    side = lax.axis_index("tensor")
    hd = HEAD_SIZE
    heads = w_query.shape[1] // hd
    kv = key_weight.shape[1] // hd
    ff = w_gate.shape[1]
    ring = Ring(lax.axis_size("dp"))
    rows = width // ring.size
    slots = ring.slots(lax.axis_index("dp"))

    def across(value):
        return lax.ppermute(value, "tensor", [(0, 1), (1, 0)])

    def halves(table):
        table = table.reshape(seqs, 2, own_len)
        return jnp.where(side == 0, table, table[:, ::-1]).reshape(seqs, length)

    kv_wide = kv * hd
    blocks = ff // TILE
    cut = (blocks + 1) // 2
    q_cols = heads * hd
    qkv_cols = q_cols + 2 * kv_wide
    out_cols = w_out.shape[0]

    def interleave(pair, first, last):
        parts = [w[:, j * TILE : (j + 1) * TILE] for j in range(first, last) for w in pair]
        return jnp.concatenate(parts, axis=1)

    def other(part):
        return part.reshape(seqs, 2, own_len, width)[:, 1]

    step = -(-blocks // 4)
    bounds = [0, step, cut, cut + step, blocks]
    Q, O, G0, G1, G2, G3, D0, D1 = range(8)
    gates = [G0, G1, G2, G3]
    gain_block = jnp.pad(jnp.stack([attn_gain, mlp_gain], axis=1), ((0, 0), (0, LANES - 2)))
    qkv_shard = jnp.concatenate([w_query, key_weight, value_weight], axis=1)
    columns_1 = cut * TILE
    v = Values()
    v.held, v.got = {}, {}

    def far_send(name):
        v.got[name] = ring.gather_far(v.held[name])

    def grow(name, send, after):
        v.held[name] = joined(tie(v.held[name], *after) if after else v.held[name], v.got[name])
        v.got[name] = send(v.held[name])
        return v.held[name]

    def near_send(name, *after):
        return grow(name, lambda value: ring.along(value, 1), after)

    def pair_send(name, *after):
        return grow(name, ring.pair, after)

    def core_send(name, *after):
        return grow(name, ring.core, after)

    def core_join(name):
        v.held[name] = joined(v.held[name], v.got[name])
        v.got[name] = v.held[name][:LANES]

    def core_send_joined(name):
        v.got[name] = ring.core(v.held[name])

    def whole(name):
        return [v.held[name], v.got[name]]

    v.held[Q] = jnp.concatenate([qkv_shard, gain_block], axis=1)
    v.held[O] = w_out.T
    down = w_down.T
    far_send(Q)
    down_pair = ring.pair(down)
    v.rows = inputs.reshape(seqs, own_len, width)
    v.grad = out_grad.reshape(seqs, own_len, width)
    got_rows = across(v.rows)
    v.down, v.down_pair = down, down_pair
    v.held[G0] = interleave((w_gate, w_up), 0, step)
    v.fence()

    near_send(Q)
    far_send(O)
    segments = halves(tie(block_ids, v.held[Q]))
    seg_row, seg_col = segments[:, None, :], segments[:, :, None]
    steps_half = jnp.arange(hd // 2, dtype=f32)
    frequency = jnp.exp(steps_half * (-2.0 * math.log(rope_base) / hd))
    angles = halves(tie(positions, v.held[Q])).reshape(tokens, 1).astype(f32) * frequency
    cos_head, sin_head = jnp.tile(jnp.cos(angles), (1, 2)), jnp.tile(jnp.sin(angles), (1, 2))
    cosine = jnp.concatenate([jnp.tile(cos_head, (1, TILE // hd + kv)), jnp.ones((tokens, kv_wide), f32)], axis=1)
    sine = jnp.concatenate([jnp.tile(sin_head, (1, TILE // hd + kv)), jnp.zeros((tokens, kv_wide), f32)], axis=1)

    v.tables = [cosine, sine, seg_row, seg_col]
    gate_up_shards = (tie(w_gate, v.held[Q]), tie(w_up, v.held[Q]))
    for name, first, last in zip(gates[1:], bounds[1:-1], bounds[2:]):
        v.held[name] = interleave(gate_up_shards, first, last)
    v.held[D0] = joined(v.down[:, :columns_1], v.down_pair[:, :columns_1])
    v.held[D1] = joined(v.down[:, columns_1:], v.down_pair[:, columns_1:])
    del v.down, v.down_pair
    v.got_rows = got_rows
    v.fence()

    sent = pair_send(Q)
    near_send(O, sent)
    far_send(G0)
    v.got_grad = across(v.grad)
    v.rows = jnp.stack([v.rows, v.got_rows], axis=1).reshape(tokens, width)
    del v.got_rows
    v.fence()

    sent = near_send(G0, pair_send(O))
    far_send(G1)
    v.far_pair = [ring.gather_far(v.held[D1][:rows])]
    core_send(Q, sent)
    both_grad = jnp.stack([v.grad, v.got_grad], axis=1).reshape(tokens, width)
    del v.got_grad
    entered = enter(both_grad, slots, None)
    v.grad, v.grad_turned = tuple(entered[:2]), tuple(entered[2:])
    v.fence()

    near_send(G1, pair_send(G0))
    core_o = [ring.core(v.held[O]), ring.core(v.got[O])]
    v.held[O], v.got[O] = joined(v.held[O], v.got[O]), core_o
    far_send(G2)
    v.attn_gain, v.mlp_gain = gain_rows(whole(Q), qkv_cols)
    entered = enter(v.rows, slots, v.attn_gain)
    del v.rows
    v.resid, v.normed = tuple(entered[:2]), tuple(entered[2:])
    v.qkv = project_qkv(v.normed, whole(Q), v.tables[0], v.tables[1], 0, qkv_cols)
    v.fence()

    near_send(G2, pair_send(G1))
    core_join(G0)
    far_send(G3)
    v.far_pair.append(ring.gather_far(v.held[D1][rows:]))
    v.got[O] = joined(*v.got[O])
    v.context, v.lse = attention_forward(v.qkv, v.tables[2], v.tables[3], seqs, heads, kv)
    v.out_part = project_back([v.context], [whole(O)])
    v.out_got = [v.out_part[w * length : (w + 1) * length] for w in range(seqs)]
    v.fence()

    near_send(G3, pair_send(G2))
    core_send_joined(G0)
    core_join(G1)
    far_send(D0)
    lines = [p.reshape(-1, rows, p.shape[1]) for p in v.far_pair]
    v.got[D1] = jnp.stack(lines, axis=1).reshape(-1, lines[0].shape[2])
    del v.far_pair
    v.out_got[0] = across(v.out_got[0])
    v.fence()

    near_send(D0, pair_send(G3))
    core_send_joined(G1)
    core_join(G2)
    for w in range(1, seqs):
        v.out_got[w] = across(v.out_got[w])
    v.fence()

    v.far, v.side, v.sums = {}, {}, {}
    v.gu, v.active, v.du = {}, {}, {}
    v.dn, v.got_dn = [None] * 2, [None] * 2
    R = [
        Reduce(ring, v, Q, lambda: v.normed, lambda: v.d_qkv),
        Reduce(ring, v, O, lambda: v.attn_grad, lambda: v.context),
    ]
    for k, name in enumerate(gates):
        R.append(Reduce(ring, v, name, lambda: v.normed_mlp, lambda k=k: v.du[k]))
    for k, name in enumerate([D0, D1]):
        R.append(Reduce(ring, v, name, lambda: v.grad, lambda k=k: v.active[k]))

    def dn_half(which, *after):
        acts = [tie(v.du[0], *after) if after else v.du[0]] + [v.du[k] for k in range(1, 4)]
        v.dn[which] = project_back(acts, [whole(n) for n in gates], None, (which,))

    near_send(D1)
    core_send_joined(G2)
    sent = core_send(G3)
    core_send(D0, sent)
    hidden, normed_mlp = middle(v.resid, v.out_part, v.out_got, v.mlp_gain, seqs, own_len)
    del v.out_part, v.out_got
    v.hidden, v.normed_mlp = tuple(hidden), tuple(normed_mlp)
    v.gu[0], v.gu[1], v.active[0] = gate_up(v.normed_mlp, whole(G0), whole(G1))
    R[D0].far()
    v.fence()

    core_send(D1)
    R[D0].send_far()
    v.gu[2], v.gu[3], v.active[1] = gate_up(v.normed_mlp, whole(G2), whole(G3))
    v.du[0], v.du[1] = swiglu_back(v.grad_turned, whole(D0), v.gu.pop(0), v.gu.pop(1))
    R[D1].far()
    v.fence()

    sent = R[D0].side()
    R[D0].send_side()
    R[D1].send_far()
    v.du[2], v.du[3] = swiglu_back(
        [tie(v.grad_turned[0], sent), v.grad_turned[1]], whole(D1), v.gu.pop(2), v.gu.pop(3)
    )
    for name in gates:
        R[name].far()
    v.fence()

    for name in gates[:3]:
        R[name].send_far()
    sent = R[D1].side()
    R[D1].send_side()
    sent = R[D0].near(sent)
    dn_half(0, sent)
    v.fence()

    v.got_dn[0] = across(v.dn[0])
    R[G3].send_far()
    sent = R[G0].side()
    R[G0].send_side()
    sent = R[D1].near(sent)
    sent = R[D0].fold(sent)
    dn_half(1, sent)
    R[G1].side(sent)
    v.fence()

    v.got_dn[1] = across(v.dn[1])
    R[G1].send_side()
    sent = R[G0].near()
    sent = R[D1].fold(sent)
    R[D0].rows()
    R[G2].side(sent)
    R[G3].side(sent)
    v.mlp_part = project_back([tie(v.active[0], sent), v.active[1]], [whole(D0), whole(D1)])
    v.mlp_other = other(v.mlp_part)
    v.fence()

    v.mlp_got = across(v.mlp_other)
    del v.mlp_other
    R[G2].send_side()
    v.attn_grad = middle_back(v.grad, v.hidden, v.dn, v.got_dn, v.mlp_gain, seqs, own_len)
    sent = R[O].far()
    R[O].send_far()
    sent = R[G1].near(sent)
    sent = R[G0].fold(sent)
    R[D1].rows()
    d_context = project([tie(v.attn_grad[0], sent), v.attn_grad[1]], whole(O), out_cols)
    v.d_qkv = attention_backward(
        v.qkv, d_context, v.lse, v.tables[2], v.tables[3], v.tables[0], v.tables[1], seqs, heads, kv
    )
    v.fence()

    R[G3].send_side()
    sent = R[Q].far(R[O].side())
    R[O].send_side()
    R[Q].send_far()
    sent = R[G2].near(sent)
    sent = R[G1].fold(sent)
    R[G0].rows()
    v.in_part = project_back([tie(v.d_qkv, sent)], [whole(Q)])
    v.in_other = other(v.in_part)
    v.output = leave(slots, v.hidden, v.mlp_part, v.mlp_got, None, True)
    v.fence()

    v.in_got = across(v.in_other)
    del v.in_other
    sent = R[Q].side()
    R[Q].send_side()
    sent = R[O].near(sent)
    sent = R[G3].near(sent)
    R[G2].fold(sent)
    R[G1].rows()
    v.fence()

    sent = R[Q].near()
    sent = R[O].fold(sent)
    R[G3].fold(sent)
    R[G2].rows()
    v.input_grad = leave(slots, v.attn_grad, v.in_part, v.in_got, (v.resid, v.attn_gain))
    v.fence()

    R[Q].fold()
    R[O].rows()
    R[G3].rows()
    v.fence()
    R[Q].rows()

    def pick(which):
        parts = [
            v.sums[gates[k]][:, (2 * j + which) * TILE : (2 * j + which + 1) * TILE]
            for k in range(4)
            for j in range(bounds[k + 1] - bounds[k])
        ]
        return jnp.concatenate(parts, axis=1)

    grad_gate, grad_up, grad_qkv = pick(0), pick(1), v.sums[Q]

    def gain_sum(weights, grads, gain):
        total = sum(jnp.sum(w.astype(f32) * g, axis=1) for w, g in zip(weights, grads))
        return total / gain.astype(f32)

    gain_sums = jnp.stack([
        gain_sum([qkv_shard], [grad_qkv], attn_gain),
        gain_sum([w_gate, w_up], [grad_gate, grad_up], mlp_gain),
    ])
    gain_sums = gain_sums + across(gain_sums)
    return (
        v.output,
        v.input_grad,
        grad_qkv[:, :q_cols],
        grad_qkv[:, q_cols : q_cols + kv_wide],
        grad_qkv[:, q_cols + kv_wide :],
        v.sums[O].T,
        grad_gate,
        grad_up,
        jnp.concatenate([v.sums[D0], v.sums[D1]], axis=1).T,
        gain_sums[0],
        gain_sums[1],
    )


def solution(mesh):
    row, col = P("dp", "tensor"), P("tensor", "dp")
    seq = P("dp", "tensor", None)
    return jax.shard_map(
        shards,
        mesh=mesh,
        in_specs=(seq, P("dp", None), P("dp", None), row, row, row, col, row, row, col, P("dp"), P("dp"), seq),
        out_specs=(seq, seq, row, row, row, col, row, row, col, P("dp"), P("dp")),
        check_vma=False,
    )
```

```python
import functools
import math

import jax
import jax.numpy as jnp
from jax import lax
from jax.experimental import pallas as pl
from jax.experimental.pallas import tpu as pltpu
from jax.sharding import PartitionSpec as P

HEAD_SIZE = 64
LANES = 128
TILE = 256
SHRINK = 10**6
epsilon = 1e-05
rope_base = 10000.0
masked_value = -1e30
bf16 = jnp.bfloat16
f32 = jnp.float32
VMEM_LIMIT = 60 * 1024 * 1024


def dot(left, right, left_dim, right_dim):
    return lax.dot_general(
        left, right, (((left_dim,), (right_dim,)), ((), ())), preferred_element_type=f32
    )


def tie(value, *others):
    return lax.optimization_barrier((value,) + others)[0]


def params(steps=1):
    return pltpu.CompilerParams(
        dimension_semantics=("arbitrary",) * steps, vmem_limit_bytes=VMEM_LIMIT
    )


def resident(shape):
    return pl.BlockSpec(
        shape, lambda *_: (0,) * len(shape), pipeline_mode=pl.Buffered(1)
    )


def cost(flops, moved, trans=0):
    return pl.CostEstimate(flops=flops // SHRINK + 1, bytes_accessed=moved // SHRINK + 1, transcendentals=0)


class Ring:
    def __init__(self, size):
        self.size = size
        self.line = size // 4
        self.reaches = [self.line >> k for k in range(1, self.line.bit_length())]

    def swap(self, value, bits):
        return lax.ppermute(value, "dp", [(i, i ^ bits) for i in range(self.size)])

    def core(self, value):
        return self.swap(value, 1)

    def pair(self, value):
        return self.swap(value, 2)

    def along(self, value, reach):
        return self.swap(value, 4 * reach)

    def slots(self, me):
        order = [0]
        for reach in self.reaches:
            order = order + [o ^ reach for o in order]
        return jnp.stack([me ^ (l * 4 + p * 2 + c) for c in range(2) for p in range(2) for l in order])

    def gather_far(self, shard):
        held = shard
        for reach in self.reaches[:-1]:
            held = jnp.concatenate([held, self.along(held, reach)], axis=0)
        return held[shard.shape[0] :] if self.line > 4 else self.along(shard, 2)


class Values:
    def fence(self):
        fields = vars(self)
        names = sorted(fields)
        fields.update(zip(names, lax.optimization_barrier([fields[n] for n in names])))


def joined(*parts):
    return jnp.concatenate(parts, axis=0)


def weight_grad(act, which, grads, adds, outs):
    tokens, width = act.shape
    columns = grads.shape[1]
    rows = width if which is None else width // 2
    tile = 2 * TILE if columns % (2 * TILE) == 0 else TILE
    at = which or 0

    def kernel(*refs):
        act_ref, grads_ref, turned_ref = refs[0], refs[1], refs[-1]

        @pl.when(pl.program_id(0) == 0)
        def _():
            turned_ref[...] = act_ref[...].astype(f32).T.astype(bf16)

        total = dot(turned_ref[...], grads_ref[...], 1, 0)
        for ref in refs[2 : 2 + len(adds)]:
            total = total + ref[...].astype(f32)
        for n, ref in enumerate(refs[2 + len(adds) : -1]):
            ref[...] = total[n * (rows // outs) : (n + 1) * (rows // outs)].astype(bf16)

    def add_spec(block):
        return pl.BlockSpec((rows, tile), lambda j: (block, j))

    return pl.pallas_call(
        kernel,
        out_shape=[jax.ShapeDtypeStruct((rows // outs, columns), bf16)] * outs,
        grid=(columns // tile,),
        in_specs=[
            pl.BlockSpec((tokens, rows), lambda j: (0, at), pipeline_mode=pl.Buffered(1)),
            pl.BlockSpec((tokens, tile), lambda j: (0, j)),
        ]
        + [add_spec(block) for _, block in adds],
        out_specs=[pl.BlockSpec((rows // outs, tile), lambda j: (0, j))] * outs,
        scratch_shapes=[pltpu.VMEM((rows, tokens), bf16)],
        compiler_params=params(),
        cost_estimate=cost(2 * tokens * rows * columns, 2 * tokens * (rows + columns) + 4 * rows * columns),
        name="weight_grad",
    )(act, grads, *[array for array, _ in adds])


class Reduce:
    def __init__(self, ring, v, name, acts, grads):
        self.ring, self.v, self.name, self.acts, self.grads = ring, v, name, acts, grads

    def part(self, half, which=None, *after):
        act = self.acts()[half]
        if which is not None:
            quarter = act.shape[1] // 2
            act = act[:, which * quarter : (which + 1) * quarter]
        return dot(tie(act, *after) if after else act, self.grads(), 0, 0)

    def far(self, *after):
        self.v.far[self.name] = self.part(1, None, *after).astype(bf16)
        return self.v.far[self.name]

    def send_far(self):
        self.v.far[self.name] = self.ring.core(self.v.far[self.name])

    def side(self, *after):
        far = self.v.far[self.name]
        quarter = far.shape[0] // 2
        out = (self.part(0, 1, *after) + far[quarter:].astype(f32)).astype(bf16)
        self.v.side[self.name] = out
        return out

    def side_ahead(self, *after):
        (out,) = weight_grad(tie(self.acts()[0], *after), 1, self.grads(), [(self.v.far[self.name], 1)], 1)
        self.v.side[self.name] = out
        return out

    def send_side(self):
        self.v.side[self.name] = self.ring.pair(self.v.side[self.name])

    def near(self, *after):
        side = self.v.side[self.name]
        out = self.part(0, 0, *after) + self.v.far[self.name][: side.shape[0]].astype(f32) + side.astype(f32)
        half = out.shape[0] // 2
        send = out[half:].astype(bf16)
        self.v.far[self.name] = out[:half].astype(bf16)
        self.v.side[self.name] = self.ring.along(send, 1)
        return self.v.far[self.name]

    def fold(self, *after):
        terms, reach = [self.v.far[self.name], self.v.side[self.name]], 2
        if after:
            terms[0] = tie(terms[0], *after)
        while True:
            rows = terms[0].shape[0] // 2
            got = self.ring.along(sum(t[rows:].astype(f32) for t in terms).astype(bf16), reach)
            terms, reach = [t[:rows] for t in terms] + [got], reach * 2
            if reach == self.ring.line:
                break
        self.v.far[self.name] = sum(t.astype(f32) for t in terms[:-1])
        self.v.side[self.name] = terms[-1]
        return self.v.far[self.name]

    def rows(self):
        self.v.sums[self.name] = self.v.far.pop(self.name) + self.v.side.pop(self.name).astype(f32)


def turned(block, line):
    return block % line * 2 + block // line


def enter(rows, slots, gain):
    count, width = rows.shape
    blocks = slots.shape[0]
    block = width // blocks
    per = blocks // 2
    half = width // 2
    step = count // 4
    norm = gain is not None
    narrow = block % LANES != 0
    if narrow:
        rows = rows.reshape(count, blocks, block)[:, slots].reshape(count, width)

    def kernel(slots_ref, x_ref, gain_ref, *outs):
        if norm:
            x = x_ref[...].astype(f32)
            factor = lax.rsqrt(jnp.mean(x * x, axis=-1, keepdims=True) + epsilon)
        for b in range(blocks):
            start = b * block if narrow else pl.multiple_of(slots_ref[b] * block, block)
            piece = x_ref[:, pl.ds(start, block)]
            at = slice((b % per) * block, (b % per + 1) * block)
            outs[b // per][:, at] = piece
            if not norm:
                there = turned(b % per, per // 2)
                outs[2 + b // per][:, there * block : (there + 1) * block] = piece
            if norm:
                g = gain_ref[:, b * block : (b + 1) * block]
                outs[2 + b // per][:, at] = (piece.astype(f32) * factor * g).astype(bf16)

    n_out = 4
    if gain is None:
        gain = jnp.ones((1, width), f32)
    return pl.pallas_call(
        kernel,
        out_shape=[jax.ShapeDtypeStruct((count, half), bf16)] * n_out,
        grid_spec=pltpu.PrefetchScalarGridSpec(
            num_scalar_prefetch=1,
            grid=(4,),
            in_specs=[
                pl.BlockSpec((step, width), lambda i, s: (i, 0)),
                pl.BlockSpec((1, width), lambda i, s: (0, 0)),
            ],
            out_specs=[pl.BlockSpec((step, half), lambda i, s: (i, 0))] * n_out,
        ),
        compiler_params=params(),
        cost_estimate=cost(10 * count * width, 2 * count * width * (1 + n_out // 2)),
        name="enter",
    )(slots, rows, gain)


def qkv_kernel(*refs):
    cos_ref, sin_ref, out_ref = refs[4:]
    raw = times_pieces(refs[:2], refs[2:4])
    lane = lax.broadcasted_iota(jnp.int32, raw.shape, 1) % HEAD_SIZE
    half = HEAD_SIZE // 2
    ahead = pltpu.roll(raw, raw.shape[1] - half, 1)
    behind = pltpu.roll(raw, half, 1)
    turned = jnp.where(lane < half, -ahead, behind)
    out_ref[...] = (raw * cos_ref[...] + turned * sin_ref[...]).astype(bf16)


def project_qkv(acts, weights, cosine, sine, first, columns):
    tokens, part = acts[0].shape
    steps = columns // TILE
    table = pl.BlockSpec((tokens, TILE), lambda j: (0, j // (steps - 1)))
    depth = weights[0].shape[0]
    return pl.pallas_call(
        qkv_kernel,
        out_shape=jax.ShapeDtypeStruct((tokens, columns), bf16),
        grid=(steps,),
        in_specs=[resident((tokens, part))] * 2
        + [pl.BlockSpec((depth, TILE), lambda j: (0, first + j))] * 2
        + [table, table],
        out_specs=pl.BlockSpec((tokens, TILE), lambda j: (0, j)),
        compiler_params=params(),
        cost_estimate=cost(8 * tokens * depth * columns, 8 * depth * columns + 4 * tokens * part),
        name="project_qkv",
    )(*acts, *weights, cosine, sine)


def times_pieces(acts, weights):
    return sum(dot(a[...], w[...], 1, 0) for a, w in zip(acts, weights))


def project_kernel(*refs):
    refs[4][...] = times_pieces(refs[:2], refs[2:4]).astype(bf16)


def project(acts, weights, columns):
    tokens, part = acts[0].shape
    depth = weights[0].shape[0]
    return pl.pallas_call(
        project_kernel,
        out_shape=jax.ShapeDtypeStruct((tokens, columns), bf16),
        grid=(columns // TILE,),
        in_specs=[resident((tokens, part))] * 2 + [pl.BlockSpec((depth, TILE), lambda j: (0, j))] * 2,
        out_specs=pl.BlockSpec((tokens, TILE), lambda j: (0, j)),
        compiler_params=params(),
        cost_estimate=cost(8 * tokens * depth * columns, 8 * depth * columns + 4 * tokens * part),
        name="project",
    )(*acts, *weights)


def project_back(acts, weights, firsts=None, halves=(0, 1)):
    tokens = acts[0].shape[0]
    depth = weights[0][0].shape[0]
    steps = depth // TILE
    count = len(acts)
    firsts = firsts or [0] * count
    wides = [a.shape[1] if not f else math.gcd(a.shape[1], f) for a, f in zip(acts, firsts)]
    parts = [(n, f // w + j, w, j) for n, (a, f, w) in enumerate(zip(acts, firsts, wides)) for j in range(a.shape[1] // w)]
    total = len(parts)

    def kernel(*refs):
        acts_in, out_ref = refs[:count], refs[-1]
        for p in range(len(halves)):
            pieces = refs[count + p * total : count + (p + 1) * total]

            @pl.when(pl.program_id(0) // steps == p)
            def _():
                out_ref[...] = sum(
                    dot(acts_in[n][:, j * w : (j + 1) * w], piece[...], 1, 1)
                    for (n, _, w, j), piece in zip(parts, pieces)
                ).astype(bf16)

    def spec(p, block, wide):
        return pl.BlockSpec((TILE, wide), lambda i: (jnp.clip(i - p * steps, 0, steps - 1), block))

    columns = sum(a.shape[1] for a in acts)
    return pl.pallas_call(
        kernel,
        out_shape=jax.ShapeDtypeStruct((tokens, len(halves) * depth), bf16),
        grid=(len(halves) * steps,),
        in_specs=[
            resident(a.shape) for a in acts
        ]
        + [spec(p, block, w) for p in range(len(halves)) for _, block, w, _ in parts],
        out_specs=pl.BlockSpec((tokens, TILE), lambda i: (0, i)),
        compiler_params=params(),
        cost_estimate=cost(8 * tokens * depth * columns, (8 * depth + 2 * tokens) * columns),
        name="project_back",
    )(*acts, *[weights[n][p] for p in halves for n, _, _, _ in parts])


def gain_rows(pieces, first):
    depth = pieces[0].shape[0]

    def kernel(*refs):
        for p in range(2):
            refs[2][:, p * depth : (p + 1) * depth] = refs[p][...].astype(f32).T[:8]

    out = pl.pallas_call(
        kernel,
        out_shape=jax.ShapeDtypeStruct((8, 2 * depth), f32),
        grid=(1,),
        in_specs=[pl.BlockSpec((depth, LANES), lambda i: (0, first // LANES))] * 2,
        out_specs=pl.BlockSpec((8, 2 * depth), lambda i: (0, 0)),
        compiler_params=params(),
        name="gain_rows",
    )(*pieces)
    return out[:1], out[1:2]


def forward_kernel(q_ref, kv_ref, seg_row, seg_col, ctx_ref, lse_ref):
    kv_heads = kv_ref.shape[1] // (2 * HEAD_SIZE)
    group = pl.program_id(1)
    keys = kv_ref[:, : kv_heads * HEAD_SIZE].astype(f32)
    values = kv_ref[:, kv_heads * HEAD_SIZE :].astype(f32)
    lane = lax.broadcasted_iota(jnp.int32, keys.shape, 1)
    low = lane < HEAD_SIZE
    here = low == (group == 0)
    both_keys = jnp.where(here, keys, pltpu.roll(keys, HEAD_SIZE, 1)).astype(bf16)
    both_values = jnp.where(here, values, pltpu.roll(values, HEAD_SIZE, 1)).astype(bf16)
    none = jnp.zeros_like(both_values)
    value_low = jnp.where(low, both_values, none)
    value_high = jnp.where(low, none, both_values)
    allowed = seg_row[...] <= seg_col[...]
    pairs = q_ref.shape[1] // (2 * HEAD_SIZE)
    for pair in range(pairs):
        cut = slice(pair * LANES, (pair + 1) * LANES)
        q = q_ref[:, cut] * bf16(HEAD_SIZE ** (-0.5))
        total = None
        for side, values_here in ((0, value_low), (1, value_high)):
            mine = jnp.where(low, q, none) if side == 0 else jnp.where(low, none, q)
            scores = jnp.where(allowed, dot(mine, both_keys, 1, 1), masked_value)
            top = jnp.max(scores, axis=-1, keepdims=True)
            weights = jnp.exp(scores - top)
            mass = jnp.sum(weights, axis=-1, keepdims=True)
            probs = (weights * (1.0 / mass)).astype(bf16)
            part = dot(probs, values_here, 1, 0)
            total = part if total is None else total + part
            lse_ref[:, 2 * pair + side : 2 * pair + side + 1] = top + jnp.log(mass)
        ctx_ref[:, cut] = total.astype(bf16)


def attention_forward(qkv, seg_row, seg_col, seqs, heads, kv):
    tokens = qkv.shape[0]
    length = tokens // seqs
    wide = heads // kv * HEAD_SIZE
    last = heads * HEAD_SIZE // (2 * kv * HEAD_SIZE)
    return pl.pallas_call(
        forward_kernel,
        out_shape=[
            jax.ShapeDtypeStruct((tokens, heads * HEAD_SIZE), bf16),
            jax.ShapeDtypeStruct((kv, tokens, heads // kv), f32),
        ],
        grid=(seqs, kv),
        in_specs=[
            pl.BlockSpec((length, wide), lambda s, g: (s, g)),
            pl.BlockSpec((length, 2 * kv * HEAD_SIZE), lambda s, g: (s, last)),
            pl.BlockSpec((None, 1, length), lambda s, g: (s, 0, 0)),
            pl.BlockSpec((None, length, 1), lambda s, g: (s, 0, 0)),
        ],
        out_specs=[
            pl.BlockSpec((length, wide), lambda s, g: (s, g)),
            pl.BlockSpec((None, length, heads // kv), lambda s, g: (g, s, 0)),
        ],
        compiler_params=params(2),
        cost_estimate=cost(16 * tokens * length * heads * HEAD_SIZE, 6 * tokens * heads * HEAD_SIZE),
        name="attention_forward",
    )(qkv, qkv, seg_row, seg_col)


def backward_kernel(q_ref, kv_ref, dctx_ref, lse_ref, seg_row, seg_col, cos_ref, sin_ref, out_ref):
    kv_heads = kv_ref.shape[1] // (2 * HEAD_SIZE)
    group = pl.program_id(1)
    wide = q_ref.shape[1]
    q_cols = kv_heads * wide
    scale = HEAD_SIZE ** (-0.5)
    half = HEAD_SIZE // 2
    keys = kv_ref[:, : kv_heads * HEAD_SIZE].astype(f32)
    values = kv_ref[:, kv_heads * HEAD_SIZE :].astype(f32)
    lane = lax.broadcasted_iota(jnp.int32, keys.shape, 1)
    low = lane < HEAD_SIZE
    here = low == (group == 0)
    both_keys = jnp.where(here, keys, pltpu.roll(keys, HEAD_SIZE, 1)).astype(bf16)
    both_values = jnp.where(here, values, pltpu.roll(values, HEAD_SIZE, 1)).astype(bf16)
    none = jnp.zeros_like(both_keys)
    key_low = jnp.where(low, both_keys, none)
    key_high = jnp.where(low, none, both_keys)
    allowed = seg_row[...] <= seg_col[...]
    cosine, sine = cos_ref[...], sin_ref[...]

    def unrotate(rows):
        turned = rows * sine
        ahead = pltpu.roll(turned, LANES - half, 1)
        behind = pltpu.roll(turned, half, 1)
        return rows * cosine + jnp.where(lane % HEAD_SIZE < half, ahead, -behind)

    dkey = jnp.zeros(keys.shape, f32)
    dvalue = jnp.zeros(keys.shape, f32)
    pairs = q_ref.shape[1] // LANES
    for pair in range(pairs):
        cut = slice(pair * LANES, (pair + 1) * LANES)
        q = q_ref[:, cut] * bf16(scale)
        dctx = dctx_ref[:, cut]
        dquery = None
        for side, keys_here in ((0, key_low), (1, key_high)):
            mine = jnp.where(low, q, none) if side == 0 else jnp.where(low, none, q)
            dmine = jnp.where(low, dctx, none) if side == 0 else jnp.where(low, none, dctx)
            scores = jnp.where(allowed, dot(mine, both_keys, 1, 1), masked_value)
            probs = jnp.exp(scores - lse_ref[:, 2 * pair + side : 2 * pair + side + 1])
            dprobs = dot(dmine, both_values, 1, 1)
            delta = jnp.sum(probs * dprobs, axis=-1, keepdims=True)
            dscores = (probs * (dprobs - delta)).astype(bf16)
            part = dot(dscores, keys_here, 1, 0)
            dquery = part if dquery is None else dquery + part
            dkey = dkey + dot(dscores, mine, 0, 0)
            dvalue = dvalue + dot(probs.astype(bf16), dmine, 0, 0)
        start = pl.multiple_of(group * wide + pair * LANES, LANES)
        out_ref[:, pl.ds(start, LANES)] = unrotate(dquery * scale).astype(bf16)
    dkey = unrotate(dkey + pltpu.roll(dkey, HEAD_SIZE, 1)).astype(bf16)
    dvalue = (dvalue + pltpu.roll(dvalue, HEAD_SIZE, 1)).astype(bf16)

    key_cut, value_cut = slice(q_cols, q_cols + LANES), slice(q_cols + LANES, q_cols + 2 * LANES)

    @pl.when(group == 0)
    def _():
        out_ref[:, key_cut] = dkey
        out_ref[:, value_cut] = dvalue

    @pl.when(group == 1)
    def _():
        out_ref[:, key_cut] = jnp.where(low, out_ref[:, key_cut], dkey)
        out_ref[:, value_cut] = jnp.where(low, out_ref[:, value_cut], dvalue)


def attention_backward(qkv, dctx, lse, seg_row, seg_col, cosine, sine, seqs, heads, kv):
    tokens, columns = qkv.shape
    length = tokens // seqs
    wide = heads // kv * HEAD_SIZE
    last = heads * HEAD_SIZE // (2 * kv * HEAD_SIZE)
    table = pl.BlockSpec((length, LANES), lambda s, g: (s, 0))
    return pl.pallas_call(
        backward_kernel,
        out_shape=jax.ShapeDtypeStruct((tokens, columns), bf16),
        grid=(seqs, kv),
        in_specs=[
            pl.BlockSpec((length, wide), lambda s, g: (s, g)),
            pl.BlockSpec((length, 2 * kv * HEAD_SIZE), lambda s, g: (s, last)),
            pl.BlockSpec((length, wide), lambda s, g: (s, g)),
            pl.BlockSpec((None, length, heads // kv), lambda s, g: (g, s, 0)),
            pl.BlockSpec((None, 1, length), lambda s, g: (s, 0, 0)),
            pl.BlockSpec((None, length, 1), lambda s, g: (s, 0, 0)),
            table,
            table,
        ],
        out_specs=pl.BlockSpec((length, columns), lambda s, g: (s, 0)),
        compiler_params=params(2),
        cost_estimate=cost(40 * tokens * length * heads * HEAD_SIZE, 10 * tokens * heads * HEAD_SIZE),
        name="attention_backward",
    )(qkv, qkv, dctx, lse, seg_row, seg_col, cosine, sine)


def gate_up(acts, first, second):
    tokens, part = acts[0].shape
    depth = first[0].shape[0]
    steps = [w[0].shape[1] // (2 * TILE) for w in (first, second)]

    def kernel(*refs):
        outs, active_ref = refs[6:8], refs[8]

        def fill(weights, gu_ref):
            both = times_pieces(refs[:2], weights)
            gate, up = both[:, :TILE], both[:, TILE:]
            gu_ref[...] = both.astype(bf16)
            active_ref[...] = (gate * (1.0 / (1.0 + jnp.exp(-gate))) * up).astype(bf16)

        pl.when(pl.program_id(0) < steps[0])(lambda: fill(refs[2:4], outs[0]))
        pl.when(pl.program_id(0) >= steps[0])(lambda: fill(refs[4:6], outs[1]))

    def low(j):
        return jnp.minimum(j, steps[0] - 1)

    def high(j):
        return jnp.maximum(j - steps[0], 0)

    columns = 2 * TILE * sum(steps)
    return pl.pallas_call(
        kernel,
        out_shape=[jax.ShapeDtypeStruct((tokens, 2 * TILE * n), bf16) for n in steps]
        + [jax.ShapeDtypeStruct((tokens, TILE * sum(steps)), bf16)],
        grid=(sum(steps),),
        in_specs=[resident((tokens, part))] * 2
        + [pl.BlockSpec((depth, 2 * TILE), lambda j: (0, low(j)))] * 2
        + [pl.BlockSpec((depth, 2 * TILE), lambda j: (0, high(j)))] * 2,
        out_specs=[
            pl.BlockSpec((tokens, 2 * TILE), lambda j: (0, low(j))),
            pl.BlockSpec((tokens, 2 * TILE), lambda j: (0, high(j))),
            pl.BlockSpec((tokens, TILE), lambda j: (0, j)),
        ],
        compiler_params=params(),
        cost_estimate=cost(4 * tokens * depth * columns, 4 * depth * columns + 4 * tokens * columns, tokens * columns),
        name="gate_up",
    )(*acts, *first, *second)


def swiglu_back(acts, weights, first, second):
    tokens, part = acts[0].shape
    depth = weights[0].shape[0]
    steps = [u.shape[1] // (2 * TILE) for u in (first, second)]

    def kernel(*refs):
        d_active = times_pieces(refs[:2], refs[2:4])

        def fill(gu_ref, out_ref):
            gate, up = gu_ref[:, :TILE].astype(f32), gu_ref[:, TILE:].astype(f32)
            sig = 1.0 / (1.0 + jnp.exp(-gate))
            out_ref[:, :TILE] = (d_active * up * sig * (1.0 + gate * (1.0 - sig))).astype(bf16)
            out_ref[:, TILE:] = (d_active * (gate * sig)).astype(bf16)

        pl.when(pl.program_id(0) < steps[0])(lambda: fill(refs[4], refs[6]))
        pl.when(pl.program_id(0) >= steps[0])(lambda: fill(refs[5], refs[7]))

    def low(j):
        return jnp.minimum(j, steps[0] - 1)

    def high(j):
        return jnp.maximum(j - steps[0], 0)

    columns = 2 * TILE * sum(steps)
    wide = [
        pl.BlockSpec((tokens, 2 * TILE), lambda j: (0, low(j))),
        pl.BlockSpec((tokens, 2 * TILE), lambda j: (0, high(j))),
    ]
    return pl.pallas_call(
        kernel,
        out_shape=[jax.ShapeDtypeStruct(u.shape, bf16) for u in (first, second)],
        grid=(sum(steps),),
        in_specs=[resident((tokens, part))] * 2 + [pl.BlockSpec((depth, TILE), lambda j: (0, j))] * 2 + wide,
        out_specs=wide,
        compiler_params=params(),
        cost_estimate=cost(4 * tokens * depth * columns, 4 * depth * columns + 4 * tokens * columns, tokens * columns),
        name="swiglu_back",
    )(*acts, *weights, first, second)


def row_specs(own_len, wide):
    mine = pl.BlockSpec((None, None, own_len, wide), lambda s, h: (s, h, 0, 0))
    theirs = pl.BlockSpec((None, None, own_len, wide), lambda s, h: (s, 1 - h, 0, 0))
    return mine, theirs


def load_rows(refs):
    return jnp.concatenate([r[...].astype(f32) for r in refs], axis=-1)


def store_rows(refs, rows):
    half = rows.shape[-1] // 2
    refs[0][...] = rows[:, :half].astype(bf16)
    refs[1][...] = rows[:, half:].astype(bf16)


def middle(resid, partial, received, gain, which, seqs, own_len, before=()):
    width = partial.shape[1]
    half = width // 2

    def kernel(res_low, res_high, par, rec, gain_ref, *refs):
        hid, norm = refs[-4:-2], refs[-2:]
        rows = load_rows([res_low, res_high]) + (par[...].astype(f32) + rec[...].astype(f32))
        factor = lax.rsqrt(jnp.mean(rows * rows, axis=-1, keepdims=True) + epsilon)
        store_rows(hid, rows)
        store_rows(norm, rows * factor * gain_ref[...])

    mine = pl.BlockSpec((None, None, own_len, half), lambda h: (which, h, 0, 0))
    full = pl.BlockSpec((None, None, own_len, width), lambda h: (which, h, 0, 0))
    theirs = pl.BlockSpec((None, own_len, width), lambda h: (1 - h, 0, 0))
    shape = (seqs, 2, own_len, half)
    tokens = seqs * 2 * own_len
    before = [r.reshape(shape) for r in before]
    outs = pl.pallas_call(
        kernel,
        out_shape=[jax.ShapeDtypeStruct(shape, bf16)] * 4,
        grid=(2,),
        in_specs=[mine, mine, full, theirs, pl.BlockSpec((1, width), lambda h: (0, 0))]
        + [pl.BlockSpec(memory_space=pl.ANY)] * len(before),
        out_specs=[mine] * 4,
        input_output_aliases={5 + n: n for n in range(len(before))},
        compiler_params=params(),
        cost_estimate=cost(5 * tokens * width, 5 * tokens * width),
        name="middle",
    )(
        *[r.reshape(shape) for r in resid],
        partial.reshape(seqs, 2, own_len, width),
        received.reshape(2, own_len, width),
        gain,
        *before,
    )
    return tuple(o.reshape(tokens, half) for o in outs)


def middle_back(grad, hidden, partial, received, gain, seqs, own_len):
    tokens, half = grad[0].shape
    width = 2 * half

    def kernel(*refs):
        rows = load_rows(refs[2:4])
        factor = lax.rsqrt(jnp.mean(rows * rows, axis=-1, keepdims=True) + epsilon)
        unit = rows * factor
        scaled = (load_rows(refs[4:6]) + load_rows(refs[6:8])) * refs[8][...]
        spread = jnp.mean(scaled * unit, axis=-1, keepdims=True)
        store_rows(refs[9:11], load_rows(refs[:2]) + factor * (scaled - unit * spread))

    mine, theirs = row_specs(own_len, half)
    shape = (seqs, 2, own_len, half)
    outs = pl.pallas_call(
        kernel,
        out_shape=[jax.ShapeDtypeStruct(shape, bf16)] * 2,
        grid=(seqs, 2),
        in_specs=[mine] * 6 + [theirs] * 2 + [pl.BlockSpec((1, width), lambda s, h: (0, 0))],
        out_specs=[mine] * 2,
        compiler_params=params(2),
        cost_estimate=cost(20 * tokens * width, 10 * tokens * width),
        name="middle_back",
    )(*[r.reshape(shape) for r in (*grad, *hidden, *partial, *received)], gain)
    return tuple(o.reshape(tokens, half) for o in outs)


def leave(slots, residual, partial, received, norm, in_turns=False):
    seqs, own_len, width = received.shape
    half = width // 2
    blocks = slots.shape[0]
    block = width // blocks
    narrow = block % LANES != 0

    def kernel(slots_ref, *refs):
        out_ref = refs[-1]
        total = refs[2][...].astype(f32) + refs[3][...].astype(f32)
        if norm is not None:
            rows = load_rows(refs[4:6])
            factor = lax.rsqrt(jnp.mean(rows * rows, axis=-1, keepdims=True) + epsilon)
            unit = rows * factor
            scaled = total * refs[6][...]
            spread = jnp.mean(scaled * unit, axis=-1, keepdims=True)
            total = factor * (scaled - unit * spread)
        residual_rows = load_rows(refs[:2])
        per = blocks // 2
        for b in range(blocks):
            start = b * block if narrow else pl.multiple_of(slots_ref[b] * block, block)
            at = b // per * per + turned(b % per, per // 2) if in_turns else b
            out = residual_rows[:, b * block : (b + 1) * block] + total[:, at * block : (at + 1) * block]
            out_ref[:, pl.ds(start, block)] = out.astype(bf16)

    mine = pl.BlockSpec((None, None, own_len, half), lambda s, t: (s, 0, 0, 0))
    full = pl.BlockSpec((None, None, own_len, width), lambda s, t: (s, 0, 0, 0))
    whole = pl.BlockSpec((None, own_len, width), lambda s, t: (s, 0, 0))
    arrays = [r.reshape(seqs, 2, own_len, half) for r in residual]
    arrays += [partial.reshape(seqs, 2, own_len, width), received]
    specs = [mine, mine, full, whole]
    if norm is not None:
        arrays += [r.reshape(seqs, 2, own_len, half) for r in norm[0]] + [norm[1]]
        specs += [mine, mine, pl.BlockSpec((1, width), lambda s, t: (0, 0))]
    out = pl.pallas_call(
        kernel,
        out_shape=jax.ShapeDtypeStruct((seqs, own_len, width), bf16),
        grid_spec=pltpu.PrefetchScalarGridSpec(
            num_scalar_prefetch=1, grid=(seqs,), in_specs=specs, out_specs=whole
        ),
        compiler_params=params(),
        cost_estimate=cost(20 * seqs * own_len * width, 12 * seqs * own_len * width),
        name="leave",
    )(slots, *arrays)
    if narrow:
        out = out.reshape(seqs, own_len, blocks, block)[:, :, jnp.argsort(slots)].reshape(seqs, own_len, width)
    return out


def shards(
    inputs,
    block_ids,
    positions,
    w_query,
    key_weight,
    value_weight,
    w_out,
    w_gate,
    w_up,
    w_down,
    attn_gain,
    mlp_gain,
    out_grad,
):
    seqs, own_len, width = inputs.shape
    length = block_ids.shape[1]
    tokens = seqs * length
    side = lax.axis_index("tensor")
    hd = HEAD_SIZE
    heads = w_query.shape[1] // hd
    kv = key_weight.shape[1] // hd
    ff = w_gate.shape[1]
    ring = Ring(lax.axis_size("dp"))
    rows = width // ring.size
    slots = ring.slots(lax.axis_index("dp"))

    def across(value):
        return lax.ppermute(value, "tensor", [(0, 1), (1, 0)])

    def halves(table):
        table = table.reshape(seqs, 2, own_len)
        return jnp.where(side == 0, table, table[:, ::-1]).reshape(seqs, length)

    kv_wide = kv * hd
    blocks = ff // TILE
    cut = (blocks + 1) // 2
    q_cols = heads * hd
    qkv_cols = q_cols + 2 * kv_wide
    out_cols = w_out.shape[0]

    def interleave(pair, first, last):
        parts = [w[:, j * TILE : (j + 1) * TILE] for j in range(first, last) for w in pair]
        return jnp.concatenate(parts, axis=1)

    def other(part):
        return part.reshape(seqs, 2, own_len, width)[:, 1]

    step = -(-blocks // 4)
    bounds = [0, step, cut, cut + step, blocks]
    Q, O, G0, G1, G2, G3, D0, D1 = range(8)
    gates = [G0, G1, G2, G3]
    gain_block = jnp.pad(jnp.stack([attn_gain, mlp_gain], axis=1), ((0, 0), (0, LANES - 2)))
    qkv_shard = jnp.concatenate([w_query, key_weight, value_weight], axis=1)
    columns_1 = cut * TILE
    v = Values()
    v.held, v.got = {}, {}

    def far_send(name):
        v.got[name] = ring.gather_far(v.held[name])

    def grow(name, send, after):
        v.held[name] = joined(tie(v.held[name], *after) if after else v.held[name], v.got[name])
        v.got[name] = send(v.held[name])
        return v.held[name]

    def near_send(name, *after):
        return grow(name, lambda value: ring.along(value, 1), after)

    def pair_send(name, *after):
        return grow(name, ring.pair, after)

    def core_send(name, *after):
        return grow(name, ring.core, after)

    def core_join(name):
        v.held[name] = joined(v.held[name], v.got[name])
        v.got[name] = v.held[name][:LANES]

    def core_send_joined(name):
        v.got[name] = ring.core(v.held[name])

    def whole(name):
        return [v.held[name], v.got[name]]

    v.held[Q] = jnp.concatenate([qkv_shard, gain_block], axis=1)
    v.held[O] = w_out.T
    down = w_down.T
    far_send(Q)
    down_pair = ring.pair(down)
    v.rows = inputs.reshape(seqs, own_len, width)
    v.grad = out_grad.reshape(seqs, own_len, width)
    got_rows = across(v.rows)
    v.down, v.down_pair = down, down_pair
    v.held[G0] = interleave((w_gate, w_up), 0, step)
    v.fence()

    near_send(Q)
    far_send(O)
    segments = halves(tie(block_ids, v.held[Q]))
    seg_row, seg_col = segments[:, None, :], segments[:, :, None]
    steps_half = jnp.arange(hd // 2, dtype=f32)
    frequency = jnp.exp(steps_half * (-2.0 * math.log(rope_base) / hd))
    angles = halves(tie(positions, v.held[Q])).reshape(tokens, 1).astype(f32) * frequency
    cos_head, sin_head = jnp.tile(jnp.cos(angles), (1, 2)), jnp.tile(jnp.sin(angles), (1, 2))
    cosine = jnp.concatenate([jnp.tile(cos_head, (1, TILE // hd + kv)), jnp.ones((tokens, kv_wide), f32)], axis=1)
    sine = jnp.concatenate([jnp.tile(sin_head, (1, TILE // hd + kv)), jnp.zeros((tokens, kv_wide), f32)], axis=1)

    v.tables = [cosine, sine, seg_row, seg_col]
    gate_up_shards = (tie(w_gate, v.held[Q]), tie(w_up, v.held[Q]))
    for name, first, last in zip(gates[1:], bounds[1:-1], bounds[2:]):
        v.held[name] = interleave(gate_up_shards, first, last)
    v.held[D0] = joined(v.down[:, :columns_1], v.down_pair[:, :columns_1])
    v.held[D1] = joined(v.down[:, columns_1:], v.down_pair[:, columns_1:])
    del v.down, v.down_pair
    v.got_rows = got_rows
    v.fence()

    sent = pair_send(Q)
    near_send(O, sent)
    far_send(G0)
    v.far_pair = [ring.gather_far(v.held[D1][:rows])]
    v.got_grad = across(v.grad)
    v.rows = jnp.stack([v.rows, v.got_rows], axis=1).reshape(tokens, width)
    del v.got_rows
    v.fence()

    sent = near_send(G0, pair_send(O))
    far_send(G1)
    core_send(Q, sent)
    both_grad = jnp.stack([v.grad, v.got_grad], axis=1).reshape(tokens, width)
    del v.got_grad
    entered = enter(both_grad, slots, None)
    v.grad, v.grad_turned = tuple(entered[:2]), tuple(entered[2:])
    v.fence()

    near_send(G1, pair_send(G0))
    core_o = [ring.core(v.held[O]), ring.core(v.got[O])]
    v.held[O], v.got[O] = joined(v.held[O], v.got[O]), core_o
    far_send(G2)
    v.attn_gain, v.mlp_gain = gain_rows(whole(Q), qkv_cols)
    entered = enter(v.rows, slots, v.attn_gain)
    del v.rows
    v.resid, v.normed = tuple(entered[:2]), tuple(entered[2:])
    v.qkv = project_qkv(v.normed, whole(Q), v.tables[0], v.tables[1], 0, qkv_cols)
    v.fence()

    near_send(G2, pair_send(G1))
    far_send(G3)
    v.far_pair.append(ring.gather_far(v.held[D1][rows:]))
    v.got[O] = joined(*v.got[O])
    v.context, v.lse = attention_forward(v.qkv, v.tables[2], v.tables[3], seqs, heads, kv)
    v.out_part = project_back([v.context], [whole(O)])
    v.out_got = [v.out_part[w * length : (w + 1) * length] for w in range(seqs)]
    v.fence()

    near_send(G3, pair_send(G2))
    core_join(G0)
    core_join(G1)
    far_send(D0)
    lines = [p.reshape(-1, rows, p.shape[1]) for p in v.far_pair]
    v.got[D1] = jnp.stack(lines, axis=1).reshape(-1, lines[0].shape[2])
    del v.far_pair
    v.out_got[0] = across(v.out_got[0])
    v.fence()

    near_send(D0, pair_send(G3))
    core_send_joined(G0)
    core_send_joined(G1)
    core_join(G2)
    v.middle = middle(v.resid, v.out_part, v.out_got[0], v.mlp_gain, 0, seqs, own_len)
    for w in range(1, seqs):
        v.out_got[w] = across(v.out_got[w])
    v.fence()

    v.far, v.side, v.sums = {}, {}, {}
    v.gu, v.active, v.du = {}, {}, {}
    v.dn, v.got_dn = [None] * 2, [None] * 2
    R = [
        Reduce(ring, v, Q, lambda: v.normed, lambda: v.d_qkv),
        Reduce(ring, v, O, lambda: v.attn_grad, lambda: v.context),
    ]
    for k, name in enumerate(gates):
        R.append(Reduce(ring, v, name, lambda: v.normed_mlp, lambda k=k: v.du[k]))
    for k, name in enumerate([D0, D1]):
        R.append(Reduce(ring, v, name, lambda: v.grad, lambda k=k: v.active[k]))

    def dn_half(which, *after):
        acts = [tie(v.du[0], *after) if after else v.du[0]] + [v.du[k] for k in range(1, 4)]
        v.dn[which] = project_back(acts, [whole(n) for n in gates], None, (which,))

    near_send(D1)
    core_send_joined(G2)
    sent = core_send(G3)
    core_send(D0, sent)
    for w in range(1, seqs):
        v.middle = middle(v.resid, v.out_part, v.out_got[w], v.mlp_gain, w, seqs, own_len, v.middle)
    v.hidden, v.normed_mlp = v.middle[:2], v.middle[2:]
    del v.out_part, v.out_got, v.middle
    v.gu[0], v.gu[1], v.active[0] = gate_up(v.normed_mlp, whole(G0), whole(G1))
    R[D0].far()
    v.fence()

    core_send(D1)
    R[D0].send_far()
    v.gu[2], v.gu[3], v.active[1] = gate_up(v.normed_mlp, whole(G2), whole(G3))
    v.du[0], v.du[1] = swiglu_back(v.grad_turned, whole(D0), v.gu.pop(0), v.gu.pop(1))
    R[D1].far()
    v.fence()

    sent = R[D0].side()
    R[D0].send_side()
    R[D1].send_far()
    v.du[2], v.du[3] = swiglu_back(
        [tie(v.grad_turned[0], sent), v.grad_turned[1]], whole(D1), v.gu.pop(2), v.gu.pop(3)
    )
    for name in gates:
        R[name].far()
    v.fence()

    for name in gates[:3]:
        R[name].send_far()
    sent = R[D1].side()
    R[D1].send_side()
    sent = R[D0].near(sent)
    dn_half(0, sent)
    v.fence()

    v.got_dn[0] = across(v.dn[0])
    R[G3].send_far()
    sent = R[G0].side()
    R[G0].send_side()
    sent = R[D1].near(sent)
    sent = R[D0].fold(sent)
    dn_half(1, sent)
    R[G1].side_ahead(sent)
    v.fence()

    v.got_dn[1] = across(v.dn[1])
    R[G1].send_side()
    sent = R[G0].near()
    sent = R[D1].fold(sent)
    R[D0].rows()
    R[G2].side_ahead(sent)
    R[G3].side_ahead(sent)
    v.mlp_part = project_back([tie(v.active[0], sent), v.active[1]], [whole(D0), whole(D1)])
    v.mlp_other = other(v.mlp_part)
    v.fence()

    R[G2].send_side()
    R[G3].send_side()
    v.attn_grad = middle_back(v.grad, v.hidden, v.dn, v.got_dn, v.mlp_gain, seqs, own_len)
    sent = R[O].far()
    R[O].send_far()
    sent = R[G1].near(sent)
    sent = R[G0].fold(sent)
    R[D1].rows()
    d_context = sum(dot(a, w, 1, 0) for a, w in zip([tie(v.attn_grad[0], sent), v.attn_grad[1]], whole(O))).astype(bf16)
    v.d_qkv = attention_backward(
        v.qkv, d_context, v.lse, v.tables[2], v.tables[3], v.tables[0], v.tables[1], seqs, heads, kv
    )
    R[Q].far()
    v.fence()

    R[Q].send_far()
    v.mlp_got = across(v.mlp_other)
    del v.mlp_other
    sent = R[O].side()
    R[O].send_side()
    sent = R[G2].near(sent)
    sent = R[G1].fold(sent)
    R[G0].rows()
    v.in_part = project_back([tie(v.d_qkv, sent)], [whole(Q)])
    v.in_other = other(v.in_part)
    v.fence()

    v.in_got = across(v.in_other)
    del v.in_other
    sent = R[Q].side()
    R[Q].send_side()
    sent = R[O].near(sent)
    sent = R[G3].near(sent)
    R[G2].fold(sent)
    R[G1].rows()
    v.output = leave(slots, v.hidden, v.mlp_part, v.mlp_got, None, True)
    v.fence()

    sent = R[Q].near()
    sent = R[O].fold(sent)
    R[G3].fold(sent)
    R[G2].rows()
    v.input_grad = leave(slots, v.attn_grad, v.in_part, v.in_got, (v.resid, v.attn_gain))
    v.fence()

    R[Q].fold()
    R[O].rows()
    R[G3].rows()
    v.fence()
    R[Q].rows()

    def pick(which):
        parts = [
            v.sums[gates[k]][:, (2 * j + which) * TILE : (2 * j + which + 1) * TILE]
            for k in range(4)
            for j in range(bounds[k + 1] - bounds[k])
        ]
        return jnp.concatenate(parts, axis=1)

    grad_gate, grad_up, grad_qkv = pick(0), pick(1), v.sums[Q]

    def gain_sum(weights, grads, gain):
        total = sum(jnp.sum(w.astype(f32) * g, axis=1) for w, g in zip(weights, grads))
        return total / gain.astype(f32)

    gain_sums = jnp.stack([
        gain_sum([qkv_shard], [grad_qkv], attn_gain),
        gain_sum([w_gate, w_up], [grad_gate, grad_up], mlp_gain),
    ])
    gain_sums = gain_sums + across(gain_sums)
    return (
        v.output,
        v.input_grad,
        grad_qkv[:, :q_cols],
        grad_qkv[:, q_cols : q_cols + kv_wide],
        grad_qkv[:, q_cols + kv_wide :],
        v.sums[O].T,
        grad_gate,
        grad_up,
        jnp.concatenate([v.sums[D0], v.sums[D1]], axis=1).T,
        gain_sums[0],
        gain_sums[1],
    )


def solution(mesh):
    row, col = P("dp", "tensor"), P("tensor", "dp")
    seq = P("dp", "tensor", None)
    return jax.shard_map(
        shards,
        mesh=mesh,
        in_specs=(seq, P("dp", None), P("dp", None), row, row, row, col, row, row, col, P("dp"), P("dp"), seq),
        out_specs=(seq, seq, row, row, row, col, row, row, col, P("dp"), P("dp")),
        check_vma=False,
    )
```

```python
import functools
import math

import jax
import jax.numpy as jnp
from jax import lax
from jax.experimental import pallas as pl
from jax.experimental.pallas import tpu as pltpu
from jax.sharding import PartitionSpec as P

HEAD_SIZE = 64
LANES = 128
TILE = 256
SHRINK = 10**6
epsilon = 1e-05
rope_base = 10000.0
masked_value = -1e30
bf16 = jnp.bfloat16
f32 = jnp.float32
VMEM_LIMIT = 60 * 1024 * 1024


def dot(left, right, left_dim, right_dim):
    return lax.dot_general(
        left, right, (((left_dim,), (right_dim,)), ((), ())), preferred_element_type=f32
    )


def tie(value, *others):
    return lax.optimization_barrier((value,) + others)[0]


def params(steps=1):
    return pltpu.CompilerParams(
        dimension_semantics=("arbitrary",) * steps, vmem_limit_bytes=VMEM_LIMIT
    )


def resident(shape):
    return pl.BlockSpec(
        shape, lambda *_: (0,) * len(shape), pipeline_mode=pl.Buffered(1)
    )


def cost(flops, moved, trans=0):
    return pl.CostEstimate(flops=flops // SHRINK + 1, bytes_accessed=moved // SHRINK + 1, transcendentals=0)


class Ring:
    def __init__(self, size):
        self.size = size
        self.line = size // 4
        self.reaches = [self.line >> k for k in range(1, self.line.bit_length())]

    def swap(self, value, bits):
        return lax.ppermute(value, "dp", [(i, i ^ bits) for i in range(self.size)])

    def core(self, value):
        return self.swap(value, 1)

    def pair(self, value):
        return self.swap(value, 2)

    def along(self, value, reach):
        return self.swap(value, 4 * reach)

    def slots(self, me):
        order = [0]
        for reach in self.reaches:
            order = order + [o ^ reach for o in order]
        return jnp.stack([me ^ (l * 4 + p * 2 + c) for c in range(2) for p in range(2) for l in order])

    def gather_far(self, shard):
        held = shard
        for reach in self.reaches[:-1]:
            held = jnp.concatenate([held, self.along(held, reach)], axis=0)
        return held[shard.shape[0] :] if self.line > 4 else self.along(shard, 2)


class Values:
    def fence(self):
        fields = vars(self)
        names = sorted(fields)
        fields.update(zip(names, lax.optimization_barrier([fields[n] for n in names])))


def joined(*parts):
    return jnp.concatenate(parts, axis=0)


def weight_grad(act, which, grads, adds, outs):
    tokens, width = act.shape
    columns = grads.shape[1]
    rows = width if which is None else width // 2
    tile = 2 * TILE if columns % (2 * TILE) == 0 else TILE
    at = which or 0

    def kernel(*refs):
        act_ref, grads_ref, turned_ref = refs[0], refs[1], refs[-1]

        @pl.when(pl.program_id(0) == 0)
        def _():
            turned_ref[...] = act_ref[...].astype(f32).T.astype(bf16)

        total = dot(turned_ref[...], grads_ref[...], 1, 0)
        for ref in refs[2 : 2 + len(adds)]:
            total = total + ref[...].astype(f32)
        for n, ref in enumerate(refs[2 + len(adds) : -1]):
            ref[...] = total[n * (rows // outs) : (n + 1) * (rows // outs)].astype(bf16)

    def add_spec(block):
        return pl.BlockSpec((rows, tile), lambda j: (block, j))

    return pl.pallas_call(
        kernel,
        out_shape=[jax.ShapeDtypeStruct((rows // outs, columns), bf16)] * outs,
        grid=(columns // tile,),
        in_specs=[
            pl.BlockSpec((tokens, rows), lambda j: (0, at), pipeline_mode=pl.Buffered(1)),
            pl.BlockSpec((tokens, tile), lambda j: (0, j)),
        ]
        + [add_spec(block) for _, block in adds],
        out_specs=[pl.BlockSpec((rows // outs, tile), lambda j: (0, j))] * outs,
        scratch_shapes=[pltpu.VMEM((rows, tokens), bf16)],
        compiler_params=params(),
        cost_estimate=cost(2 * tokens * rows * columns, 2 * tokens * (rows + columns) + 4 * rows * columns),
        name="weight_grad",
    )(act, grads, *[array for array, _ in adds])


class Reduce:
    def __init__(self, ring, v, name, acts, grads):
        self.ring, self.v, self.name, self.acts, self.grads = ring, v, name, acts, grads

    def part(self, half, which=None, *after):
        act = self.acts()[half]
        if which is not None:
            quarter = act.shape[1] // 2
            act = act[:, which * quarter : (which + 1) * quarter]
        return dot(tie(act, *after) if after else act, self.grads(), 0, 0)

    def far(self, *after):
        self.v.far[self.name] = self.part(1, None, *after).astype(bf16)
        return self.v.far[self.name]

    def send_far(self):
        self.v.far[self.name] = self.ring.core(self.v.far[self.name])

    def side(self, *after):
        far = self.v.far[self.name]
        quarter = far.shape[0] // 2
        out = (self.part(0, 1, *after) + far[quarter:].astype(f32)).astype(bf16)
        self.v.side[self.name] = out
        return out

    def side_ahead(self, *after):
        (out,) = weight_grad(tie(self.acts()[0], *after), 1, self.grads(), [(self.v.far[self.name], 1)], 1)
        self.v.side[self.name] = out
        return out

    def send_side(self):
        self.v.side[self.name] = self.ring.pair(self.v.side[self.name])

    def near(self, *after):
        side = self.v.side[self.name]
        out = self.part(0, 0, *after) + self.v.far[self.name][: side.shape[0]].astype(f32) + side.astype(f32)
        half = out.shape[0] // 2
        send = out[half:].astype(bf16)
        self.v.far[self.name] = out[:half].astype(bf16)
        self.v.side[self.name] = self.ring.along(send, 1)
        return self.v.far[self.name]

    def fold(self, *after):
        terms, reach = [self.v.far[self.name], self.v.side[self.name]], 2
        if after:
            terms[0] = tie(terms[0], *after)
        while True:
            rows = terms[0].shape[0] // 2
            got = self.ring.along(sum(t[rows:].astype(f32) for t in terms).astype(bf16), reach)
            terms, reach = [t[:rows] for t in terms] + [got], reach * 2
            if reach == self.ring.line:
                break
        self.v.far[self.name] = sum(t.astype(f32) for t in terms[:-1])
        self.v.side[self.name] = terms[-1]
        return self.v.far[self.name]

    def rows(self):
        self.v.sums[self.name] = self.v.far.pop(self.name) + self.v.side.pop(self.name).astype(f32)


def turned(block, line):
    return block % line * 2 + block // line


def enter(rows, slots, gain):
    count, width = rows.shape
    blocks = slots.shape[0]
    block = width // blocks
    per = blocks // 2
    half = width // 2
    step = count // 4
    norm = gain is not None
    narrow = block % LANES != 0
    if narrow:
        rows = rows.reshape(count, blocks, block)[:, slots].reshape(count, width)

    def kernel(slots_ref, x_ref, gain_ref, *outs):
        if norm:
            x = x_ref[...].astype(f32)
            factor = lax.rsqrt(jnp.mean(x * x, axis=-1, keepdims=True) + epsilon)
        for b in range(blocks):
            start = b * block if narrow else pl.multiple_of(slots_ref[b] * block, block)
            piece = x_ref[:, pl.ds(start, block)]
            at = slice((b % per) * block, (b % per + 1) * block)
            outs[b // per][:, at] = piece
            if not norm:
                there = turned(b % per, per // 2)
                outs[2 + b // per][:, there * block : (there + 1) * block] = piece
            if norm:
                g = gain_ref[:, b * block : (b + 1) * block]
                outs[2 + b // per][:, at] = (piece.astype(f32) * factor * g).astype(bf16)

    n_out = 4
    if gain is None:
        gain = jnp.ones((1, width), f32)
    return pl.pallas_call(
        kernel,
        out_shape=[jax.ShapeDtypeStruct((count, half), bf16)] * n_out,
        grid_spec=pltpu.PrefetchScalarGridSpec(
            num_scalar_prefetch=1,
            grid=(4,),
            in_specs=[
                pl.BlockSpec((step, width), lambda i, s: (i, 0)),
                pl.BlockSpec((1, width), lambda i, s: (0, 0)),
            ],
            out_specs=[pl.BlockSpec((step, half), lambda i, s: (i, 0))] * n_out,
        ),
        compiler_params=params(),
        cost_estimate=cost(10 * count * width, 2 * count * width * (1 + n_out // 2)),
        name="enter",
    )(slots, rows, gain)


def qkv_kernel(*refs):
    cos_ref, sin_ref, out_ref = refs[4:]
    raw = times_pieces(refs[:2], refs[2:4])
    lane = lax.broadcasted_iota(jnp.int32, raw.shape, 1) % HEAD_SIZE
    half = HEAD_SIZE // 2
    ahead = pltpu.roll(raw, raw.shape[1] - half, 1)
    behind = pltpu.roll(raw, half, 1)
    turned = jnp.where(lane < half, -ahead, behind)
    out_ref[...] = (raw * cos_ref[...] + turned * sin_ref[...]).astype(bf16)


def project_qkv(acts, weights, cosine, sine, first, columns):
    tokens, part = acts[0].shape
    steps = columns // TILE
    table = pl.BlockSpec((tokens, TILE), lambda j: (0, j // (steps - 1)))
    depth = weights[0].shape[0]
    return pl.pallas_call(
        qkv_kernel,
        out_shape=jax.ShapeDtypeStruct((tokens, columns), bf16),
        grid=(steps,),
        in_specs=[resident((tokens, part))] * 2
        + [pl.BlockSpec((depth, TILE), lambda j: (0, first + j))] * 2
        + [table, table],
        out_specs=pl.BlockSpec((tokens, TILE), lambda j: (0, j)),
        compiler_params=params(),
        cost_estimate=cost(8 * tokens * depth * columns, 8 * depth * columns + 4 * tokens * part),
        name="project_qkv",
    )(*acts, *weights, cosine, sine)


def times_pieces(acts, weights):
    per, rows = len(weights) // 2, weights[0].shape[0]
    return sum(dot(acts[i // per][:, i % per * rows : (i % per + 1) * rows], w[...], 1, 0) for i, w in enumerate(weights))


def project_kernel(*refs):
    refs[4][...] = times_pieces(refs[:2], refs[2:4]).astype(bf16)


def project(acts, weights, columns):
    tokens, part = acts[0].shape
    depth = weights[0].shape[0]
    return pl.pallas_call(
        project_kernel,
        out_shape=jax.ShapeDtypeStruct((tokens, columns), bf16),
        grid=(columns // TILE,),
        in_specs=[resident((tokens, part))] * 2 + [pl.BlockSpec((depth, TILE), lambda j: (0, j))] * 2,
        out_specs=pl.BlockSpec((tokens, TILE), lambda j: (0, j)),
        compiler_params=params(),
        cost_estimate=cost(8 * tokens * depth * columns, 8 * depth * columns + 4 * tokens * part),
        name="project",
    )(*acts, *weights)


def project_back(acts, weights, firsts=None, halves=(0, 1)):
    tokens = acts[0].shape[0]
    depth = weights[0][0].shape[0]
    steps = depth // TILE
    count = len(acts)
    firsts = firsts or [0] * count
    wides = [a.shape[1] if not f else math.gcd(a.shape[1], f) for a, f in zip(acts, firsts)]
    parts = [(n, f // w + j, w, j) for n, (a, f, w) in enumerate(zip(acts, firsts, wides)) for j in range(a.shape[1] // w)]
    total = len(parts)

    def kernel(*refs):
        acts_in, out_ref = refs[:count], refs[-1]
        for p in range(len(halves)):
            pieces = refs[count + p * total : count + (p + 1) * total]

            @pl.when(pl.program_id(0) // steps == p)
            def _():
                out_ref[...] = sum(
                    dot(acts_in[n][:, j * w : (j + 1) * w], piece[...], 1, 1)
                    for (n, _, w, j), piece in zip(parts, pieces)
                ).astype(bf16)

    def spec(p, block, wide):
        return pl.BlockSpec((TILE, wide), lambda i: (jnp.clip(i - p * steps, 0, steps - 1), block))

    columns = sum(a.shape[1] for a in acts)
    return pl.pallas_call(
        kernel,
        out_shape=jax.ShapeDtypeStruct((tokens, len(halves) * depth), bf16),
        grid=(len(halves) * steps,),
        in_specs=[
            resident(a.shape) for a in acts
        ]
        + [spec(p, block, w) for p in range(len(halves)) for _, block, w, _ in parts],
        out_specs=pl.BlockSpec((tokens, TILE), lambda i: (0, i)),
        compiler_params=params(),
        cost_estimate=cost(8 * tokens * depth * columns, (8 * depth + 2 * tokens) * columns),
        name="project_back",
    )(*acts, *[weights[n][p] for p in halves for n, _, _, _ in parts])


def gain_rows(pieces, first):
    depth = pieces[0].shape[0]

    def kernel(*refs):
        for p in range(2):
            refs[2][:, p * depth : (p + 1) * depth] = refs[p][...].astype(f32).T[:8]

    out = pl.pallas_call(
        kernel,
        out_shape=jax.ShapeDtypeStruct((8, 2 * depth), f32),
        grid=(1,),
        in_specs=[pl.BlockSpec((depth, LANES), lambda i: (0, first // LANES))] * 2,
        out_specs=pl.BlockSpec((8, 2 * depth), lambda i: (0, 0)),
        compiler_params=params(),
        name="gain_rows",
    )(*pieces)
    return out[:1], out[1:2]


def forward_kernel(q_ref, kv_ref, seg_row, seg_col, ctx_ref, lse_ref):
    kv_heads = kv_ref.shape[1] // (2 * HEAD_SIZE)
    group = pl.program_id(1)
    keys = kv_ref[:, : kv_heads * HEAD_SIZE].astype(f32)
    values = kv_ref[:, kv_heads * HEAD_SIZE :].astype(f32)
    lane = lax.broadcasted_iota(jnp.int32, keys.shape, 1)
    low = lane < HEAD_SIZE
    here = low == (group == 0)
    both_keys = jnp.where(here, keys, pltpu.roll(keys, HEAD_SIZE, 1)).astype(bf16)
    both_values = jnp.where(here, values, pltpu.roll(values, HEAD_SIZE, 1)).astype(bf16)
    none = jnp.zeros_like(both_values)
    value_low = jnp.where(low, both_values, none)
    value_high = jnp.where(low, none, both_values)
    allowed = seg_row[...] <= seg_col[...]
    pairs = q_ref.shape[1] // (2 * HEAD_SIZE)
    for pair in range(pairs):
        cut = slice(pair * LANES, (pair + 1) * LANES)
        q = q_ref[:, cut] * bf16(HEAD_SIZE ** (-0.5))
        total = None
        for side, values_here in ((0, value_low), (1, value_high)):
            mine = jnp.where(low, q, none) if side == 0 else jnp.where(low, none, q)
            scores = jnp.where(allowed, dot(mine, both_keys, 1, 1), masked_value)
            top = jnp.max(scores, axis=-1, keepdims=True)
            weights = jnp.exp(scores - top)
            mass = jnp.sum(weights, axis=-1, keepdims=True)
            probs = (weights * (1.0 / mass)).astype(bf16)
            part = dot(probs, values_here, 1, 0)
            total = part if total is None else total + part
            lse_ref[:, 2 * pair + side : 2 * pair + side + 1] = top + jnp.log(mass)
        ctx_ref[:, cut] = total.astype(bf16)


def attention_forward(qkv, seg_row, seg_col, seqs, heads, kv):
    tokens = qkv.shape[0]
    length = tokens // seqs
    wide = heads // kv * HEAD_SIZE
    last = heads * HEAD_SIZE // (2 * kv * HEAD_SIZE)
    return pl.pallas_call(
        forward_kernel,
        out_shape=[
            jax.ShapeDtypeStruct((tokens, heads * HEAD_SIZE), bf16),
            jax.ShapeDtypeStruct((kv, tokens, heads // kv), f32),
        ],
        grid=(seqs, kv),
        in_specs=[
            pl.BlockSpec((length, wide), lambda s, g: (s, g)),
            pl.BlockSpec((length, 2 * kv * HEAD_SIZE), lambda s, g: (s, last)),
            pl.BlockSpec((None, 1, length), lambda s, g: (s, 0, 0)),
            pl.BlockSpec((None, length, 1), lambda s, g: (s, 0, 0)),
        ],
        out_specs=[
            pl.BlockSpec((length, wide), lambda s, g: (s, g)),
            pl.BlockSpec((None, length, heads // kv), lambda s, g: (g, s, 0)),
        ],
        compiler_params=params(2),
        cost_estimate=cost(16 * tokens * length * heads * HEAD_SIZE, 6 * tokens * heads * HEAD_SIZE),
        name="attention_forward",
    )(qkv, qkv, seg_row, seg_col)


def backward_kernel(q_ref, kv_ref, dctx_ref, lse_ref, seg_row, seg_col, cos_ref, sin_ref, out_ref):
    kv_heads = kv_ref.shape[1] // (2 * HEAD_SIZE)
    group = pl.program_id(1)
    wide = q_ref.shape[1]
    q_cols = kv_heads * wide
    scale = HEAD_SIZE ** (-0.5)
    half = HEAD_SIZE // 2
    keys = kv_ref[:, : kv_heads * HEAD_SIZE].astype(f32)
    values = kv_ref[:, kv_heads * HEAD_SIZE :].astype(f32)
    lane = lax.broadcasted_iota(jnp.int32, keys.shape, 1)
    low = lane < HEAD_SIZE
    here = low == (group == 0)
    both_keys = jnp.where(here, keys, pltpu.roll(keys, HEAD_SIZE, 1)).astype(bf16)
    both_values = jnp.where(here, values, pltpu.roll(values, HEAD_SIZE, 1)).astype(bf16)
    none = jnp.zeros_like(both_keys)
    key_low = jnp.where(low, both_keys, none)
    key_high = jnp.where(low, none, both_keys)
    allowed = seg_row[...] <= seg_col[...]
    cosine, sine = cos_ref[...], sin_ref[...]

    def unrotate(rows):
        turned = rows * sine
        ahead = pltpu.roll(turned, LANES - half, 1)
        behind = pltpu.roll(turned, half, 1)
        return rows * cosine + jnp.where(lane % HEAD_SIZE < half, ahead, -behind)

    dkey = jnp.zeros(keys.shape, f32)
    dvalue = jnp.zeros(keys.shape, f32)
    pairs = q_ref.shape[1] // LANES
    for pair in range(pairs):
        cut = slice(pair * LANES, (pair + 1) * LANES)
        q = q_ref[:, cut] * bf16(scale)
        dctx = dctx_ref[:, cut]
        dquery = None
        for side, keys_here in ((0, key_low), (1, key_high)):
            mine = jnp.where(low, q, none) if side == 0 else jnp.where(low, none, q)
            dmine = jnp.where(low, dctx, none) if side == 0 else jnp.where(low, none, dctx)
            scores = jnp.where(allowed, dot(mine, both_keys, 1, 1), masked_value)
            probs = jnp.exp(scores - lse_ref[:, 2 * pair + side : 2 * pair + side + 1])
            dprobs = dot(dmine, both_values, 1, 1)
            delta = jnp.sum(probs * dprobs, axis=-1, keepdims=True)
            dscores = (probs * (dprobs - delta)).astype(bf16)
            part = dot(dscores, keys_here, 1, 0)
            dquery = part if dquery is None else dquery + part
            dkey = dkey + dot(dscores, mine, 0, 0)
            dvalue = dvalue + dot(probs.astype(bf16), dmine, 0, 0)
        start = pl.multiple_of(group * wide + pair * LANES, LANES)
        out_ref[:, pl.ds(start, LANES)] = unrotate(dquery * scale).astype(bf16)
    dkey = unrotate(dkey + pltpu.roll(dkey, HEAD_SIZE, 1)).astype(bf16)
    dvalue = (dvalue + pltpu.roll(dvalue, HEAD_SIZE, 1)).astype(bf16)

    key_cut, value_cut = slice(q_cols, q_cols + LANES), slice(q_cols + LANES, q_cols + 2 * LANES)

    @pl.when(group == 0)
    def _():
        out_ref[:, key_cut] = dkey
        out_ref[:, value_cut] = dvalue

    @pl.when(group == 1)
    def _():
        out_ref[:, key_cut] = jnp.where(low, out_ref[:, key_cut], dkey)
        out_ref[:, value_cut] = jnp.where(low, out_ref[:, value_cut], dvalue)


def attention_backward(qkv, dctx, lse, seg_row, seg_col, cosine, sine, seqs, heads, kv):
    tokens, columns = qkv.shape
    length = tokens // seqs
    wide = heads // kv * HEAD_SIZE
    last = heads * HEAD_SIZE // (2 * kv * HEAD_SIZE)
    table = pl.BlockSpec((length, LANES), lambda s, g: (s, 0))
    return pl.pallas_call(
        backward_kernel,
        out_shape=jax.ShapeDtypeStruct((tokens, columns), bf16),
        grid=(seqs, kv),
        in_specs=[
            pl.BlockSpec((length, wide), lambda s, g: (s, g)),
            pl.BlockSpec((length, 2 * kv * HEAD_SIZE), lambda s, g: (s, last)),
            pl.BlockSpec((length, wide), lambda s, g: (s, g)),
            pl.BlockSpec((None, length, heads // kv), lambda s, g: (g, s, 0)),
            pl.BlockSpec((None, 1, length), lambda s, g: (s, 0, 0)),
            pl.BlockSpec((None, length, 1), lambda s, g: (s, 0, 0)),
            table,
            table,
        ],
        out_specs=pl.BlockSpec((length, columns), lambda s, g: (s, 0)),
        compiler_params=params(2),
        cost_estimate=cost(40 * tokens * length * heads * HEAD_SIZE, 10 * tokens * heads * HEAD_SIZE),
        name="attention_backward",
    )(qkv, qkv, dctx, lse, seg_row, seg_col, cosine, sine)


def gate_up(acts, first, second):
    tokens, part = acts[0].shape
    depth = 2 * part
    steps = [w[0].shape[1] // (2 * TILE) for w in (first, second)]
    last = 2 + len(first)

    def kernel(*refs):
        outs, active_ref = refs[-3:-1], refs[-1]

        def fill(weights, gu_ref):
            both = times_pieces(refs[:2], weights)
            gate, up = both[:, :TILE], both[:, TILE:]
            gu_ref[...] = both.astype(bf16)
            active_ref[...] = (gate * (1.0 / (1.0 + jnp.exp(-gate))) * up).astype(bf16)

        pl.when(pl.program_id(0) < steps[0])(lambda: fill(refs[2:last], outs[0]))
        pl.when(pl.program_id(0) >= steps[0])(lambda: fill(refs[last:-3], outs[1]))

    def low(j):
        return jnp.minimum(j, steps[0] - 1)

    def high(j):
        return jnp.maximum(j - steps[0], 0)

    columns = 2 * TILE * sum(steps)
    return pl.pallas_call(
        kernel,
        out_shape=[jax.ShapeDtypeStruct((tokens, 2 * TILE * n), bf16) for n in steps]
        + [jax.ShapeDtypeStruct((tokens, TILE * sum(steps)), bf16)],
        grid=(sum(steps),),
        in_specs=[resident((tokens, part))] * 2
        + [pl.BlockSpec((w.shape[0], 2 * TILE), lambda j: (0, low(j))) for w in first]
        + [pl.BlockSpec((w.shape[0], 2 * TILE), lambda j: (0, high(j))) for w in second],
        out_specs=[
            pl.BlockSpec((tokens, 2 * TILE), lambda j: (0, low(j))),
            pl.BlockSpec((tokens, 2 * TILE), lambda j: (0, high(j))),
            pl.BlockSpec((tokens, TILE), lambda j: (0, j)),
        ],
        compiler_params=params(),
        cost_estimate=cost(4 * tokens * depth * columns, 4 * depth * columns + 4 * tokens * columns, tokens * columns),
        name="gate_up",
    )(*acts, *first, *second)


def swiglu_back(acts, weights, first, second):
    tokens, part = acts[0].shape
    depth = 2 * part
    last = 2 + len(weights)
    steps = [u.shape[1] // (2 * TILE) for u in (first, second)]

    def kernel(*refs):
        d_active = times_pieces(refs[:2], refs[2:last])

        def fill(gu_ref, out_ref):
            gate, up = gu_ref[:, :TILE].astype(f32), gu_ref[:, TILE:].astype(f32)
            sig = 1.0 / (1.0 + jnp.exp(-gate))
            out_ref[:, :TILE] = (d_active * up * sig * (1.0 + gate * (1.0 - sig))).astype(bf16)
            out_ref[:, TILE:] = (d_active * (gate * sig)).astype(bf16)

        pl.when(pl.program_id(0) < steps[0])(lambda: fill(refs[last], refs[-2]))
        pl.when(pl.program_id(0) >= steps[0])(lambda: fill(refs[last + 1], refs[-1]))

    def low(j):
        return jnp.minimum(j, steps[0] - 1)

    def high(j):
        return jnp.maximum(j - steps[0], 0)

    columns = 2 * TILE * sum(steps)
    wide = [
        pl.BlockSpec((tokens, 2 * TILE), lambda j: (0, low(j))),
        pl.BlockSpec((tokens, 2 * TILE), lambda j: (0, high(j))),
    ]
    return pl.pallas_call(
        kernel,
        out_shape=[jax.ShapeDtypeStruct(u.shape, bf16) for u in (first, second)],
        grid=(sum(steps),),
        in_specs=[resident((tokens, part))] * 2 + [pl.BlockSpec((w.shape[0], TILE), lambda j: (0, j)) for w in weights] + wide,
        out_specs=wide,
        compiler_params=params(),
        cost_estimate=cost(4 * tokens * depth * columns, 4 * depth * columns + 4 * tokens * columns, tokens * columns),
        name="swiglu_back",
    )(*acts, *weights, first, second)


def row_specs(own_len, wide):
    mine = pl.BlockSpec((None, None, own_len, wide), lambda s, h: (s, h, 0, 0))
    theirs = pl.BlockSpec((None, None, own_len, wide), lambda s, h: (s, 1 - h, 0, 0))
    return mine, theirs


def load_rows(refs):
    return jnp.concatenate([r[...].astype(f32) for r in refs], axis=-1)


def store_rows(refs, rows):
    half = rows.shape[-1] // 2
    refs[0][...] = rows[:, :half].astype(bf16)
    refs[1][...] = rows[:, half:].astype(bf16)


def middle(resid, partial, received, gain, which, seqs, own_len, before=()):
    width = partial.shape[1]
    half = width // 2

    def kernel(res_low, res_high, par, rec, gain_ref, *refs):
        hid, norm = refs[-4:-2], refs[-2:]
        rows = load_rows([res_low, res_high]) + (par[...].astype(f32) + rec[...].astype(f32))
        factor = lax.rsqrt(jnp.mean(rows * rows, axis=-1, keepdims=True) + epsilon)
        store_rows(hid, rows)
        store_rows(norm, rows * factor * gain_ref[...])

    mine = pl.BlockSpec((None, None, own_len, half), lambda h: (which, h, 0, 0))
    full = pl.BlockSpec((None, None, own_len, width), lambda h: (which, h, 0, 0))
    theirs = pl.BlockSpec((None, own_len, width), lambda h: (1 - h, 0, 0))
    shape = (seqs, 2, own_len, half)
    tokens = seqs * 2 * own_len
    before = [r.reshape(shape) for r in before]
    outs = pl.pallas_call(
        kernel,
        out_shape=[jax.ShapeDtypeStruct(shape, bf16)] * 4,
        grid=(2,),
        in_specs=[mine, mine, full, theirs, pl.BlockSpec((1, width), lambda h: (0, 0))]
        + [pl.BlockSpec(memory_space=pl.ANY)] * len(before),
        out_specs=[mine] * 4,
        input_output_aliases={5 + n: n for n in range(len(before))},
        compiler_params=params(),
        cost_estimate=cost(5 * tokens * width, 5 * tokens * width),
        name="middle",
    )(
        *[r.reshape(shape) for r in resid],
        partial.reshape(seqs, 2, own_len, width),
        received.reshape(2, own_len, width),
        gain,
        *before,
    )
    return tuple(o.reshape(tokens, half) for o in outs)


def middle_back(grad, hidden, partial, received, gain, seqs, own_len):
    tokens, half = grad[0].shape
    width = 2 * half

    def kernel(*refs):
        rows = load_rows(refs[2:4])
        factor = lax.rsqrt(jnp.mean(rows * rows, axis=-1, keepdims=True) + epsilon)
        unit = rows * factor
        scaled = (load_rows(refs[4:6]) + load_rows(refs[6:8])) * refs[8][...]
        spread = jnp.mean(scaled * unit, axis=-1, keepdims=True)
        store_rows(refs[9:11], load_rows(refs[:2]) + factor * (scaled - unit * spread))

    mine, theirs = row_specs(own_len, half)
    shape = (seqs, 2, own_len, half)
    outs = pl.pallas_call(
        kernel,
        out_shape=[jax.ShapeDtypeStruct(shape, bf16)] * 2,
        grid=(seqs, 2),
        in_specs=[mine] * 6 + [theirs] * 2 + [pl.BlockSpec((1, width), lambda s, h: (0, 0))],
        out_specs=[mine] * 2,
        compiler_params=params(2),
        cost_estimate=cost(20 * tokens * width, 10 * tokens * width),
        name="middle_back",
    )(*[r.reshape(shape) for r in (*grad, *hidden, *partial, *received)], gain)
    return tuple(o.reshape(tokens, half) for o in outs)


def leave(slots, residual, partial, received, norm, in_turns=False):
    seqs, own_len, width = received.shape
    half = width // 2
    blocks = slots.shape[0]
    block = width // blocks
    narrow = block % LANES != 0

    def kernel(slots_ref, *refs):
        out_ref = refs[-1]
        total = refs[2][...].astype(f32) + refs[3][...].astype(f32)
        if norm is not None:
            rows = load_rows(refs[4:6])
            factor = lax.rsqrt(jnp.mean(rows * rows, axis=-1, keepdims=True) + epsilon)
            unit = rows * factor
            scaled = total * refs[6][...]
            spread = jnp.mean(scaled * unit, axis=-1, keepdims=True)
            total = factor * (scaled - unit * spread)
        residual_rows = load_rows(refs[:2])
        per = blocks // 2
        for b in range(blocks):
            start = b * block if narrow else pl.multiple_of(slots_ref[b] * block, block)
            at = b // per * per + turned(b % per, per // 2) if in_turns else b
            out = residual_rows[:, b * block : (b + 1) * block] + total[:, at * block : (at + 1) * block]
            out_ref[:, pl.ds(start, block)] = out.astype(bf16)

    mine = pl.BlockSpec((None, None, own_len, half), lambda s, t: (s, 0, 0, 0))
    full = pl.BlockSpec((None, None, own_len, width), lambda s, t: (s, 0, 0, 0))
    whole = pl.BlockSpec((None, own_len, width), lambda s, t: (s, 0, 0))
    arrays = [r.reshape(seqs, 2, own_len, half) for r in residual]
    arrays += [partial.reshape(seqs, 2, own_len, width), received]
    specs = [mine, mine, full, whole]
    if norm is not None:
        arrays += [r.reshape(seqs, 2, own_len, half) for r in norm[0]] + [norm[1]]
        specs += [mine, mine, pl.BlockSpec((1, width), lambda s, t: (0, 0))]
    out = pl.pallas_call(
        kernel,
        out_shape=jax.ShapeDtypeStruct((seqs, own_len, width), bf16),
        grid_spec=pltpu.PrefetchScalarGridSpec(
            num_scalar_prefetch=1, grid=(seqs,), in_specs=specs, out_specs=whole
        ),
        compiler_params=params(),
        cost_estimate=cost(20 * seqs * own_len * width, 12 * seqs * own_len * width),
        name="leave",
    )(slots, *arrays)
    if narrow:
        out = out.reshape(seqs, own_len, blocks, block)[:, :, jnp.argsort(slots)].reshape(seqs, own_len, width)
    return out


def shards(
    inputs,
    block_ids,
    positions,
    w_query,
    key_weight,
    value_weight,
    w_out,
    w_gate,
    w_up,
    w_down,
    attn_gain,
    mlp_gain,
    out_grad,
):
    seqs, own_len, width = inputs.shape
    length = block_ids.shape[1]
    tokens = seqs * length
    side = lax.axis_index("tensor")
    hd = HEAD_SIZE
    heads = w_query.shape[1] // hd
    kv = key_weight.shape[1] // hd
    ff = w_gate.shape[1]
    ring = Ring(lax.axis_size("dp"))
    rows = width // ring.size
    slots = ring.slots(lax.axis_index("dp"))

    def across(value):
        return lax.ppermute(value, "tensor", [(0, 1), (1, 0)])

    def halves(table):
        table = table.reshape(seqs, 2, own_len)
        return jnp.where(side == 0, table, table[:, ::-1]).reshape(seqs, length)

    kv_wide = kv * hd
    blocks = ff // TILE
    cut = (blocks + 1) // 2
    q_cols = heads * hd
    qkv_cols = q_cols + 2 * kv_wide
    out_cols = w_out.shape[0]

    def interleave(pair, first, last):
        parts = [w[:, j * TILE : (j + 1) * TILE] for j in range(first, last) for w in pair]
        return jnp.concatenate(parts, axis=1)

    def other(part):
        return part.reshape(seqs, 2, own_len, width)[:, 1]

    step = -(-blocks // 4)
    bounds = [0, step, cut, cut + step, blocks]
    Q, O, G0, G1, G2, G3, D0, D1 = range(8)
    gates = [G0, G1, G2, G3]
    gain_block = jnp.pad(jnp.stack([attn_gain, mlp_gain], axis=1), ((0, 0), (0, LANES - 2)))
    qkv_shard = jnp.concatenate([w_query, key_weight, value_weight], axis=1)
    columns_1 = cut * TILE
    v = Values()
    v.held, v.got = {}, {}

    def far_send(name):
        v.got[name] = ring.gather_far(v.held[name])

    def grow(name, send, after):
        v.held[name] = joined(tie(v.held[name], *after) if after else v.held[name], v.got[name])
        v.got[name] = send(v.held[name])
        return v.held[name]

    def near_send(name, *after):
        return grow(name, lambda value: ring.along(value, 1), after)

    def pair_send(name, *after):
        return grow(name, ring.pair, after)

    def core_send(name, *after):
        return grow(name, ring.core, after)

    def core_join(name):
        v.held[name] = joined(v.held[name], v.got[name])
        v.got[name] = v.held[name][:LANES]

    def core_send_joined(name):
        v.got[name] = ring.core(v.held[name])

    def whole(name):
        return [v.held[name], v.got[name]]

    v.held[Q] = jnp.concatenate([qkv_shard, gain_block], axis=1)
    v.held[O] = w_out.T
    down = w_down.T
    far_send(Q)
    down_pair = ring.pair(down)
    v.rows = inputs.reshape(seqs, own_len, width)
    v.grad = out_grad.reshape(seqs, own_len, width)
    got_rows = across(v.rows)
    v.down, v.down_pair = down, down_pair
    v.held[G0] = interleave((w_gate, w_up), 0, step)
    v.fence()

    near_send(Q)
    far_send(O)
    segments = halves(tie(block_ids, v.held[Q]))
    seg_row, seg_col = segments[:, None, :], segments[:, :, None]
    steps_half = jnp.arange(hd // 2, dtype=f32)
    frequency = jnp.exp(steps_half * (-2.0 * math.log(rope_base) / hd))
    angles = halves(tie(positions, v.held[Q])).reshape(tokens, 1).astype(f32) * frequency
    cos_head, sin_head = jnp.tile(jnp.cos(angles), (1, 2)), jnp.tile(jnp.sin(angles), (1, 2))
    cosine = jnp.concatenate([jnp.tile(cos_head, (1, TILE // hd + kv)), jnp.ones((tokens, kv_wide), f32)], axis=1)
    sine = jnp.concatenate([jnp.tile(sin_head, (1, TILE // hd + kv)), jnp.zeros((tokens, kv_wide), f32)], axis=1)

    v.tables = [cosine, sine, seg_row, seg_col]
    gate_up_shards = (tie(w_gate, v.held[Q]), tie(w_up, v.held[Q]))
    for name, first, last in zip(gates[1:], bounds[1:-1], bounds[2:]):
        v.held[name] = interleave(gate_up_shards, first, last)
    v.held[D0] = joined(v.down[:, :columns_1], v.down_pair[:, :columns_1])
    v.held[D1] = joined(v.down[:, columns_1:], v.down_pair[:, columns_1:])
    del v.down, v.down_pair
    v.got_rows = got_rows
    v.fence()

    sent = pair_send(Q)
    near_send(O, sent)
    far_send(G0)
    v.far_pair = [ring.gather_far(v.held[D1][:rows])]
    v.got_grad = across(v.grad)
    v.rows = jnp.stack([v.rows, v.got_rows], axis=1).reshape(tokens, width)
    del v.got_rows
    v.fence()

    sent = near_send(G0, pair_send(O))
    far_send(G1)
    core_send(Q, sent)
    both_grad = jnp.stack([v.grad, v.got_grad], axis=1).reshape(tokens, width)
    del v.got_grad
    entered = enter(both_grad, slots, None)
    v.grad, v.grad_turned = tuple(entered[:2]), tuple(entered[2:])
    v.fence()

    near_send(G1, pair_send(G0))
    core_o = [ring.core(v.held[O]), ring.core(v.got[O])]
    v.held[O], v.got[O] = joined(v.held[O], v.got[O]), core_o
    far_send(G2)
    v.attn_gain, v.mlp_gain = gain_rows(whole(Q), qkv_cols)
    entered = enter(v.rows, slots, v.attn_gain)
    del v.rows
    v.resid, v.normed = tuple(entered[:2]), tuple(entered[2:])
    v.qkv = project_qkv(v.normed, whole(Q), v.tables[0], v.tables[1], 0, qkv_cols)
    v.fence()

    near_send(G2, pair_send(G1))
    far_send(G3)
    v.far_pair.append(ring.gather_far(v.held[D1][rows:]))
    v.got[O] = joined(*v.got[O])
    v.context, v.lse = attention_forward(v.qkv, v.tables[2], v.tables[3], seqs, heads, kv)
    v.out_part = project_back([v.context], [whole(O)])
    v.out_got = [v.out_part[w * length : (w + 1) * length] for w in range(seqs)]
    v.fence()

    near_send(G3, pair_send(G2))
    core_join(G0)
    core_join(G1)
    far_send(D0)
    lines = [p.reshape(-1, rows, p.shape[1]) for p in v.far_pair]
    v.got[D1] = jnp.stack(lines, axis=1).reshape(-1, lines[0].shape[2])
    del v.far_pair
    v.out_got[0] = across(v.out_got[0])
    v.fence()

    near_send(D0, pair_send(G3))
    core_send_joined(G0)
    core_send_joined(G1)
    core_join(G2)
    v.middle = middle(v.resid, v.out_part, v.out_got[0], v.mlp_gain, 0, seqs, own_len)
    for w in range(1, seqs):
        v.out_got[w] = across(v.out_got[w])
    v.fence()

    v.far, v.side, v.sums = {}, {}, {}
    v.gu, v.active, v.du = {}, {}, {}
    v.dn, v.got_dn = [None] * 2, [None] * 2
    R = [
        Reduce(ring, v, Q, lambda: v.normed, lambda: v.d_qkv),
        Reduce(ring, v, O, lambda: v.attn_grad, lambda: v.context),
    ]
    for k, name in enumerate(gates):
        R.append(Reduce(ring, v, name, lambda: v.normed_mlp, lambda k=k: v.du[k]))
    for k, name in enumerate([D0, D1]):
        R.append(Reduce(ring, v, name, lambda: v.grad, lambda k=k: v.active[k]))

    def dn_half(which, *after):
        acts = [tie(v.du[0], *after) if after else v.du[0]] + [v.du[k] for k in range(1, 4)]
        v.dn[which] = project_back(acts, [whole(n) for n in gates], None, (which,))

    near_send(D1)
    core_send_joined(G2)
    v.last = [v.held[G3], v.got[G3], ring.core(v.held[G3]), ring.core(v.got[G3])]
    core_send(D0)
    for w in range(1, seqs):
        v.middle = middle(v.resid, v.out_part, v.out_got[w], v.mlp_gain, w, seqs, own_len, v.middle)
    v.hidden, v.normed_mlp = v.middle[:2], v.middle[2:]
    del v.out_part, v.out_got, v.middle
    v.gu[0], v.gu[1], v.active[0] = gate_up(v.normed_mlp, whole(G0), whole(G1))
    R[D0].far()
    v.fence()

    v.last_down = [v.held[D1], v.got[D1], ring.core(v.held[D1]), ring.core(v.got[D1])]
    R[D0].send_far()
    v.gu[2], v.gu[3], v.active[1] = gate_up(v.normed_mlp, whole(G2), v.last)
    v.du[0], v.du[1] = swiglu_back(v.grad_turned, whole(D0), v.gu.pop(0), v.gu.pop(1))
    R[D1].far()
    v.fence()

    sent = R[D0].side()
    R[D0].send_side()
    R[D1].send_far()
    v.du[2], v.du[3] = swiglu_back(
        [tie(v.grad_turned[0], sent), v.grad_turned[1]], v.last_down, v.gu.pop(2), v.gu.pop(3)
    )
    v.held[G3] = joined(tie(v.last[0], sent), v.last[1])
    for name in gates:
        R[name].far()
    v.fence()

    for name in gates[:3]:
        R[name].send_far()
    sent = R[D1].side()
    R[D1].send_side()
    sent = R[D0].near(sent)
    dn_half(0, sent)
    v.got[G3] = joined(tie(v.last[2], sent), v.last[3])
    del v.last
    v.fence()

    v.got_dn[0] = across(v.dn[0])
    R[G3].send_far()
    sent = R[G0].side()
    R[G0].send_side()
    sent = R[D1].near(sent)
    sent = R[D0].fold(sent)
    dn_half(1, sent)
    v.held[D1] = joined(tie(v.last_down[0], sent), v.last_down[1])
    v.got[D1] = joined(tie(v.last_down[2], sent), v.last_down[3])
    del v.last_down
    R[G1].side_ahead(sent)
    v.fence()

    v.got_dn[1] = across(v.dn[1])
    R[G1].send_side()
    sent = R[G0].near()
    sent = R[D1].fold(sent)
    R[D0].rows()
    R[G2].side_ahead(sent)
    R[G3].side_ahead(sent)
    v.mlp_part = project_back([tie(v.active[0], sent), v.active[1]], [whole(D0), whole(D1)])
    v.mlp_other = other(v.mlp_part)
    v.fence()

    R[G2].send_side()
    R[G3].send_side()
    v.attn_grad = middle_back(v.grad, v.hidden, v.dn, v.got_dn, v.mlp_gain, seqs, own_len)
    sent = R[O].far()
    R[O].send_far()
    sent = R[G1].near(sent)
    sent = R[G0].fold(sent)
    R[D1].rows()
    d_context = sum(dot(a, w, 1, 0) for a, w in zip([tie(v.attn_grad[0], sent), v.attn_grad[1]], whole(O))).astype(bf16)
    v.d_qkv = attention_backward(
        v.qkv, d_context, v.lse, v.tables[2], v.tables[3], v.tables[0], v.tables[1], seqs, heads, kv
    )
    R[Q].far()
    v.fence()

    R[Q].send_far()
    v.mlp_got = across(v.mlp_other)
    del v.mlp_other
    sent = R[O].side()
    R[O].send_side()
    sent = R[G2].near(sent)
    sent = R[G1].fold(sent)
    R[G0].rows()
    v.in_part = project_back([tie(v.d_qkv, sent)], [whole(Q)])
    v.in_other = other(v.in_part)
    v.fence()

    v.in_got = across(v.in_other)
    del v.in_other
    sent = R[Q].side()
    R[Q].send_side()
    sent = R[O].near(sent)
    sent = R[G3].near(sent)
    R[G2].fold(sent)
    R[G1].rows()
    v.output = leave(slots, v.hidden, v.mlp_part, v.mlp_got, None, True)
    v.fence()

    sent = R[Q].near()
    sent = R[O].fold(sent)
    R[G3].fold(sent)
    R[G2].rows()
    v.input_grad = leave(slots, v.attn_grad, v.in_part, v.in_got, (v.resid, v.attn_gain))
    v.fence()

    R[Q].fold()
    R[O].rows()
    R[G3].rows()
    v.fence()
    R[Q].rows()

    def pick(which):
        parts = [
            v.sums[gates[k]][:, (2 * j + which) * TILE : (2 * j + which + 1) * TILE]
            for k in range(4)
            for j in range(bounds[k + 1] - bounds[k])
        ]
        return jnp.concatenate(parts, axis=1)

    grad_gate, grad_up, grad_qkv = pick(0), pick(1), v.sums[Q]

    def gain_sum(weights, grads, gain):
        total = sum(jnp.sum(w.astype(f32) * g, axis=1) for w, g in zip(weights, grads))
        return total / gain.astype(f32)

    gain_sums = jnp.stack([
        gain_sum([qkv_shard], [grad_qkv], attn_gain),
        gain_sum([w_gate, w_up], [grad_gate, grad_up], mlp_gain),
    ])
    gain_sums = gain_sums + across(gain_sums)
    return (
        v.output,
        v.input_grad,
        grad_qkv[:, :q_cols],
        grad_qkv[:, q_cols : q_cols + kv_wide],
        grad_qkv[:, q_cols + kv_wide :],
        v.sums[O].T,
        grad_gate,
        grad_up,
        jnp.concatenate([v.sums[D0], v.sums[D1]], axis=1).T,
        gain_sums[0],
        gain_sums[1],
    )


def solution(mesh):
    row, col = P("dp", "tensor"), P("tensor", "dp")
    seq = P("dp", "tensor", None)
    return jax.shard_map(
        shards,
        mesh=mesh,
        in_specs=(seq, P("dp", None), P("dp", None), row, row, row, col, row, row, col, P("dp"), P("dp"), seq),
        out_specs=(seq, seq, row, row, row, col, row, row, col, P("dp"), P("dp")),
        check_vma=False,
    )
```

```python
import functools
import math

import jax
import jax.numpy as jnp
from jax import lax
from jax.experimental import pallas as pl
from jax.experimental.pallas import tpu as pltpu
from jax.sharding import PartitionSpec as P

HEAD_SIZE = 64
LANES = 128
TILE = 256
SHRINK = 10**6
epsilon = 1e-05
rope_base = 10000.0
masked_value = -1e30
bf16 = jnp.bfloat16
f32 = jnp.float32
VMEM_LIMIT = 60 * 1024 * 1024


def dot(left, right, left_dim, right_dim):
    return lax.dot_general(
        left, right, (((left_dim,), (right_dim,)), ((), ())), preferred_element_type=f32
    )


def tie(value, *others):
    return lax.optimization_barrier((value,) + others)[0]


def params(steps=1):
    return pltpu.CompilerParams(
        dimension_semantics=("arbitrary",) * steps, vmem_limit_bytes=VMEM_LIMIT
    )


def resident(shape):
    return pl.BlockSpec(
        shape, lambda *_: (0,) * len(shape), pipeline_mode=pl.Buffered(1)
    )


def cost(flops, moved, trans=0):
    return pl.CostEstimate(flops=flops // SHRINK + 1, bytes_accessed=moved // SHRINK + 1, transcendentals=0)


class Ring:
    def __init__(self, size):
        self.size = size
        self.line = size // 4
        self.reaches = [self.line >> k for k in range(1, self.line.bit_length())]

    def swap(self, value, bits):
        return lax.ppermute(value, "dp", [(i, i ^ bits) for i in range(self.size)])

    def core(self, value):
        return self.swap(value, 1)

    def pair(self, value):
        return self.swap(value, 2)

    def along(self, value, reach):
        return self.swap(value, 4 * reach)

    def slots(self, me):
        order = [0]
        for reach in self.reaches:
            order = order + [o ^ reach for o in order]
        return jnp.stack([me ^ (l * 4 + p * 2 + c) for c in range(2) for p in range(2) for l in order])

    def gather_far(self, shard):
        held = shard
        for reach in self.reaches[:-1]:
            held = jnp.concatenate([held, self.along(held, reach)], axis=0)
        return held[shard.shape[0] :] if self.line > 4 else self.along(shard, 2)


class Values:
    def fence(self):
        fields = vars(self)
        names = sorted(fields)
        fields.update(zip(names, lax.optimization_barrier([fields[n] for n in names])))


def joined(*parts):
    return jnp.concatenate(parts, axis=0)


def weight_grad(act, which, grads, adds, outs):
    tokens, width = act.shape
    columns = grads.shape[1]
    rows = width if which is None else width // 2
    tile = 2 * TILE if columns % (2 * TILE) == 0 else TILE
    at = which or 0

    def kernel(*refs):
        act_ref, grads_ref, turned_ref = refs[0], refs[1], refs[-1]

        @pl.when(pl.program_id(0) == 0)
        def _():
            turned_ref[...] = act_ref[...].astype(f32).T.astype(bf16)

        total = dot(turned_ref[...], grads_ref[...], 1, 0)
        for ref in refs[2 : 2 + len(adds)]:
            total = total + ref[...].astype(f32)
        for n, ref in enumerate(refs[2 + len(adds) : -1]):
            ref[...] = total[n * (rows // outs) : (n + 1) * (rows // outs)].astype(bf16)

    def add_spec(block):
        return pl.BlockSpec((rows, tile), lambda j: (block, j))

    return pl.pallas_call(
        kernel,
        out_shape=[jax.ShapeDtypeStruct((rows // outs, columns), bf16)] * outs,
        grid=(columns // tile,),
        in_specs=[
            pl.BlockSpec((tokens, rows), lambda j: (0, at), pipeline_mode=pl.Buffered(1)),
            pl.BlockSpec((tokens, tile), lambda j: (0, j)),
        ]
        + [add_spec(block) for _, block in adds],
        out_specs=[pl.BlockSpec((rows // outs, tile), lambda j: (0, j))] * outs,
        scratch_shapes=[pltpu.VMEM((rows, tokens), bf16)],
        compiler_params=params(),
        cost_estimate=cost(2 * tokens * rows * columns, 2 * tokens * (rows + columns) + 4 * rows * columns),
        name="weight_grad",
    )(act, grads, *[array for array, _ in adds])


class Reduce:
    def __init__(self, ring, v, name, acts, grads):
        self.ring, self.v, self.name, self.acts, self.grads = ring, v, name, acts, grads

    def part(self, half, which=None, *after):
        act = self.acts()[half]
        if which is not None:
            quarter = act.shape[1] // 2
            act = act[:, which * quarter : (which + 1) * quarter]
        return dot(tie(act, *after) if after else act, self.grads(), 0, 0)

    def far(self, *after):
        self.v.far[self.name] = self.part(1, None, *after).astype(bf16)
        return self.v.far[self.name]

    def send_far(self):
        self.v.far[self.name] = self.ring.core(self.v.far[self.name])

    def side(self, *after):
        far = self.v.far[self.name]
        quarter = far.shape[0] // 2
        out = (self.part(0, 1, *after) + far[quarter:].astype(f32)).astype(bf16)
        self.v.side[self.name] = out
        return out

    def side_ahead(self, *after):
        (out,) = weight_grad(tie(self.acts()[0], *after), 1, self.grads(), [(self.v.far[self.name], 1)], 1)
        self.v.side[self.name] = out
        return out

    def send_side(self):
        self.v.side[self.name] = self.ring.pair(self.v.side[self.name])

    def near(self, *after):
        side = self.v.side[self.name]
        out = self.part(0, 0, *after) + self.v.far[self.name][: side.shape[0]].astype(f32) + side.astype(f32)
        half = out.shape[0] // 2
        send = out[half:].astype(bf16)
        self.v.far[self.name] = out[:half].astype(bf16)
        self.v.side[self.name] = self.ring.along(send, 1)
        return self.v.far[self.name]

    def fold(self, *after):
        terms, reach = [self.v.far[self.name], self.v.side[self.name]], 2
        if after:
            terms[0] = tie(terms[0], *after)
        while True:
            rows = terms[0].shape[0] // 2
            got = self.ring.along(sum(t[rows:].astype(f32) for t in terms).astype(bf16), reach)
            terms, reach = [t[:rows] for t in terms] + [got], reach * 2
            if reach == self.ring.line:
                break
        self.v.far[self.name] = sum(t.astype(f32) for t in terms[:-1])
        self.v.side[self.name] = terms[-1]
        return self.v.far[self.name]

    def rows(self):
        self.v.sums[self.name] = self.v.far.pop(self.name) + self.v.side.pop(self.name).astype(f32)


def turned(block, line):
    return block % line * 2 + block // line


def enter(rows, slots, gain):
    count, width = rows.shape
    blocks = slots.shape[0]
    block = width // blocks
    per = blocks // 2
    half = width // 2
    step = count // 4
    norm = gain is not None
    narrow = block % LANES != 0
    if narrow:
        rows = rows.reshape(count, blocks, block)[:, slots].reshape(count, width)

    def kernel(slots_ref, x_ref, gain_ref, *outs):
        if norm:
            x = x_ref[...].astype(f32)
            factor = lax.rsqrt(jnp.mean(x * x, axis=-1, keepdims=True) + epsilon)
        for b in range(blocks):
            start = b * block if narrow else pl.multiple_of(slots_ref[b] * block, block)
            piece = x_ref[:, pl.ds(start, block)]
            at = slice((b % per) * block, (b % per + 1) * block)
            outs[b // per][:, at] = piece
            if not norm:
                there = turned(b % per, per // 2)
                outs[2 + b // per][:, there * block : (there + 1) * block] = piece
            if norm:
                g = gain_ref[:, b * block : (b + 1) * block]
                outs[2 + b // per][:, at] = (piece.astype(f32) * factor * g).astype(bf16)

    n_out = 4
    if gain is None:
        gain = jnp.ones((1, width), f32)
    return pl.pallas_call(
        kernel,
        out_shape=[jax.ShapeDtypeStruct((count, half), bf16)] * n_out,
        grid_spec=pltpu.PrefetchScalarGridSpec(
            num_scalar_prefetch=1,
            grid=(4,),
            in_specs=[
                pl.BlockSpec((step, width), lambda i, s: (i, 0)),
                pl.BlockSpec((1, width), lambda i, s: (0, 0)),
            ],
            out_specs=[pl.BlockSpec((step, half), lambda i, s: (i, 0))] * n_out,
        ),
        compiler_params=params(),
        cost_estimate=cost(10 * count * width, 2 * count * width * (1 + n_out // 2)),
        name="enter",
    )(slots, rows, gain)


def qkv_kernel(*refs):
    cos_ref, sin_ref, out_ref = refs[4:]
    raw = times_pieces(refs[:2], refs[2:4])
    lane = lax.broadcasted_iota(jnp.int32, raw.shape, 1) % HEAD_SIZE
    half = HEAD_SIZE // 2
    ahead = pltpu.roll(raw, raw.shape[1] - half, 1)
    behind = pltpu.roll(raw, half, 1)
    turned = jnp.where(lane < half, -ahead, behind)
    out_ref[...] = (raw * cos_ref[...] + turned * sin_ref[...]).astype(bf16)


def project_qkv(acts, weights, cosine, sine, first, columns):
    tokens, part = acts[0].shape
    steps = columns // TILE
    table = pl.BlockSpec((tokens, TILE), lambda j: (0, j // (steps - 1)))
    depth = weights[0].shape[0]
    return pl.pallas_call(
        qkv_kernel,
        out_shape=jax.ShapeDtypeStruct((tokens, columns), bf16),
        grid=(steps,),
        in_specs=[resident((tokens, part))] * 2
        + [pl.BlockSpec((depth, TILE), lambda j: (0, first + j))] * 2
        + [table, table],
        out_specs=pl.BlockSpec((tokens, TILE), lambda j: (0, j)),
        compiler_params=params(),
        cost_estimate=cost(8 * tokens * depth * columns, 8 * depth * columns + 4 * tokens * part),
        name="project_qkv",
    )(*acts, *weights, cosine, sine)


def times_pieces(acts, weights):
    per, rows = len(weights) // 2, weights[0].shape[0]
    return sum(dot(acts[i // per][:, i % per * rows : (i % per + 1) * rows], w[...], 1, 0) for i, w in enumerate(weights))


def project_kernel(*refs):
    refs[4][...] = times_pieces(refs[:2], refs[2:4]).astype(bf16)


def project(acts, weights, columns):
    tokens, part = acts[0].shape
    depth = weights[0].shape[0]
    return pl.pallas_call(
        project_kernel,
        out_shape=jax.ShapeDtypeStruct((tokens, columns), bf16),
        grid=(columns // TILE,),
        in_specs=[resident((tokens, part))] * 2 + [pl.BlockSpec((depth, TILE), lambda j: (0, j))] * 2,
        out_specs=pl.BlockSpec((tokens, TILE), lambda j: (0, j)),
        compiler_params=params(),
        cost_estimate=cost(8 * tokens * depth * columns, 8 * depth * columns + 4 * tokens * part),
        name="project",
    )(*acts, *weights)


def project_back(acts, weights, firsts=None, halves=(0, 1)):
    tokens = acts[0].shape[0]
    depth = weights[0][0].shape[0]
    steps = depth // TILE
    count = len(acts)
    firsts = firsts or [0] * count
    wides = [a.shape[1] if not f else math.gcd(a.shape[1], f) for a, f in zip(acts, firsts)]
    parts = [(n, f // w + j, w, j) for n, (a, f, w) in enumerate(zip(acts, firsts, wides)) for j in range(a.shape[1] // w)]
    total = len(parts)

    def kernel(*refs):
        acts_in, out_ref = refs[:count], refs[-1]
        for p in range(len(halves)):
            pieces = refs[count + p * total : count + (p + 1) * total]

            @pl.when(pl.program_id(0) // steps == p)
            def _():
                out_ref[...] = sum(
                    dot(acts_in[n][:, j * w : (j + 1) * w], piece[...], 1, 1)
                    for (n, _, w, j), piece in zip(parts, pieces)
                ).astype(bf16)

    def spec(p, block, wide):
        return pl.BlockSpec((TILE, wide), lambda i: (jnp.clip(i - p * steps, 0, steps - 1), block))

    columns = sum(a.shape[1] for a in acts)
    return pl.pallas_call(
        kernel,
        out_shape=jax.ShapeDtypeStruct((tokens, len(halves) * depth), bf16),
        grid=(len(halves) * steps,),
        in_specs=[
            resident(a.shape) for a in acts
        ]
        + [spec(p, block, w) for p in range(len(halves)) for _, block, w, _ in parts],
        out_specs=pl.BlockSpec((tokens, TILE), lambda i: (0, i)),
        compiler_params=params(),
        cost_estimate=cost(8 * tokens * depth * columns, (8 * depth + 2 * tokens) * columns),
        name="project_back",
    )(*acts, *[weights[n][p] for p in halves for n, _, _, _ in parts])


def gain_rows(pieces, first):
    depth = pieces[0].shape[0]

    def kernel(*refs):
        for p in range(2):
            refs[2][:, p * depth : (p + 1) * depth] = refs[p][...].astype(f32).T[:8]

    out = pl.pallas_call(
        kernel,
        out_shape=jax.ShapeDtypeStruct((8, 2 * depth), f32),
        grid=(1,),
        in_specs=[pl.BlockSpec((depth, LANES), lambda i: (0, first // LANES))] * 2,
        out_specs=pl.BlockSpec((8, 2 * depth), lambda i: (0, 0)),
        compiler_params=params(),
        name="gain_rows",
    )(*pieces)
    return out[:1], out[1:2]


def forward_kernel(q_ref, kv_ref, seg_row, seg_col, ctx_ref, lse_ref):
    kv_heads = kv_ref.shape[1] // (2 * HEAD_SIZE)
    group = pl.program_id(0)
    keys = kv_ref[:, : kv_heads * HEAD_SIZE].astype(f32)
    values = kv_ref[:, kv_heads * HEAD_SIZE :].astype(f32)
    lane = lax.broadcasted_iota(jnp.int32, keys.shape, 1)
    low = lane < HEAD_SIZE
    here = low == (group == 0)
    both_keys = jnp.where(here, keys, pltpu.roll(keys, HEAD_SIZE, 1)).astype(bf16)
    both_values = jnp.where(here, values, pltpu.roll(values, HEAD_SIZE, 1)).astype(bf16)
    none = jnp.zeros_like(both_values)
    value_low = jnp.where(low, both_values, none)
    value_high = jnp.where(low, none, both_values)
    allowed = seg_row[...] <= seg_col[...]
    pairs = q_ref.shape[1] // (2 * HEAD_SIZE)
    for pair in range(pairs):
        cut = slice(pair * LANES, (pair + 1) * LANES)
        q = q_ref[:, cut] * bf16(HEAD_SIZE ** (-0.5))
        total = None
        for side, values_here in ((0, value_low), (1, value_high)):
            mine = jnp.where(low, q, none) if side == 0 else jnp.where(low, none, q)
            scores = jnp.where(allowed, dot(mine, both_keys, 1, 1), masked_value)
            top = jnp.max(scores, axis=-1, keepdims=True)
            weights = jnp.exp(scores - top)
            mass = jnp.sum(weights, axis=-1, keepdims=True)
            probs = (weights * (1.0 / mass)).astype(bf16)
            part = dot(probs, values_here, 1, 0)
            total = part if total is None else total + part
            lse_ref[:, 2 * pair + side : 2 * pair + side + 1] = top + jnp.log(mass)
        ctx_ref[:, cut] = total.astype(bf16)


def attention_forward(qkv, seg_row, seg_col, seqs, heads, kv, which, before=()):
    tokens = qkv.shape[0]
    length = tokens // seqs
    wide = heads // kv * HEAD_SIZE
    last = heads * HEAD_SIZE // (2 * kv * HEAD_SIZE)

    def kernel(*refs):
        forward_kernel(*refs[:4], *refs[-2:])

    return pl.pallas_call(
        kernel,
        out_shape=[
            jax.ShapeDtypeStruct((tokens, heads * HEAD_SIZE), bf16),
            jax.ShapeDtypeStruct((kv, tokens, heads // kv), f32),
        ],
        grid=(kv,),
        in_specs=[
            pl.BlockSpec((length, wide), lambda g: (which, g)),
            pl.BlockSpec((length, 2 * kv * HEAD_SIZE), lambda g: (which, last)),
            pl.BlockSpec((None, 1, length), lambda g: (which, 0, 0)),
            pl.BlockSpec((None, length, 1), lambda g: (which, 0, 0)),
        ]
        + [pl.BlockSpec(memory_space=pl.ANY)] * len(before),
        out_specs=[
            pl.BlockSpec((length, wide), lambda g: (which, g)),
            pl.BlockSpec((None, length, heads // kv), lambda g: (g, which, 0)),
        ],
        input_output_aliases={4 + n: n for n in range(len(before))},
        compiler_params=params(),
        cost_estimate=cost(16 * length * length * heads * HEAD_SIZE, 6 * length * heads * HEAD_SIZE),
        name="attention_forward",
    )(qkv, qkv, seg_row, seg_col, *before)


def backward_kernel(q_ref, kv_ref, dctx_ref, lse_ref, seg_row, seg_col, cos_ref, sin_ref, out_ref):
    kv_heads = kv_ref.shape[1] // (2 * HEAD_SIZE)
    group = pl.program_id(1)
    wide = q_ref.shape[1]
    q_cols = kv_heads * wide
    scale = HEAD_SIZE ** (-0.5)
    half = HEAD_SIZE // 2
    keys = kv_ref[:, : kv_heads * HEAD_SIZE].astype(f32)
    values = kv_ref[:, kv_heads * HEAD_SIZE :].astype(f32)
    lane = lax.broadcasted_iota(jnp.int32, keys.shape, 1)
    low = lane < HEAD_SIZE
    here = low == (group == 0)
    both_keys = jnp.where(here, keys, pltpu.roll(keys, HEAD_SIZE, 1)).astype(bf16)
    both_values = jnp.where(here, values, pltpu.roll(values, HEAD_SIZE, 1)).astype(bf16)
    none = jnp.zeros_like(both_keys)
    key_low = jnp.where(low, both_keys, none)
    key_high = jnp.where(low, none, both_keys)
    allowed = seg_row[...] <= seg_col[...]
    cosine, sine = cos_ref[...], sin_ref[...]

    def unrotate(rows):
        turned = rows * sine
        ahead = pltpu.roll(turned, LANES - half, 1)
        behind = pltpu.roll(turned, half, 1)
        return rows * cosine + jnp.where(lane % HEAD_SIZE < half, ahead, -behind)

    dkey = jnp.zeros(keys.shape, f32)
    dvalue = jnp.zeros(keys.shape, f32)
    pairs = q_ref.shape[1] // LANES
    for pair in range(pairs):
        cut = slice(pair * LANES, (pair + 1) * LANES)
        q = q_ref[:, cut] * bf16(scale)
        dctx = dctx_ref[:, cut]
        dquery = None
        for side, keys_here in ((0, key_low), (1, key_high)):
            mine = jnp.where(low, q, none) if side == 0 else jnp.where(low, none, q)
            dmine = jnp.where(low, dctx, none) if side == 0 else jnp.where(low, none, dctx)
            scores = jnp.where(allowed, dot(mine, both_keys, 1, 1), masked_value)
            probs = jnp.exp(scores - lse_ref[:, 2 * pair + side : 2 * pair + side + 1])
            dprobs = dot(dmine, both_values, 1, 1)
            delta = jnp.sum(probs * dprobs, axis=-1, keepdims=True)
            dscores = (probs * (dprobs - delta)).astype(bf16)
            part = dot(dscores, keys_here, 1, 0)
            dquery = part if dquery is None else dquery + part
            dkey = dkey + dot(dscores, mine, 0, 0)
            dvalue = dvalue + dot(probs.astype(bf16), dmine, 0, 0)
        start = pl.multiple_of(group * wide + pair * LANES, LANES)
        out_ref[:, pl.ds(start, LANES)] = unrotate(dquery * scale).astype(bf16)
    dkey = unrotate(dkey + pltpu.roll(dkey, HEAD_SIZE, 1)).astype(bf16)
    dvalue = (dvalue + pltpu.roll(dvalue, HEAD_SIZE, 1)).astype(bf16)

    key_cut, value_cut = slice(q_cols, q_cols + LANES), slice(q_cols + LANES, q_cols + 2 * LANES)

    @pl.when(group == 0)
    def _():
        out_ref[:, key_cut] = dkey
        out_ref[:, value_cut] = dvalue

    @pl.when(group == 1)
    def _():
        out_ref[:, key_cut] = jnp.where(low, out_ref[:, key_cut], dkey)
        out_ref[:, value_cut] = jnp.where(low, out_ref[:, value_cut], dvalue)


def attention_backward(qkv, dctx, lse, seg_row, seg_col, cosine, sine, seqs, heads, kv):
    tokens, columns = qkv.shape
    length = tokens // seqs
    wide = heads // kv * HEAD_SIZE
    last = heads * HEAD_SIZE // (2 * kv * HEAD_SIZE)
    table = pl.BlockSpec((length, LANES), lambda s, g: (s, 0))
    return pl.pallas_call(
        backward_kernel,
        out_shape=jax.ShapeDtypeStruct((tokens, columns), bf16),
        grid=(seqs, kv),
        in_specs=[
            pl.BlockSpec((length, wide), lambda s, g: (s, g)),
            pl.BlockSpec((length, 2 * kv * HEAD_SIZE), lambda s, g: (s, last)),
            pl.BlockSpec((length, wide), lambda s, g: (s, g)),
            pl.BlockSpec((None, length, heads // kv), lambda s, g: (g, s, 0)),
            pl.BlockSpec((None, 1, length), lambda s, g: (s, 0, 0)),
            pl.BlockSpec((None, length, 1), lambda s, g: (s, 0, 0)),
            table,
            table,
        ],
        out_specs=pl.BlockSpec((length, columns), lambda s, g: (s, 0)),
        compiler_params=params(2),
        cost_estimate=cost(40 * tokens * length * heads * HEAD_SIZE, 10 * tokens * heads * HEAD_SIZE),
        name="attention_backward",
    )(qkv, qkv, dctx, lse, seg_row, seg_col, cosine, sine)


def gate_up(acts, first, second):
    tokens, part = acts[0].shape
    depth = 2 * part
    steps = [w[0].shape[1] // (2 * TILE) for w in (first, second)]
    last = 2 + len(first)

    def kernel(*refs):
        outs, active_ref = refs[-3:-1], refs[-1]

        def fill(weights, gu_ref):
            both = times_pieces(refs[:2], weights)
            gate, up = both[:, :TILE], both[:, TILE:]
            gu_ref[...] = both.astype(bf16)
            active_ref[...] = (gate * (1.0 / (1.0 + jnp.exp(-gate))) * up).astype(bf16)

        pl.when(pl.program_id(0) < steps[0])(lambda: fill(refs[2:last], outs[0]))
        pl.when(pl.program_id(0) >= steps[0])(lambda: fill(refs[last:-3], outs[1]))

    def low(j):
        return jnp.minimum(j, steps[0] - 1)

    def high(j):
        return jnp.maximum(j - steps[0], 0)

    columns = 2 * TILE * sum(steps)
    return pl.pallas_call(
        kernel,
        out_shape=[jax.ShapeDtypeStruct((tokens, 2 * TILE * n), bf16) for n in steps]
        + [jax.ShapeDtypeStruct((tokens, TILE * sum(steps)), bf16)],
        grid=(sum(steps),),
        in_specs=[resident((tokens, part))] * 2
        + [pl.BlockSpec((w.shape[0], 2 * TILE), lambda j: (0, low(j))) for w in first]
        + [pl.BlockSpec((w.shape[0], 2 * TILE), lambda j: (0, high(j))) for w in second],
        out_specs=[
            pl.BlockSpec((tokens, 2 * TILE), lambda j: (0, low(j))),
            pl.BlockSpec((tokens, 2 * TILE), lambda j: (0, high(j))),
            pl.BlockSpec((tokens, TILE), lambda j: (0, j)),
        ],
        compiler_params=params(),
        cost_estimate=cost(4 * tokens * depth * columns, 4 * depth * columns + 4 * tokens * columns, tokens * columns),
        name="gate_up",
    )(*acts, *first, *second)


def swiglu_back(acts, weights, first, second):
    tokens, part = acts[0].shape
    depth = 2 * part
    last = 2 + len(weights)
    steps = [u.shape[1] // (2 * TILE) for u in (first, second)]

    def kernel(*refs):
        d_active = times_pieces(refs[:2], refs[2:last])

        def fill(gu_ref, out_ref):
            gate, up = gu_ref[:, :TILE].astype(f32), gu_ref[:, TILE:].astype(f32)
            sig = 1.0 / (1.0 + jnp.exp(-gate))
            out_ref[:, :TILE] = (d_active * up * sig * (1.0 + gate * (1.0 - sig))).astype(bf16)
            out_ref[:, TILE:] = (d_active * (gate * sig)).astype(bf16)

        pl.when(pl.program_id(0) < steps[0])(lambda: fill(refs[last], refs[-2]))
        pl.when(pl.program_id(0) >= steps[0])(lambda: fill(refs[last + 1], refs[-1]))

    def low(j):
        return jnp.minimum(j, steps[0] - 1)

    def high(j):
        return jnp.maximum(j - steps[0], 0)

    columns = 2 * TILE * sum(steps)
    wide = [
        pl.BlockSpec((tokens, 2 * TILE), lambda j: (0, low(j))),
        pl.BlockSpec((tokens, 2 * TILE), lambda j: (0, high(j))),
    ]
    return pl.pallas_call(
        kernel,
        out_shape=[jax.ShapeDtypeStruct(u.shape, bf16) for u in (first, second)],
        grid=(sum(steps),),
        in_specs=[resident((tokens, part))] * 2 + [pl.BlockSpec((w.shape[0], TILE), lambda j: (0, j)) for w in weights] + wide,
        out_specs=wide,
        compiler_params=params(),
        cost_estimate=cost(4 * tokens * depth * columns, 4 * depth * columns + 4 * tokens * columns, tokens * columns),
        name="swiglu_back",
    )(*acts, *weights, first, second)


def row_specs(own_len, wide):
    mine = pl.BlockSpec((None, None, own_len, wide), lambda s, h: (s, h, 0, 0))
    theirs = pl.BlockSpec((None, None, own_len, wide), lambda s, h: (s, 1 - h, 0, 0))
    return mine, theirs


def load_rows(refs):
    return jnp.concatenate([r[...].astype(f32) for r in refs], axis=-1)


def store_rows(refs, rows):
    half = rows.shape[-1] // 2
    refs[0][...] = rows[:, :half].astype(bf16)
    refs[1][...] = rows[:, half:].astype(bf16)


def middle(resid, partial, received, gain, which, seqs, own_len, before=()):
    width = partial.shape[1]
    half = width // 2

    def kernel(res_low, res_high, par, rec, gain_ref, *refs):
        hid, norm = refs[-4:-2], refs[-2:]
        rows = load_rows([res_low, res_high]) + (par[...].astype(f32) + rec[...].astype(f32))
        factor = lax.rsqrt(jnp.mean(rows * rows, axis=-1, keepdims=True) + epsilon)
        store_rows(hid, rows)
        store_rows(norm, rows * factor * gain_ref[...])

    mine = pl.BlockSpec((None, None, own_len, half), lambda h: (which, h, 0, 0))
    full = pl.BlockSpec((None, None, own_len, width), lambda h: (which, h, 0, 0))
    theirs = pl.BlockSpec((None, own_len, width), lambda h: (1 - h, 0, 0))
    shape = (seqs, 2, own_len, half)
    tokens = seqs * 2 * own_len
    before = [r.reshape(shape) for r in before]
    outs = pl.pallas_call(
        kernel,
        out_shape=[jax.ShapeDtypeStruct(shape, bf16)] * 4,
        grid=(2,),
        in_specs=[mine, mine, full, theirs, pl.BlockSpec((1, width), lambda h: (0, 0))]
        + [pl.BlockSpec(memory_space=pl.ANY)] * len(before),
        out_specs=[mine] * 4,
        input_output_aliases={5 + n: n for n in range(len(before))},
        compiler_params=params(),
        cost_estimate=cost(5 * tokens * width, 5 * tokens * width),
        name="middle",
    )(
        *[r.reshape(shape) for r in resid],
        partial.reshape(seqs, 2, own_len, width),
        received.reshape(2, own_len, width),
        gain,
        *before,
    )
    return tuple(o.reshape(tokens, half) for o in outs)


def middle_back(grad, hidden, partial, received, gain, seqs, own_len):
    tokens, half = grad[0].shape
    width = 2 * half

    def kernel(*refs):
        rows = load_rows(refs[2:4])
        factor = lax.rsqrt(jnp.mean(rows * rows, axis=-1, keepdims=True) + epsilon)
        unit = rows * factor
        scaled = (load_rows(refs[4:6]) + load_rows(refs[6:8])) * refs[8][...]
        spread = jnp.mean(scaled * unit, axis=-1, keepdims=True)
        store_rows(refs[9:11], load_rows(refs[:2]) + factor * (scaled - unit * spread))

    mine, theirs = row_specs(own_len, half)
    shape = (seqs, 2, own_len, half)
    outs = pl.pallas_call(
        kernel,
        out_shape=[jax.ShapeDtypeStruct(shape, bf16)] * 2,
        grid=(seqs, 2),
        in_specs=[mine] * 6 + [theirs] * 2 + [pl.BlockSpec((1, width), lambda s, h: (0, 0))],
        out_specs=[mine] * 2,
        compiler_params=params(2),
        cost_estimate=cost(20 * tokens * width, 10 * tokens * width),
        name="middle_back",
    )(*[r.reshape(shape) for r in (*grad, *hidden, *partial, *received)], gain)
    return tuple(o.reshape(tokens, half) for o in outs)


def leave(slots, residual, partial, received, norm, in_turns=False):
    seqs, own_len, width = received.shape
    half = width // 2
    blocks = slots.shape[0]
    block = width // blocks
    narrow = block % LANES != 0

    def kernel(slots_ref, *refs):
        out_ref = refs[-1]
        total = refs[2][...].astype(f32) + refs[3][...].astype(f32)
        if norm is not None:
            rows = load_rows(refs[4:6])
            factor = lax.rsqrt(jnp.mean(rows * rows, axis=-1, keepdims=True) + epsilon)
            unit = rows * factor
            scaled = total * refs[6][...]
            spread = jnp.mean(scaled * unit, axis=-1, keepdims=True)
            total = factor * (scaled - unit * spread)
        residual_rows = load_rows(refs[:2])
        per = blocks // 2
        for b in range(blocks):
            start = b * block if narrow else pl.multiple_of(slots_ref[b] * block, block)
            at = b // per * per + turned(b % per, per // 2) if in_turns else b
            out = residual_rows[:, b * block : (b + 1) * block] + total[:, at * block : (at + 1) * block]
            out_ref[:, pl.ds(start, block)] = out.astype(bf16)

    mine = pl.BlockSpec((None, None, own_len, half), lambda s, t: (s, 0, 0, 0))
    full = pl.BlockSpec((None, None, own_len, width), lambda s, t: (s, 0, 0, 0))
    whole = pl.BlockSpec((None, own_len, width), lambda s, t: (s, 0, 0))
    arrays = [r.reshape(seqs, 2, own_len, half) for r in residual]
    arrays += [partial.reshape(seqs, 2, own_len, width), received]
    specs = [mine, mine, full, whole]
    if norm is not None:
        arrays += [r.reshape(seqs, 2, own_len, half) for r in norm[0]] + [norm[1]]
        specs += [mine, mine, pl.BlockSpec((1, width), lambda s, t: (0, 0))]
    out = pl.pallas_call(
        kernel,
        out_shape=jax.ShapeDtypeStruct((seqs, own_len, width), bf16),
        grid_spec=pltpu.PrefetchScalarGridSpec(
            num_scalar_prefetch=1, grid=(seqs,), in_specs=specs, out_specs=whole
        ),
        compiler_params=params(),
        cost_estimate=cost(20 * seqs * own_len * width, 12 * seqs * own_len * width),
        name="leave",
    )(slots, *arrays)
    if narrow:
        out = out.reshape(seqs, own_len, blocks, block)[:, :, jnp.argsort(slots)].reshape(seqs, own_len, width)
    return out


def shards(
    inputs,
    block_ids,
    positions,
    w_query,
    key_weight,
    value_weight,
    w_out,
    w_gate,
    w_up,
    w_down,
    attn_gain,
    mlp_gain,
    out_grad,
):
    seqs, own_len, width = inputs.shape
    length = block_ids.shape[1]
    tokens = seqs * length
    side = lax.axis_index("tensor")
    hd = HEAD_SIZE
    heads = w_query.shape[1] // hd
    kv = key_weight.shape[1] // hd
    ff = w_gate.shape[1]
    ring = Ring(lax.axis_size("dp"))
    rows = width // ring.size
    slots = ring.slots(lax.axis_index("dp"))

    def across(value):
        return lax.ppermute(value, "tensor", [(0, 1), (1, 0)])

    def halves(table):
        table = table.reshape(seqs, 2, own_len)
        return jnp.where(side == 0, table, table[:, ::-1]).reshape(seqs, length)

    kv_wide = kv * hd
    blocks = ff // TILE
    cut = (blocks + 1) // 2
    q_cols = heads * hd
    qkv_cols = q_cols + 2 * kv_wide
    out_cols = w_out.shape[0]

    def interleave(pair, first, last):
        parts = [w[:, j * TILE : (j + 1) * TILE] for j in range(first, last) for w in pair]
        return jnp.concatenate(parts, axis=1)

    def other(part):
        return part.reshape(seqs, 2, own_len, width)[:, 1]

    step = -(-blocks // 4)
    bounds = [0, step, cut, cut + step, blocks]
    Q, O, G0, G1, G2, G3, D0, D1 = range(8)
    gates = [G0, G1, G2, G3]
    gain_block = jnp.pad(jnp.stack([attn_gain, mlp_gain], axis=1), ((0, 0), (0, LANES - 2)))
    qkv_shard = jnp.concatenate([w_query, key_weight, value_weight], axis=1)
    columns_1 = cut * TILE
    v = Values()
    v.held, v.got = {}, {}

    def far_send(name):
        v.got[name] = ring.gather_far(v.held[name])

    def grow(name, send, after):
        v.held[name] = joined(tie(v.held[name], *after) if after else v.held[name], v.got[name])
        v.got[name] = send(v.held[name])
        return v.held[name]

    def near_send(name, *after):
        return grow(name, lambda value: ring.along(value, 1), after)

    def pair_send(name, *after):
        return grow(name, ring.pair, after)

    def core_send(name, *after):
        return grow(name, ring.core, after)

    def core_join(name):
        v.held[name] = joined(v.held[name], v.got[name])
        v.got[name] = v.held[name][:LANES]

    def core_send_joined(name):
        v.got[name] = ring.core(v.held[name])

    def whole(name):
        return [v.held[name], v.got[name]]

    v.held[Q] = jnp.concatenate([qkv_shard, gain_block], axis=1)
    v.held[O] = w_out.T
    down = w_down.T
    far_send(Q)
    v.rows = inputs.reshape(seqs, own_len, width)
    v.grad = out_grad.reshape(seqs, own_len, width)
    got_rows = across(v.rows)
    v.down = down
    v.fence()

    near_send(Q)
    far_send(O)
    v.down_pair = ring.pair(v.down)
    segments = halves(tie(block_ids, v.held[Q]))
    seg_row, seg_col = segments[:, None, :], segments[:, :, None]
    steps_half = jnp.arange(hd // 2, dtype=f32)
    frequency = jnp.exp(steps_half * (-2.0 * math.log(rope_base) / hd))
    angles = halves(tie(positions, v.held[Q])).reshape(tokens, 1).astype(f32) * frequency
    cos_head, sin_head = jnp.tile(jnp.cos(angles), (1, 2)), jnp.tile(jnp.sin(angles), (1, 2))
    cosine = jnp.concatenate([jnp.tile(cos_head, (1, TILE // hd + kv)), jnp.ones((tokens, kv_wide), f32)], axis=1)
    sine = jnp.concatenate([jnp.tile(sin_head, (1, TILE // hd + kv)), jnp.zeros((tokens, kv_wide), f32)], axis=1)

    v.tables = [cosine, sine, seg_row, seg_col]
    gate_up_shards = (tie(w_gate, v.held[Q]), tie(w_up, v.held[Q]))
    for name, first, last in zip(gates, bounds[:-1], bounds[1:]):
        v.held[name] = interleave(gate_up_shards, first, last)
    v.down_1, v.down_2 = v.down[:, :columns_1], v.down[:, columns_1:]
    del v.down
    v.got_rows = got_rows
    v.fence()

    sent = pair_send(Q)
    near_send(O, sent)
    far_send(G0)
    v.far_pair = [ring.gather_far(v.down_2)]
    v.held[D0] = joined(v.down_1, v.down_pair[:, :columns_1])
    v.held[D1] = joined(v.down_2, v.down_pair[:, columns_1:])
    del v.down_1, v.down_2, v.down_pair
    v.got_grad = across(v.grad)
    v.rows = jnp.stack([v.rows, v.got_rows], axis=1).reshape(tokens, width)
    del v.got_rows
    v.fence()

    sent = near_send(G0, pair_send(O))
    far_send(G1)
    core_send(Q, sent)
    both_grad = jnp.stack([v.grad, v.got_grad], axis=1).reshape(tokens, width)
    del v.got_grad
    entered = enter(both_grad, slots, None)
    v.grad, v.grad_turned = tuple(entered[:2]), tuple(entered[2:])
    v.fence()

    near_send(G1, pair_send(G0))
    core_o = [ring.core(v.held[O]), ring.core(v.got[O])]
    v.held[O], v.got[O] = joined(v.held[O], v.got[O]), core_o
    far_send(G2)
    v.attn_gain, v.mlp_gain = gain_rows(whole(Q), qkv_cols)
    entered = enter(v.rows, slots, v.attn_gain)
    del v.rows
    v.resid, v.normed = tuple(entered[:2]), tuple(entered[2:])
    v.qkv = project_qkv(v.normed, whole(Q), v.tables[0], v.tables[1], 0, qkv_cols)
    v.attended = attention_forward(v.qkv, v.tables[2], v.tables[3], seqs, heads, kv, 0)
    v.fence()

    near_send(G2, pair_send(G1))
    far_send(G3)
    v.far_pair.append(ring.gather_far(v.held[D1][rows:]))
    v.got[O] = joined(*v.got[O])
    for w in range(1, seqs):
        v.attended = attention_forward(v.qkv, v.tables[2], v.tables[3], seqs, heads, kv, w, v.attended)
    v.context, v.lse = v.attended
    del v.attended
    v.out_part = project_back([v.context], [whole(O)])
    v.out_got = [v.out_part[w * length : (w + 1) * length] for w in range(seqs)]
    v.fence()

    near_send(G3, pair_send(G2))
    core_join(G0)
    core_join(G1)
    far_send(D0)
    lines = [p.reshape(-1, rows, p.shape[1]) for p in v.far_pair]
    v.got[D1] = jnp.stack(lines, axis=1).reshape(-1, lines[0].shape[2])
    del v.far_pair
    v.out_got[0] = across(v.out_got[0])
    v.fence()

    near_send(D0, pair_send(G3))
    core_send_joined(G0)
    core_send_joined(G1)
    core_join(G2)
    v.middle = middle(v.resid, v.out_part, v.out_got[0], v.mlp_gain, 0, seqs, own_len)
    for w in range(1, seqs):
        v.out_got[w] = across(v.out_got[w])
    v.fence()

    v.far, v.side, v.sums = {}, {}, {}
    v.gu, v.active, v.du = {}, {}, {}
    v.dn, v.got_dn = [None] * 2, [None] * 2
    R = [
        Reduce(ring, v, Q, lambda: v.normed, lambda: v.d_qkv),
        Reduce(ring, v, O, lambda: v.attn_grad, lambda: v.context),
    ]
    for k, name in enumerate(gates):
        R.append(Reduce(ring, v, name, lambda: v.normed_mlp, lambda k=k: v.du[k]))
    for k, name in enumerate([D0, D1]):
        R.append(Reduce(ring, v, name, lambda: v.grad, lambda k=k: v.active[k]))

    def dn_half(which, *after):
        acts = [tie(v.du[0], *after) if after else v.du[0]] + [v.du[k] for k in range(1, 4)]
        v.dn[which] = project_back(acts, [whole(n) for n in gates], None, (which,))

    near_send(D1)
    core_send_joined(G2)
    v.last = [v.held[G3], v.got[G3], ring.core(v.held[G3]), ring.core(v.got[G3])]
    core_send(D0)
    for w in range(1, seqs):
        v.middle = middle(v.resid, v.out_part, v.out_got[w], v.mlp_gain, w, seqs, own_len, v.middle)
    v.hidden, v.normed_mlp = v.middle[:2], v.middle[2:]
    del v.out_part, v.out_got, v.middle
    v.gu[0], v.gu[1], v.active[0] = gate_up(v.normed_mlp, whole(G0), whole(G1))
    R[D0].far()
    v.fence()

    v.last_down = [v.held[D1], v.got[D1], ring.core(v.held[D1]), ring.core(v.got[D1])]
    R[D0].send_far()
    v.gu[2], v.gu[3], v.active[1] = gate_up(v.normed_mlp, whole(G2), v.last)
    v.du[0], v.du[1] = swiglu_back(v.grad_turned, whole(D0), v.gu.pop(0), v.gu.pop(1))
    R[D1].far()
    v.fence()

    sent = R[D0].side()
    R[D0].send_side()
    R[D1].send_far()
    v.du[2], v.du[3] = swiglu_back(
        [tie(v.grad_turned[0], sent), v.grad_turned[1]], v.last_down, v.gu.pop(2), v.gu.pop(3)
    )
    v.held[G3] = joined(tie(v.last[0], sent), v.last[1])
    for name in gates:
        R[name].far()
    v.fence()

    for name in gates[:3]:
        R[name].send_far()
    sent = R[D1].side()
    R[D1].send_side()
    sent = R[D0].near(sent)
    dn_half(0, sent)
    v.got[G3] = joined(tie(v.last[2], sent), v.last[3])
    del v.last
    v.fence()

    v.got_dn[0] = across(v.dn[0])
    R[G3].send_far()
    sent = R[G0].side()
    R[G0].send_side()
    sent = R[D1].near(sent)
    sent = R[D0].fold(sent)
    dn_half(1, sent)
    v.held[D1] = joined(tie(v.last_down[0], sent), v.last_down[1])
    v.got[D1] = joined(tie(v.last_down[2], sent), v.last_down[3])
    del v.last_down
    R[G1].side_ahead(sent)
    v.fence()

    v.got_dn[1] = across(v.dn[1])
    R[G1].send_side()
    sent = R[G0].near()
    sent = R[D1].fold(sent)
    R[D0].rows()
    R[G2].side_ahead(sent)
    R[G3].side_ahead(sent)
    v.mlp_part = project_back([tie(v.active[0], sent), v.active[1]], [whole(D0), whole(D1)])
    v.mlp_other = other(v.mlp_part)
    v.fence()

    R[G2].send_side()
    R[G3].send_side()
    v.attn_grad = middle_back(v.grad, v.hidden, v.dn, v.got_dn, v.mlp_gain, seqs, own_len)
    sent = R[O].far()
    R[O].send_far()
    sent = R[G1].near(sent)
    sent = R[G0].fold(sent)
    R[D1].rows()
    d_context = sum(dot(a, w, 1, 0) for a, w in zip([tie(v.attn_grad[0], sent), v.attn_grad[1]], whole(O))).astype(bf16)
    v.d_qkv = attention_backward(
        v.qkv, d_context, v.lse, v.tables[2], v.tables[3], v.tables[0], v.tables[1], seqs, heads, kv
    )
    R[Q].far()
    v.fence()

    R[Q].send_far()
    v.mlp_got = across(v.mlp_other)
    del v.mlp_other
    sent = R[O].side()
    R[O].send_side()
    sent = R[G2].near(sent)
    sent = R[G1].fold(sent)
    R[G0].rows()
    v.in_part = project_back([tie(v.d_qkv, sent)], [whole(Q)])
    v.in_other = other(v.in_part)
    v.fence()

    sent = R[Q].side()
    R[Q].send_side()
    sent = R[O].near(sent)
    sent = R[G3].near(sent)
    R[G2].fold(sent)
    R[G1].rows()
    v.output = leave(slots, v.hidden, v.mlp_part, v.mlp_got, None, True)
    v.fence()

    v.in_got = across(v.in_other)
    del v.in_other
    sent = R[Q].near()
    sent = R[O].fold(sent)
    R[G3].fold(sent)
    R[G2].rows()
    v.fence()

    R[Q].fold()
    v.input_grad = leave(slots, v.attn_grad, v.in_part, v.in_got, (v.resid, v.attn_gain))
    R[O].rows()
    R[G3].rows()
    v.fence()
    R[Q].rows()

    def pick(which):
        parts = [
            v.sums[gates[k]][:, (2 * j + which) * TILE : (2 * j + which + 1) * TILE]
            for k in range(4)
            for j in range(bounds[k + 1] - bounds[k])
        ]
        return jnp.concatenate(parts, axis=1)

    grad_gate, grad_up, grad_qkv = pick(0), pick(1), v.sums[Q]

    def gain_sum(weights, grads, gain):
        total = sum(jnp.sum(w.astype(f32) * g, axis=1) for w, g in zip(weights, grads))
        return total / gain.astype(f32)

    gain_sums = jnp.stack([
        gain_sum([qkv_shard], [grad_qkv], attn_gain),
        gain_sum([w_gate, w_up], [grad_gate, grad_up], mlp_gain),
    ])
    gain_sums = gain_sums + across(gain_sums)
    return (
        v.output,
        v.input_grad,
        grad_qkv[:, :q_cols],
        grad_qkv[:, q_cols : q_cols + kv_wide],
        grad_qkv[:, q_cols + kv_wide :],
        v.sums[O].T,
        grad_gate,
        grad_up,
        jnp.concatenate([v.sums[D0], v.sums[D1]], axis=1).T,
        gain_sums[0],
        gain_sums[1],
    )


def solution(mesh):
    row, col = P("dp", "tensor"), P("tensor", "dp")
    seq = P("dp", "tensor", None)
    return jax.shard_map(
        shards,
        mesh=mesh,
        in_specs=(seq, P("dp", None), P("dp", None), row, row, row, col, row, row, col, P("dp"), P("dp"), seq),
        out_specs=(seq, seq, row, row, row, col, row, row, col, P("dp"), P("dp")),
        check_vma=False,
    )
```
